256 devices in a mesh: req: 32 (over x, y, core), tp: 8 (over z).
Axes of the slice: x: 4, y: 4, z: 8, core: 2. Of those that a mesh axis runs over, the one named last changes fastest.
Arguments:
- hidden: bfloat16 [1024, 24, 2560], P('req', None, 'tp'), may hold values from -6 to 6
- norm_gain: float32 [2560], replicated, may hold values from 0.25 to 1.75
- w_query: bfloat16 [2560, 2560], P(None, 'tp'), may hold values from -0.125 to 0.125
- w_keyval: bfloat16 [1280, 2560], P('tp'), may hold values from -0.125 to 0.125
- w_out: bfloat16 [2560, 2560], P('tp'), may hold values from -0.25 to 0.25
- kv_cache: bfloat16 [1024, 1280, 512], P('req', 'tp'), as said below
- lengths: int32 [1024], P('req'), may hold values from 2 to 508, as said below
- parents: int32 [1024, 24], P('req'), may hold values from 0 to 22, as said below
- accepted: int32 [1024, 4], P('req'), may hold values from 0 to 6, as said below
- slot_of: int32 [1024], P('req'), may hold values from 0 to 1023, as said below
Outputs:
- out_rows: bfloat16 [1024, 24, 2560], P('req', None, 'tp')
- new_cache: bfloat16 [1024, 1280, 512], P('req', 'tp')
The draws below stay inside these ranges and needn't reach their ends.
Inputs may be any that keep to these rules, and one draw needn't show every extreme that they name: `lengths`: some request has exactly 508 cached tokens. parents[r, 0] = 0 and parents[r, t] is t - 1 or max(t - 2, 0) for t >= 1. accepted[r, m] is the tree token at depth m on the path from token 0 to one token of request r, so accepted[r, 0] = 0. A permutation; the 32 requests held by req index i go to 32 different req indices, one to each: a request of index i lands in slot d * 32 + i, where d = slot_of // 32. `kv_cache`: keys and values of cached tokens; positions at or past a request's length are not read.
All inputs are finite; a program needn't handle non-finite values.
Results may differ from the reference program's by a relative error of at most 0.012.
Values may be sent and summed in bfloat16 or wider, within the bound.
No kernel may reach another device: no remote copies, remote signals or barrier semaphores. Data moves between devices by JAX's collectives and lax.ppermute only.
A program may use at most 128 MiB of HBM per device.

```python
import math
import jax
import jax.numpy as jnp
from jax import lax

D = 2560
H = 32
KVH = 8
HD = 80
TREE = 24
CACHE = 512
DEPTH = 4
REQ_DEV = 32
REQS = 1024
N_REQ = 32
N_TP = 8


def length_values(key):
    top_length = CACHE - DEPTH
    source = jnp.arange(REQS, dtype=jnp.int32) // REQ_DEV
    ceiling = 2 + (top_length - 2) * (1 + source % 4) // 4
    drawn = jax.random.randint(jax.random.fold_in(key, 11), (REQS,), 2, ceiling + 1)
    chosen = jax.random.randint(jax.random.fold_in(key, 12), (), 0, REQS)
    return jnp.where(jnp.arange(REQS, dtype=jnp.int32) == chosen, top_length, drawn).astype(jnp.int32)


def tree_parents(key):
    steps_back = jax.random.randint(jax.random.fold_in(key, 21), (REQS, TREE), 1, 3)
    first_last = jnp.logical_and(jnp.arange(REQS, dtype=jnp.int32)[:, None] == 0, jnp.arange(TREE, dtype=jnp.int32)[None, :] == TREE - 1)
    steps_back = jnp.where(first_last, 1, steps_back)
    return jnp.maximum(jnp.arange(TREE, dtype=jnp.int32)[None, :] - steps_back, 0).astype(jnp.int32)


def draw_lengths(key, part):
    return length_values(key)


def draw_parents(key, part):
    return tree_parents(key)


def draw_accepted(key, part):
    parents = tree_parents(key)
    end_token = (TREE - 1 - jax.random.randint(jax.random.fold_in(key, 22), (REQS,), 0, 2)).astype(jnp.int32)

    def climb_up(index_step, state):
        ancestor_chain, current = state
        ancestor_chain = ancestor_chain.at[:, index_step].set(current)
        current = jnp.take_along_axis(parents, current[:, None], axis=1)[:, 0]
        return (ancestor_chain, current)
    ancestor_chain, finished = lax.fori_loop(0, TREE, climb_up, (jnp.zeros((REQS, TREE), jnp.int32), end_token))
    depths = jnp.sum((ancestor_chain != 0).astype(jnp.int32), axis=1)
    levels = jnp.arange(DEPTH, dtype=jnp.int32)
    return jnp.take_along_axis(ancestor_chain, depths[:, None] - levels[None, :], axis=1).astype(jnp.int32)


def draw_slot_of(key, part):
    length_grid = length_values(key).reshape(N_REQ, REQ_DEV)
    local_index = jnp.arange(REQ_DEV, dtype=jnp.int32)
    ordering = length_grid * REQ_DEV + local_index[None, :]
    ranking = jnp.argsort(jnp.argsort(-ordering, axis=1, stable=True), axis=1, stable=True).astype(jnp.int32)
    offset = jax.random.randint(jax.random.fold_in(key, 13), (N_REQ, 1), 0, N_REQ)
    target = (ranking + offset) % N_REQ
    source_index = jnp.arange(N_REQ, dtype=jnp.int32)[:, None]
    return (target * REQ_DEV + source_index).reshape(REQS).astype(jnp.int32)


def draw_kv_cache(key, part):
    lane_count = KVH * 2 * HD
    drawn = jnp.clip(jax.random.normal(jax.random.fold_in(key, 33), (REQS, lane_count, CACHE), jnp.float32), -6.0, 6.0)
    return drawn.astype(jnp.bfloat16)


def shard_levels(own_key, extent, cuts, smallest, high):
    gain = 1.0
    for position, parts in cuts:
        steps = jax.random.uniform(jax.random.fold_in(jax.random.fold_in(own_key, 6), position), (parts,), jnp.float32, smallest / len(cuts), high / len(cuts))
        gain = gain * jnp.repeat(jnp.exp(steps), extent[position] // parts).reshape((-1,) + (1,) * (len(extent) - 1 - position))
    return gain


def bell_draw(own_key, extent, width, reach, shards=(), kind=jnp.bfloat16):
    gain = shard_levels(own_key, extent, shards, -0.22, 0.18) if shards else 1.0
    entries = jax.random.normal(own_key, extent, jnp.float32) * width * gain
    return jnp.minimum(jnp.maximum(entries, -reach), reach).astype(kind)


def setup_inputs(seed: int = 0) -> dict:
    seeds = jax.random.split(jax.random.key(seed), 11)
    return {
        "hidden": bell_draw(seeds[0], (REQS, TREE, D), 1.0, 6.0, ((0, 32), (2, 8))),
        "norm_gain": jnp.clip(1.0 + 0.15 * jax.random.normal(seeds[1], (D,), jnp.float32), 0.25, 1.75),
        "w_query": bell_draw(seeds[2], (D, H * HD), D ** -0.5, 0.125, ((1, 8),)),
        "w_keyval": bell_draw(seeds[3], (KVH * 2 * HD, D), D ** -0.5, 0.125, ((0, 8),)),
        "w_out": bell_draw(seeds[4], (H * HD, D), (H * HD // 4) ** -0.5, 0.25, ((0, 8),)),
        "kv_cache": draw_kv_cache(jax.random.fold_in(seeds[10], 71), 0),
        "lengths": draw_lengths(jax.random.fold_in(seeds[10], 71), 0),
        "parents": draw_parents(jax.random.fold_in(seeds[10], 71), 0),
        "accepted": draw_accepted(jax.random.fold_in(seeds[10], 71), 0),
        "slot_of": draw_slot_of(jax.random.fold_in(seeds[10], 71), 0),
    }


def ancestry(parents):
    tree_size = parents.shape[-1]
    tokens = jnp.arange(tree_size, dtype=jnp.int32)

    def follow(index_step, state):
        marks, depths, current = state
        marks = jnp.logical_or(marks, current[..., :, None] == tokens)
        depths = depths + (current != 0).astype(jnp.int32)
        current = jnp.take_along_axis(parents, current, axis=-1)
        return (marks, depths, current)
    start = jnp.broadcast_to(tokens, parents.shape)
    marks = jnp.zeros(parents.shape + (tree_size,), jnp.bool_)
    marks, depths, finished = lax.fori_loop(0, tree_size, follow, (marks, jnp.zeros(parents.shape, jnp.int32), start))
    return (marks, depths)

def rope_tables(positions):
    frequency = 10000.0 ** (-2.0 * jnp.arange(HD // 2, dtype=jnp.float32) / HD)
    angles = positions.astype(jnp.float32)[..., None] * frequency
    return (jnp.cos(angles), jnp.sin(angles))

def rotate_pairs(values, cosines, sines):
    half_size = values.shape[-1] // 2
    first_half = values[..., :half_size]
    second_half = values[..., half_size:]
    return jnp.concatenate([first_half * cosines - second_half * sines, second_half * cosines + first_half * sines], axis=-1)

def place_columns(kept_rows, new_columns, start):
    return lax.dynamic_update_slice(kept_rows, new_columns, (jnp.zeros((), jnp.int32), start.astype(jnp.int32)))

def reference(hidden, norm_gain, w_query, w_keyval, w_out, kv_cache, lengths, parents, accepted, slot_of):
    requests, tree_size, full_width = hidden.shape
    cache_len = kv_cache.shape[2]
    group_size = H // KVH
    score_scale = 1.0 / math.sqrt(HD)
    values = hidden.astype(jnp.float32)
    spread = lax.optimization_barrier(jnp.mean(values * values, axis=-1, keepdims=True))
    normed = (values * lax.rsqrt(spread + 1e-05) * norm_gain).astype(jnp.bfloat16)
    flat_rows = normed.reshape(requests * tree_size, full_width)
    query = jnp.dot(flat_rows, w_query, preferred_element_type=jnp.float32).reshape(requests, tree_size, KVH, group_size, HD)
    keyval = lax.dot_general(flat_rows, w_keyval, (((1,), (1,)), ((), ())), preferred_element_type=jnp.float32).reshape(requests, tree_size, KVH, 2, HD)
    ancestors, depths = ancestry(parents)
    cosines, sines = rope_tables(lengths[:, None] + depths)
    query = rotate_pairs(query, cosines[:, :, None, None], sines[:, :, None, None]).astype(jnp.bfloat16)
    keys = rotate_pairs(keyval[:, :, :, 0], cosines[:, :, None], sines[:, :, None]).astype(jnp.bfloat16)
    tree_values = keyval[:, :, :, 1].astype(jnp.bfloat16)
    tree_kv = jnp.stack([keys, tree_values], axis=3).reshape(requests, tree_size, KVH * 2 * HD)
    positions = jnp.arange(cache_len, dtype=jnp.int32)

    def attend(pieces):
        query_one, kv_one, cache_one, length_one, marks_one = pieces
        cache_rows = jnp.transpose(cache_one, (1, 0))
        joined = jnp.concatenate([cache_rows, kv_one], axis=0).reshape(cache_len + tree_size, KVH, 2, HD).astype(jnp.float32)
        live_cache = jnp.broadcast_to(positions < length_one, (tree_size, cache_len))
        live = jnp.concatenate([live_cache, marks_one], axis=1)
        scores = jnp.einsum('tgqe,cge->gqtc', query_one.astype(jnp.float32), joined[:, :, 0]) * score_scale
        scores = jnp.where(live, scores, -jnp.inf)
        row_max = lax.optimization_barrier(jnp.max(scores, axis=-1, keepdims=True))
        weights = jnp.exp(scores - row_max)
        probs = (weights / lax.optimization_barrier(jnp.sum(weights, axis=-1, keepdims=True))).astype(jnp.bfloat16)
        context = jnp.einsum('gqtc,cge->tgqe', probs.astype(jnp.float32), joined[:, :, 1])
        return context.astype(jnp.bfloat16).reshape(tree_size, H * HD)
    context = lax.map(attend, (query, tree_kv, kv_cache, lengths, ancestors))
    flat_context = context.reshape(requests * tree_size, H * HD)
    heads_width = H * HD // N_TP
    summed = jnp.zeros((requests * tree_size, full_width), jnp.float32)
    for group_index in range(N_TP):
        lower = group_index * heads_width
        partial_value = jnp.dot(flat_context[:, lower:lower + heads_width], w_out[lower:lower + heads_width], preferred_element_type=jnp.float32).astype(jnp.bfloat16)
        summed = summed + partial_value.astype(jnp.float32)
    out_rows = (values + summed.reshape(requests, tree_size, full_width)).astype(jnp.bfloat16)
    accepted_kv = jnp.transpose(jnp.take_along_axis(tree_kv, accepted[:, :, None], axis=1), (0, 2, 1))
    live_rows = positions[None, :] < lengths[:, None]
    kept = jnp.where(live_rows[:, None, :], kv_cache, jnp.zeros((), jnp.bfloat16))
    compacted = jax.vmap(place_columns)(kept, accepted_kv, lengths)
    new_cache = jnp.zeros_like(compacted).at[slot_of].set(compacted)
    return (out_rows, new_cache)
```

```python
import math

import jax
import jax.numpy as jnp
from jax import lax
from jax.experimental import pallas as pl
from jax.experimental.pallas import tpu as pltpu
from jax.sharding import PartitionSpec as P

H = 32
KVH = 8
HD = 80
D = 2560
TREE = 24
CACHE = 512
DEPTH = 4
N_TP = 8
GROUP = H // KVH
LANES = 128
REQ_BLOCK = 8
ROWS = REQ_BLOCK * TREE
HALF = ROWS // 2
PACKED = 2 * ROWS + HALF
WIDTH = D // N_TP
NEG = -1e30
EXTRA = 16
BF = jnp.bfloat16
F32 = jnp.float32
VMEM_LIMIT = 56 * 1024 * 1024


def lane_index(shape):
    return lax.broadcasted_iota(jnp.int32, shape, len(shape) - 1)


def swap_halves(tile):
    return pltpu.roll(tile, 64, 1)


def pack_kernel(parity, x_ref, o_ref):
    x = x_ref[...].astype(F32)
    t0 = x[:, 0:128]
    t1 = x[:, 128:256]
    t2 = jnp.concatenate([x[:, 256:320], jnp.zeros((ROWS, 64), F32)], axis=1)
    low = lane_index((ROWS, LANES)) < 64
    low_half = lane_index((HALF, LANES)) < 64
    even = jnp.bitwise_and(parity[0], 1) == 0

    @pl.when(even)
    def _():
        o_ref[0, 0:ROWS] = t0.astype(BF)
        o_ref[0, ROWS : 2 * ROWS] = t1.astype(BF)
        o_ref[0, 2 * ROWS : PACKED] = jnp.where(
            low_half, t2[:HALF], swap_halves(t2[HALF:])
        ).astype(BF)

    @pl.when(jnp.logical_not(even))
    def _():
        s0, s1, s2 = swap_halves(t0), swap_halves(t1), swap_halves(t2)
        o_ref[0, 0:ROWS] = jnp.where(low, s0, s1).astype(BF)
        o_ref[0, ROWS : 2 * ROWS] = jnp.where(low, s1, s2).astype(BF)
        o_ref[0, 2 * ROWS : PACKED] = jnp.where(low_half, t0[:HALF], s0[HALF:]).astype(BF)


def pack_rows(rows, parity):
    blocks = rows.shape[0] // ROWS
    return pl.pallas_call(
        pack_kernel,
        out_shape=jax.ShapeDtypeStruct((blocks, PACKED, LANES), BF),
        grid_spec=pltpu.PrefetchScalarGridSpec(
            num_scalar_prefetch=1,
            grid=(blocks,),
            in_specs=[pl.BlockSpec((ROWS, WIDTH), lambda b, p: (b, 0))],
            out_specs=pl.BlockSpec((1, PACKED, LANES), lambda b, p: (b, 0, 0)),
        ),
        name="pack_rows",
    )(parity, rows)


def finish_kernel(parity, s_ref, x_ref, o_ref):
    m0 = s_ref[0, 0:ROWS].astype(F32)
    m1 = s_ref[0, ROWS : 2 * ROWS].astype(F32)
    packed_tail = s_ref[0, 2 * ROWS : PACKED].astype(F32)
    tail = jnp.concatenate([packed_tail, swap_halves(packed_tail)], axis=0)
    low = lane_index((ROWS, LANES)) < 64
    even = jnp.bitwise_and(parity[0], 1) == 0

    @pl.when(even)
    def _():
        total = jnp.concatenate([m0, m1, tail], axis=1)[:, :WIDTH]
        o_ref[...] = (x_ref[...].astype(F32) + total).astype(BF)

    @pl.when(jnp.logical_not(even))
    def _():
        s0, s1 = swap_halves(m0), swap_halves(m1)
        total = jnp.concatenate(
            [jnp.where(low, tail, s0), jnp.where(low, s0, s1), s1], axis=1
        )[:, :WIDTH]
        o_ref[...] = (x_ref[...].astype(F32) + total).astype(BF)


def finish_rows(summed, rows, parity):
    blocks = rows.shape[0] // ROWS
    return pl.pallas_call(
        finish_kernel,
        out_shape=jax.ShapeDtypeStruct(rows.shape, BF),
        grid_spec=pltpu.PrefetchScalarGridSpec(
            num_scalar_prefetch=1,
            grid=(blocks,),
            in_specs=[
                pl.BlockSpec((1, PACKED, LANES), lambda b, p: (b, 0, 0)),
                pl.BlockSpec((ROWS, WIDTH), lambda b, p: (b, 0)),
            ],
            out_specs=pl.BlockSpec((ROWS, WIDTH), lambda b, p: (b, 0)),
        ),
        name="finish_rows",
    )(parity, summed, rows)


def prep_kernel(parents_ref, cos_ref, sin_ref, step_ref, bias_out, cos_out, sin_out):
    requests = parents_ref.shape[0]
    lane = lane_index((requests, LANES))
    step_cos = step_ref[0:1, :]
    step_sin = step_ref[1:2, :]
    sign = step_ref[2:3, :]
    parents = parents_ref[...]
    marks = jnp.where(lane == 0, 1.0, 0.0)
    cosines, sines = cos_ref[...], sin_ref[...]
    older = (marks, cosines, sines)
    newer = older
    for t in range(TREE):
        if t > 0:
            near = jnp.broadcast_to(parents[:, t : t + 1], (requests, LANES)) == t - 1
            marks, cosines, sines = (jnp.where(near, a, b) for a, b in zip(newer, older))
            marks = jnp.where(lane == t, 1.0, marks)
            if t > 0:
                cosines, sines = (
                    cosines * step_cos - sines * step_sin,
                    sines * step_cos + cosines * step_sin,
                )
            older, newer = newer, (marks, cosines, sines)
        bias_out[:, t, :] = jnp.where(marks > 0.5, 0.0, NEG)
        cos_out[:, t, :] = cosines
        sin_out[:, t, :] = sines * sign


def prepare_tables(parents, lengths):
    requests = parents.shape[0]
    lane = jnp.arange(LANES)
    pair = jnp.where(lane < HD // 2, lane, lane - HD // 2)
    frequency = 10000.0 ** (-2.0 * pair.astype(F32) / HD)
    angles = lengths.astype(F32)[:, None] * frequency[None, :]
    sign = jnp.where(lane < HD // 2, -1.0, jnp.where(lane < HD, 1.0, 0.0))
    steps = jnp.stack([jnp.cos(frequency), jnp.sin(frequency), sign] + [sign] * 5)
    table = jax.ShapeDtypeStruct((requests, TREE, LANES), F32)
    return pl.pallas_call(
        prep_kernel, out_shape=(table, table, table), name="prepare_tables"
    )(parents, jnp.cos(angles), jnp.sin(angles), steps)


def order_kernel(order, cache_ref, key_ref, value_ref, key_sems, value_sems):
    copies = []
    for d in range(cache_ref.shape[0]):
        source = order[d]
        copies.append(
            pltpu.make_async_copy(
                cache_ref.at[source, pl.ds(0, HD)], key_ref.at[d], key_sems.at[d]
            )
        )
        copies.append(
            pltpu.make_async_copy(
                cache_ref.at[source, pl.ds(HD, HD)],
                value_ref.at[d, pl.ds(0, HD)],
                value_sems.at[d],
            )
        )
    for copy in copies:
        copy.start()
    for copy in copies:
        copy.wait()


def order_cache(kv_cache, send_order):
    held = kv_cache.shape[0]
    return pl.pallas_call(
        order_kernel,
        out_shape=(
            jax.ShapeDtypeStruct((held, HD, CACHE), BF),
            jax.ShapeDtypeStruct((held, HD + EXTRA, CACHE), BF),
        ),
        grid_spec=pltpu.PrefetchScalarGridSpec(
            num_scalar_prefetch=1,
            grid=(1,),
            in_specs=[pl.BlockSpec(memory_space=pl.ANY)],
            out_specs=(pl.BlockSpec(memory_space=pl.ANY), pl.BlockSpec(memory_space=pl.ANY)),
            scratch_shapes=[
                pltpu.SemaphoreType.DMA((held,)),
                pltpu.SemaphoreType.DMA((held,)),
            ],
        ),
        name="order_cache",
    )(send_order, kv_cache)


def layer_kernel(
    lengths,
    accepted,
    destination,
    x_ref,
    wq_ref,
    wkv_ref,
    wo_ref,
    cache_ref,
    bias_ref,
    cos_ref,
    sin_ref,
    send_in,
    out_ref,
    send_out,
    xs,
    qkv,
    ctx,
    wo,
    extra,
    sems,
    *,
    first_block,
):
    b = pl.program_id(0)

    @pl.when(b == 0)
    def _():
        wo[...] = jnp.zeros_like(wo)
        for h in range(GROUP):
            wo[h * LANES : h * LANES + HD] = wo_ref[h * HD : (h + 1) * HD]
        ctx[...] = jnp.zeros_like(ctx)
        extra[...] = jnp.zeros_like(extra)

    low_half = lane_index((HALF, LANES)) < 64
    squares = jnp.zeros((ROWS, LANES), F32)
    for j in range(N_TP // 2):
        base = j * 5 * LANES
        for device, at in ((2 * j, base), (2 * j + 1, base + 3 * LANES)):
            for part in range(2):
                piece = x_ref[device, 0, part * ROWS : (part + 1) * ROWS]
                xs[:, at + part * LANES : at + (part + 1) * LANES] = piece
                wide = piece.astype(F32)
                squares = squares + wide * wide
        even_tail = x_ref[2 * j, 0, 2 * ROWS : PACKED].astype(F32)
        odd_tail = x_ref[2 * j + 1, 0, 2 * ROWS : PACKED].astype(F32)
        tail = jnp.concatenate(
            [
                jnp.where(low_half, even_tail, swap_halves(odd_tail)),
                jnp.where(low_half, swap_halves(even_tail), odd_tail),
            ],
            axis=0,
        )
        xs[:, base + 2 * LANES : base + 3 * LANES] = tail.astype(BF)
        squares = squares + tail * tail
    scale = lax.rsqrt(jnp.sum(squares, axis=1, keepdims=True) * (1.0 / D) + 1e-05)
    flat = xs[...]
    query = jnp.dot(flat, wq_ref[...], preferred_element_type=F32) * scale
    keyval = jnp.dot(flat, wkv_ref[...], preferred_element_type=F32) * scale
    cosines = cos_ref[...].reshape(ROWS, LANES)
    sines = sin_ref[...].reshape(ROWS, LANES)
    first = lane_index((ROWS, LANES)) < HD // 2

    def rotate(tile):
        other = jnp.where(
            first, pltpu.roll(tile, LANES - HD // 2, 1), pltpu.roll(tile, HD // 2, 1)
        )
        return tile * cosines + other * sines

    for h in range(GROUP):
        qkv[:, h * LANES : (h + 1) * LANES] = rotate(query[:, h * LANES : (h + 1) * LANES])
    qkv[:, GROUP * LANES : (GROUP + 1) * LANES] = rotate(keyval[:, :LANES])
    qkv[:, (GROUP + 1) * LANES :] = keyval[:, LANES:]

    factor = math.log2(math.e) / math.sqrt(HD)
    column = lane_index((GROUP * TREE, CACHE))
    extra_row = lax.broadcasted_iota(jnp.int32, (EXTRA, LANES), 0)
    pick_row = lax.broadcasted_iota(jnp.int32, (EXTRA, TREE), 0)
    pick_column = lane_index((EXTRA, TREE))
    copies = []
    for i in range(REQ_BLOCK):
        r = (first_block + b) * REQ_BLOCK + i
        length = lengths[r]
        rows = slice(i * TREE, (i + 1) * TREE)
        q = jnp.concatenate(
            [qkv[rows, h * LANES : (h + 1) * LANES] for h in range(GROUP)], axis=0
        ).astype(BF)
        k = qkv[rows, GROUP * LANES : (GROUP + 1) * LANES].astype(BF)
        v = qkv[rows, (GROUP + 1) * LANES :].astype(BF)
        cached = jnp.dot(q[:, :HD], cache_ref[i, 0:HD], preferred_element_type=F32)
        cached = jnp.where(column < length, cached * factor, NEG)
        fresh = lax.dot_general(q, k, (((1,), (1,)), ((), ())), preferred_element_type=F32)
        bias = bias_ref[i][:, :TREE]
        fresh = fresh * factor + jnp.concatenate([bias] * GROUP, axis=0)
        top = jnp.maximum(
            jnp.max(cached, axis=1, keepdims=True), jnp.max(fresh, axis=1, keepdims=True)
        )
        cached = jnp.exp2(cached - top)
        fresh = jnp.exp2(fresh - top)
        total = jnp.sum(cached, axis=1, keepdims=True) + jnp.sum(fresh, axis=1, keepdims=True)
        mixed = lax.dot_general(
            cached.astype(BF),
            cache_ref[i, HD : 2 * HD],
            (((1,), (1,)), ((), ())),
            preferred_element_type=F32,
        ) + jnp.dot(fresh.astype(BF), v[:, :HD], preferred_element_type=F32)
        mixed = mixed / total
        for h in range(GROUP):
            ctx[rows, h * LANES : h * LANES + HD] = mixed[h * TREE : (h + 1) * TREE]

        wanted = jnp.full((EXTRA, TREE), -1, jnp.int32)
        for m in range(DEPTH):
            wanted = jnp.where(pick_row == m, accepted[r * DEPTH + m], wanted)
        pick = jnp.where(pick_column == wanted, 1.0, 0.0).astype(BF)
        new_keys = jnp.dot(pick, k, preferred_element_type=F32)
        new_values = jnp.dot(pick, v, preferred_element_type=F32)
        coarse = (length // 16).astype(F32)
        fine = (length % 16).astype(F32)
        new_keys = jnp.where(extra_row == 8, coarse, jnp.where(extra_row == 9, fine, new_keys))
        extra[i, :, 0:LANES] = new_keys.astype(BF)
        extra[i, :, LANES : 2 * LANES] = new_values.astype(BF)
        copies.append(
            pltpu.make_async_copy(
                extra.at[i], send_out.at[destination[r], pl.ds(HD, EXTRA)], sems.at[i]
            )
        )
        copies[-1].start()

    partial = jnp.dot(ctx[...].astype(BF), wo[...], preferred_element_type=F32)
    for j in range(N_TP // 2):
        base = j * 5 * LANES
        for device, at in ((2 * j, base), (2 * j + 1, base + 3 * LANES)):
            for part in range(2):
                out_ref[device, 0, part * ROWS : (part + 1) * ROWS] = partial[
                    :, at + part * LANES : at + (part + 1) * LANES
                ].astype(BF)
        tail = partial[:, base + 2 * LANES : base + 3 * LANES]
        out_ref[2 * j, 0, 2 * ROWS : PACKED] = jnp.where(
            low_half, tail[:HALF], swap_halves(tail[HALF:])
        ).astype(BF)
        out_ref[2 * j + 1, 0, 2 * ROWS : PACKED] = jnp.where(
            low_half, swap_halves(tail[:HALF]), tail[HALF:]
        ).astype(BF)
    for copy in copies:
        copy.wait()


def verify_layer(
    gathered, wq, wkv, w_out, kv_cache, tables, lengths, accepted, destination, send, first_block
):
    blocks = gathered.shape[1]
    full = lambda b, *_: (0, 0)
    packed = pl.BlockSpec((N_TP, 1, PACKED, LANES), lambda b, *_: (0, b, 0, 0))
    table = pl.BlockSpec((REQ_BLOCK, TREE, LANES), lambda b, *_: (first_block + b, 0, 0))
    anywhere = pl.BlockSpec(memory_space=pl.ANY)

    def body(*refs):
        layer_kernel(*refs, first_block=first_block)

    return pl.pallas_call(
        body,
        out_shape=(
            jax.ShapeDtypeStruct((N_TP, blocks, PACKED, LANES), BF),
            jax.ShapeDtypeStruct(send.shape, BF),
        ),
        grid_spec=pltpu.PrefetchScalarGridSpec(
            num_scalar_prefetch=3,
            grid=(blocks,),
            in_specs=[
                packed,
                pl.BlockSpec(wq.shape, full),
                pl.BlockSpec(wkv.shape, full),
                pl.BlockSpec(w_out.shape, full),
                pl.BlockSpec(
                    (REQ_BLOCK, 2 * HD, CACHE), lambda b, *_: (first_block + b, 0, 0)
                ),
                table,
                table,
                table,
                anywhere,
            ],
            out_specs=(packed, anywhere),
            scratch_shapes=[
                pltpu.VMEM((ROWS, D), BF),
                pltpu.VMEM((ROWS, (GROUP + 2) * LANES), F32),
                pltpu.VMEM((ROWS, GROUP * LANES), F32),
                pltpu.VMEM((GROUP * LANES, D), BF),
                pltpu.VMEM((REQ_BLOCK, EXTRA, CACHE), BF),
                pltpu.SemaphoreType.DMA((REQ_BLOCK,)),
            ],
        ),
        input_output_aliases={11: 1},
        compiler_params=pltpu.CompilerParams(vmem_limit_bytes=VMEM_LIMIT),
        name="verify_layer",
    )(
        lengths,
        accepted,
        destination,
        gathered,
        wq,
        wkv,
        w_out,
        kv_cache,
        *tables,
        send,
    )


def assemble_kernel(key_ref, value_ref, o_ref):
    column = lane_index((HD, CACHE))
    place_row = lax.broadcasted_iota(jnp.int32, (EXTRA, CACHE), 0)
    place_column = lane_index((EXTRA, CACHE))
    for i in range(key_ref.shape[0]):
        extra = value_ref[i, HD : HD + EXTRA]
        wide = extra[:, :LANES].astype(F32)
        length = (wide[8:9] * 16.0 + wide[9:10]).astype(jnp.int32)
        length = jnp.concatenate([length] * (CACHE // LANES), axis=1)
        place = jnp.where(
            jnp.logical_and(place_column == length + place_row, place_row < DEPTH), 1.0, 0.0
        ).astype(BF)
        live = column < length
        for part, ref in ((0, key_ref), (1, value_ref)):
            new = lax.dot_general(
                extra[:, part * LANES : part * LANES + LANES],
                place,
                (((0,), (0,)), ((), ())),
                preferred_element_type=F32,
            )[:HD]
            o_ref[i, part * HD : (part + 1) * HD] = jnp.where(
                live, ref[i, 0:HD].astype(F32), new
            ).astype(BF)


def assemble_cache(keys, values):
    held = keys.shape[0]
    step = 4
    return pl.pallas_call(
        assemble_kernel,
        out_shape=jax.ShapeDtypeStruct((held, 2 * HD, CACHE), BF),
        grid=(held // step,),
        in_specs=[
            pl.BlockSpec((step, HD, CACHE), lambda s: (s, 0, 0)),
            pl.BlockSpec((step, HD + EXTRA, CACHE), lambda s: (s, 0, 0)),
        ],
        out_specs=pl.BlockSpec((step, 2 * HD, CACHE), lambda s: (s, 0, 0)),
        name="assemble_cache",
    )(keys, values)


def spread_heads(heads):
    source = jnp.arange(heads * HD)[:, None]
    target = jnp.arange(heads * LANES)[None, :]
    return (source // HD * LANES + source % HD == target).astype(BF)


def exchange(values):
    return lax.all_to_all(values, "req", split_axis=0, concat_axis=0, tiled=True)


def per_device(
    hidden, norm_gain, w_query, w_keyval, w_out, kv_cache, lengths, parents, accepted, slot_of
):
    held = hidden.shape[0]
    rows = hidden.reshape(held * TREE, WIDTH)
    parity = lax.axis_index("tp").astype(jnp.int32).reshape(1)
    packed = pack_rows(rows, parity)
    gathered = lax.all_gather(packed, "tp", axis=0, tiled=False)

    destination = slot_of // held
    peer_index = jnp.arange(held, dtype=jnp.int32)
    matches = (destination[None, :] == peer_index[:, None]).astype(jnp.int32)
    send_order = jnp.sum(matches * peer_index[None, :], axis=1)
    key_send, value_send = order_cache(kv_cache, send_order)
    key_received = exchange(key_send)

    tables = prepare_tables(parents, lengths)
    gain = norm_gain[:, None]
    wq = (jnp.dot(w_query, spread_heads(GROUP), preferred_element_type=F32) * gain).astype(BF)
    wkv = lax.dot_general(
        w_keyval, spread_heads(2), (((0,), (0,)), ((), ())), preferred_element_type=F32
    )
    wkv = (wkv * gain).astype(BF)

    key_received, value_send = lax.optimization_barrier((key_received, value_send))
    partial, value_send = verify_layer(
        gathered,
        wq,
        wkv,
        w_out,
        kv_cache,
        tables,
        lengths,
        accepted.reshape(-1),
        destination,
        value_send,
        0,
    )
    summed = lax.psum_scatter(partial, "tp", scatter_dimension=0, tiled=True)
    value_received = exchange(value_send)
    new_cache = assemble_cache(key_received, value_received)
    out_rows = finish_rows(summed.reshape(-1, PACKED, LANES), rows, parity)
    return (out_rows.reshape(hidden.shape), new_cache)


def solution(mesh):
    in_specs = (
        P("req", None, "tp"),
        P(),
        P(None, "tp"),
        P("tp", None),
        P("tp", None),
        P("req", "tp", None),
        P("req"),
        P("req", None),
        P("req", None),
        P("req"),
    )
    out_specs = (P("req", None, "tp"), P("req", "tp", None))
    return jax.shard_map(
        per_device, mesh=mesh, in_specs=in_specs, out_specs=out_specs, check_vma=False
    )
```

```python
import math

import jax
import jax.numpy as jnp
from jax import lax
from jax.experimental import pallas as pl
from jax.experimental.pallas import tpu as pltpu
from jax.sharding import PartitionSpec as P

H = 32
KVH = 8
HD = 80
D = 2560
TREE = 24
CACHE = 512
DEPTH = 4
N_TP = 8
GROUP = H // KVH
LANES = 128
REQ_BLOCK = 8
ROWS = REQ_BLOCK * TREE
HALF = ROWS // 2
PACKED = 2 * ROWS + HALF
WIDTH = D // N_TP
NEG = -1e30
EXTRA = 16
BF = jnp.bfloat16
F32 = jnp.float32
VMEM_LIMIT = 56 * 1024 * 1024


def lane_index(shape):
    return lax.broadcasted_iota(jnp.int32, shape, len(shape) - 1)


def swap_halves(tile):
    return pltpu.roll(tile, 64, 1)


def pack_kernel(parity, x_ref, o_ref):
    x = x_ref[...].astype(F32)
    t0 = x[:, 0:128]
    t1 = x[:, 128:256]
    t2 = jnp.concatenate([x[:, 256:320], jnp.zeros((ROWS, 64), F32)], axis=1)
    low = lane_index((ROWS, LANES)) < 64
    low_half = lane_index((HALF, LANES)) < 64
    even = jnp.bitwise_and(parity[0], 1) == 0

    @pl.when(even)
    def _():
        o_ref[0, 0:ROWS] = t0.astype(BF)
        o_ref[0, ROWS : 2 * ROWS] = t1.astype(BF)
        o_ref[0, 2 * ROWS : PACKED] = jnp.where(
            low_half, t2[:HALF], swap_halves(t2[HALF:])
        ).astype(BF)

    @pl.when(jnp.logical_not(even))
    def _():
        s0, s1, s2 = swap_halves(t0), swap_halves(t1), swap_halves(t2)
        o_ref[0, 0:ROWS] = jnp.where(low, s0, s1).astype(BF)
        o_ref[0, ROWS : 2 * ROWS] = jnp.where(low, s1, s2).astype(BF)
        o_ref[0, 2 * ROWS : PACKED] = jnp.where(low_half, t0[:HALF], s0[HALF:]).astype(BF)


def pack_rows(rows, parity):
    blocks = rows.shape[0] // ROWS
    return pl.pallas_call(
        pack_kernel,
        out_shape=jax.ShapeDtypeStruct((blocks, PACKED, LANES), BF),
        grid_spec=pltpu.PrefetchScalarGridSpec(
            num_scalar_prefetch=1,
            grid=(blocks,),
            in_specs=[pl.BlockSpec((ROWS, WIDTH), lambda b, p: (b, 0))],
            out_specs=pl.BlockSpec((1, PACKED, LANES), lambda b, p: (b, 0, 0)),
        ),
        name="pack_rows",
    )(parity, rows)


def finish_kernel(parity, s_ref, x_ref, o_ref):
    m0 = s_ref[0, 0:ROWS].astype(F32)
    m1 = s_ref[0, ROWS : 2 * ROWS].astype(F32)
    packed_tail = s_ref[0, 2 * ROWS : PACKED].astype(F32)
    tail = jnp.concatenate([packed_tail, swap_halves(packed_tail)], axis=0)
    low = lane_index((ROWS, LANES)) < 64
    even = jnp.bitwise_and(parity[0], 1) == 0

    @pl.when(even)
    def _():
        total = jnp.concatenate([m0, m1, tail], axis=1)[:, :WIDTH]
        o_ref[...] = (x_ref[...].astype(F32) + total).astype(BF)

    @pl.when(jnp.logical_not(even))
    def _():
        s0, s1 = swap_halves(m0), swap_halves(m1)
        total = jnp.concatenate(
            [jnp.where(low, tail, s0), jnp.where(low, s0, s1), s1], axis=1
        )[:, :WIDTH]
        o_ref[...] = (x_ref[...].astype(F32) + total).astype(BF)


def finish_rows(summed, rows, parity):
    blocks = rows.shape[0] // ROWS
    return pl.pallas_call(
        finish_kernel,
        out_shape=jax.ShapeDtypeStruct(rows.shape, BF),
        grid_spec=pltpu.PrefetchScalarGridSpec(
            num_scalar_prefetch=1,
            grid=(blocks,),
            in_specs=[
                pl.BlockSpec((1, PACKED, LANES), lambda b, p: (b, 0, 0)),
                pl.BlockSpec((ROWS, WIDTH), lambda b, p: (b, 0)),
            ],
            out_specs=pl.BlockSpec((ROWS, WIDTH), lambda b, p: (b, 0)),
        ),
        name="finish_rows",
    )(parity, summed, rows)


def prep_kernel(parents_ref, cos_ref, sin_ref, step_ref, bias_out, cos_out, sin_out):
    requests = parents_ref.shape[0]
    lane = lane_index((requests, LANES))
    step_cos = step_ref[0:1, :]
    step_sin = step_ref[1:2, :]
    sign = step_ref[2:3, :]
    parents = parents_ref[...]
    marks = jnp.where(lane == 0, 1.0, 0.0)
    cosines, sines = cos_ref[...], sin_ref[...]
    older = (marks, cosines, sines)
    newer = older
    for t in range(TREE):
        if t > 0:
            near = jnp.broadcast_to(parents[:, t : t + 1], (requests, LANES)) == t - 1
            marks, cosines, sines = (jnp.where(near, a, b) for a, b in zip(newer, older))
            marks = jnp.where(lane == t, 1.0, marks)
            if t > 0:
                cosines, sines = (
                    cosines * step_cos - sines * step_sin,
                    sines * step_cos + cosines * step_sin,
                )
            older, newer = newer, (marks, cosines, sines)
        bias_out[:, t, :] = jnp.where(marks > 0.5, 0.0, NEG)
        cos_out[:, t, :] = cosines
        sin_out[:, t, :] = sines * sign


def prepare_tables(parents, lengths):
    requests = parents.shape[0]
    lane = jnp.arange(LANES)
    pair = jnp.where(lane < HD // 2, lane, lane - HD // 2)
    frequency = 10000.0 ** (-2.0 * pair.astype(F32) / HD)
    angles = lengths.astype(F32)[:, None] * frequency[None, :]
    sign = jnp.where(lane < HD // 2, -1.0, jnp.where(lane < HD, 1.0, 0.0))
    steps = jnp.stack([jnp.cos(frequency), jnp.sin(frequency), sign] + [sign] * 5)
    table = jax.ShapeDtypeStruct((requests, TREE, LANES), F32)
    return pl.pallas_call(
        prep_kernel, out_shape=(table, table, table), name="prepare_tables"
    )(parents, jnp.cos(angles), jnp.sin(angles), steps)


def order_kernel(order, cache_ref, key_ref, value_ref, buffer, load_sems, key_sems, value_sems):
    loads, stores = [], []
    for d in range(cache_ref.shape[0]):
        loads.append(
            pltpu.make_async_copy(cache_ref.at[order[d]], buffer.at[d], load_sems.at[d])
        )
        loads[-1].start()
    for d, load in enumerate(loads):
        load.wait()
        stores.append(
            pltpu.make_async_copy(buffer.at[d, pl.ds(0, HD)], key_ref.at[d], key_sems.at[d])
        )
        stores.append(
            pltpu.make_async_copy(
                buffer.at[d, pl.ds(HD, HD)], value_ref.at[d, pl.ds(0, HD)], value_sems.at[d]
            )
        )
        stores[-2].start()
        stores[-1].start()
    for store in stores:
        store.wait()


def order_cache(kv_cache, send_order):
    held = kv_cache.shape[0]
    return pl.pallas_call(
        order_kernel,
        out_shape=(
            jax.ShapeDtypeStruct((held, HD, CACHE), BF),
            jax.ShapeDtypeStruct((held, HD + EXTRA, CACHE), BF),
        ),
        grid_spec=pltpu.PrefetchScalarGridSpec(
            num_scalar_prefetch=1,
            grid=(1,),
            in_specs=[pl.BlockSpec(memory_space=pl.ANY)],
            out_specs=(pl.BlockSpec(memory_space=pl.ANY), pl.BlockSpec(memory_space=pl.ANY)),
            scratch_shapes=[
                pltpu.VMEM(kv_cache.shape, BF),
                pltpu.SemaphoreType.DMA((held,)),
                pltpu.SemaphoreType.DMA((held,)),
                pltpu.SemaphoreType.DMA((held,)),
            ],
        ),
        compiler_params=pltpu.CompilerParams(vmem_limit_bytes=VMEM_LIMIT),
        name="order_cache",
    )(send_order, kv_cache)


def layer_kernel(
    lengths,
    accepted,
    destination,
    x_ref,
    wq_ref,
    wkv_ref,
    wo_ref,
    cache_ref,
    bias_ref,
    cos_ref,
    sin_ref,
    send_in,
    out_ref,
    send_out,
    xs,
    qkv,
    ctx,
    wo,
    extra,
    sems,
    *,
    first_block,
):
    b = pl.program_id(0)

    @pl.when(b == 0)
    def _():
        wo[...] = jnp.zeros_like(wo)
        for h in range(GROUP):
            wo[h * LANES : h * LANES + HD] = wo_ref[h * HD : (h + 1) * HD]
        ctx[...] = jnp.zeros_like(ctx)
        extra[...] = jnp.zeros_like(extra)

    low_half = lane_index((HALF, LANES)) < 64
    squares = jnp.zeros((ROWS, LANES), F32)
    for j in range(N_TP // 2):
        base = j * 5 * LANES
        for device, at in ((2 * j, base), (2 * j + 1, base + 3 * LANES)):
            for part in range(2):
                piece = x_ref[device, 0, part * ROWS : (part + 1) * ROWS]
                xs[:, at + part * LANES : at + (part + 1) * LANES] = piece
                wide = piece.astype(F32)
                squares = squares + wide * wide
        even_tail = x_ref[2 * j, 0, 2 * ROWS : PACKED].astype(F32)
        odd_tail = x_ref[2 * j + 1, 0, 2 * ROWS : PACKED].astype(F32)
        tail = jnp.concatenate(
            [
                jnp.where(low_half, even_tail, swap_halves(odd_tail)),
                jnp.where(low_half, swap_halves(even_tail), odd_tail),
            ],
            axis=0,
        )
        xs[:, base + 2 * LANES : base + 3 * LANES] = tail.astype(BF)
        squares = squares + tail * tail
    scale = lax.rsqrt(jnp.sum(squares, axis=1, keepdims=True) * (1.0 / D) + 1e-05)
    flat = xs[...]
    query = jnp.dot(flat, wq_ref[...], preferred_element_type=F32) * scale
    keyval = jnp.dot(flat, wkv_ref[...], preferred_element_type=F32) * scale
    cosines = cos_ref[...].reshape(ROWS, LANES)
    sines = sin_ref[...].reshape(ROWS, LANES)
    first = lane_index((ROWS, LANES)) < HD // 2

    def rotate(tile):
        other = jnp.where(
            first, pltpu.roll(tile, LANES - HD // 2, 1), pltpu.roll(tile, HD // 2, 1)
        )
        return tile * cosines + other * sines

    for h in range(GROUP):
        qkv[:, h * LANES : (h + 1) * LANES] = rotate(query[:, h * LANES : (h + 1) * LANES])
    qkv[:, GROUP * LANES : (GROUP + 1) * LANES] = rotate(keyval[:, :LANES])
    qkv[:, (GROUP + 1) * LANES :] = keyval[:, LANES:]

    factor = math.log2(math.e) / math.sqrt(HD)
    column = lane_index((GROUP * TREE, CACHE))
    extra_row = lax.broadcasted_iota(jnp.int32, (EXTRA, LANES), 0)
    pick_row = lax.broadcasted_iota(jnp.int32, (EXTRA, TREE), 0)
    pick_column = lane_index((EXTRA, TREE))
    copies = []
    for i in range(REQ_BLOCK):
        r = (first_block + b) * REQ_BLOCK + i
        length = lengths[r]
        rows = slice(i * TREE, (i + 1) * TREE)
        q = jnp.concatenate(
            [qkv[rows, h * LANES : (h + 1) * LANES] for h in range(GROUP)], axis=0
        ).astype(BF)
        k = qkv[rows, GROUP * LANES : (GROUP + 1) * LANES].astype(BF)
        v = qkv[rows, (GROUP + 1) * LANES :].astype(BF)
        cached = jnp.dot(q[:, :HD], cache_ref[i, 0:HD], preferred_element_type=F32)
        cached = jnp.where(column < length, cached * factor, NEG)
        fresh = lax.dot_general(q, k, (((1,), (1,)), ((), ())), preferred_element_type=F32)
        bias = bias_ref[i][:, :TREE]
        fresh = fresh * factor + jnp.concatenate([bias] * GROUP, axis=0)
        top = jnp.maximum(
            jnp.max(cached, axis=1, keepdims=True), jnp.max(fresh, axis=1, keepdims=True)
        )
        cached = jnp.exp2(cached - top)
        fresh = jnp.exp2(fresh - top)
        total = jnp.sum(cached, axis=1, keepdims=True) + jnp.sum(fresh, axis=1, keepdims=True)
        mixed = lax.dot_general(
            cached.astype(BF),
            cache_ref[i, HD : 2 * HD],
            (((1,), (1,)), ((), ())),
            preferred_element_type=F32,
        ) + jnp.dot(fresh.astype(BF), v[:, :HD], preferred_element_type=F32)
        mixed = mixed / total
        for h in range(GROUP):
            ctx[rows, h * LANES : h * LANES + HD] = mixed[h * TREE : (h + 1) * TREE]

        wanted = jnp.full((EXTRA, TREE), -1, jnp.int32)
        for m in range(DEPTH):
            wanted = jnp.where(pick_row == m, accepted[r * DEPTH + m], wanted)
        pick = jnp.where(pick_column == wanted, 1.0, 0.0).astype(BF)
        new_keys = jnp.dot(pick, k, preferred_element_type=F32)
        new_values = jnp.dot(pick, v, preferred_element_type=F32)
        coarse = (length // 16).astype(F32)
        fine = (length % 16).astype(F32)
        new_keys = jnp.where(extra_row == 8, coarse, jnp.where(extra_row == 9, fine, new_keys))
        extra[i, :, 0:LANES] = new_keys.astype(BF)
        extra[i, :, LANES : 2 * LANES] = new_values.astype(BF)
        copies.append(
            pltpu.make_async_copy(
                extra.at[i], send_out.at[destination[r], pl.ds(HD, EXTRA)], sems.at[i]
            )
        )
        copies[-1].start()

    partial = jnp.dot(ctx[...].astype(BF), wo[...], preferred_element_type=F32)
    for j in range(N_TP // 2):
        base = j * 5 * LANES
        for device, at in ((2 * j, base), (2 * j + 1, base + 3 * LANES)):
            for part in range(2):
                out_ref[device, 0, part * ROWS : (part + 1) * ROWS] = partial[
                    :, at + part * LANES : at + (part + 1) * LANES
                ].astype(BF)
        tail = partial[:, base + 2 * LANES : base + 3 * LANES]
        out_ref[2 * j, 0, 2 * ROWS : PACKED] = jnp.where(
            low_half, tail[:HALF], swap_halves(tail[HALF:])
        ).astype(BF)
        out_ref[2 * j + 1, 0, 2 * ROWS : PACKED] = jnp.where(
            low_half, swap_halves(tail[:HALF]), tail[HALF:]
        ).astype(BF)
    for copy in copies:
        copy.wait()


def verify_layer(
    gathered, wq, wkv, w_out, kv_cache, tables, lengths, accepted, destination, send, first_block
):
    blocks = gathered.shape[1]
    full = lambda b, *_: (0, 0)
    packed = pl.BlockSpec((N_TP, 1, PACKED, LANES), lambda b, *_: (0, b, 0, 0))
    table = pl.BlockSpec((REQ_BLOCK, TREE, LANES), lambda b, *_: (first_block + b, 0, 0))
    anywhere = pl.BlockSpec(memory_space=pl.ANY)

    def body(*refs):
        layer_kernel(*refs, first_block=first_block)

    return pl.pallas_call(
        body,
        out_shape=(
            jax.ShapeDtypeStruct((N_TP, blocks, PACKED, LANES), BF),
            jax.ShapeDtypeStruct(send.shape, BF),
        ),
        grid_spec=pltpu.PrefetchScalarGridSpec(
            num_scalar_prefetch=3,
            grid=(blocks,),
            in_specs=[
                packed,
                pl.BlockSpec(wq.shape, full),
                pl.BlockSpec(wkv.shape, full),
                pl.BlockSpec(w_out.shape, full),
                pl.BlockSpec(
                    (REQ_BLOCK, 2 * HD, CACHE), lambda b, *_: (first_block + b, 0, 0)
                ),
                table,
                table,
                table,
                anywhere,
            ],
            out_specs=(packed, anywhere),
            scratch_shapes=[
                pltpu.VMEM((ROWS, D), BF),
                pltpu.VMEM((ROWS, (GROUP + 2) * LANES), F32),
                pltpu.VMEM((ROWS, GROUP * LANES), F32),
                pltpu.VMEM((GROUP * LANES, D), BF),
                pltpu.VMEM((REQ_BLOCK, EXTRA, CACHE), BF),
                pltpu.SemaphoreType.DMA((REQ_BLOCK,)),
            ],
        ),
        input_output_aliases={11: 1},
        compiler_params=pltpu.CompilerParams(vmem_limit_bytes=VMEM_LIMIT),
        name="verify_layer",
    )(
        lengths,
        accepted,
        destination,
        gathered,
        wq,
        wkv,
        w_out,
        kv_cache,
        *tables,
        send,
    )


def assemble_kernel(key_ref, value_ref, o_ref):
    column = lane_index((HD, CACHE))
    place_row = lax.broadcasted_iota(jnp.int32, (EXTRA, CACHE), 0)
    place_column = lane_index((EXTRA, CACHE))
    for i in range(key_ref.shape[0]):
        extra = value_ref[i, HD : HD + EXTRA]
        wide = extra[:, :LANES].astype(F32)
        length = (wide[8:9] * 16.0 + wide[9:10]).astype(jnp.int32)
        length = jnp.concatenate([length] * (CACHE // LANES), axis=1)
        place = jnp.where(
            jnp.logical_and(place_column == length + place_row, place_row < DEPTH), 1.0, 0.0
        ).astype(BF)
        live = column < length
        for part, ref in ((0, key_ref), (1, value_ref)):
            new = lax.dot_general(
                extra[:, part * LANES : part * LANES + LANES],
                place,
                (((0,), (0,)), ((), ())),
                preferred_element_type=F32,
            )[:HD]
            o_ref[i, part * HD : (part + 1) * HD] = jnp.where(
                live, ref[i, 0:HD].astype(F32), new
            ).astype(BF)


def assemble_cache(keys, values):
    held = keys.shape[0]
    step = 4
    return pl.pallas_call(
        assemble_kernel,
        out_shape=jax.ShapeDtypeStruct((held, 2 * HD, CACHE), BF),
        grid=(held // step,),
        in_specs=[
            pl.BlockSpec((step, HD, CACHE), lambda s: (s, 0, 0)),
            pl.BlockSpec((step, HD + EXTRA, CACHE), lambda s: (s, 0, 0)),
        ],
        out_specs=pl.BlockSpec((step, 2 * HD, CACHE), lambda s: (s, 0, 0)),
        name="assemble_cache",
    )(keys, values)


def spread_heads(heads):
    source = jnp.arange(heads * HD)[:, None]
    target = jnp.arange(heads * LANES)[None, :]
    return (source // HD * LANES + source % HD == target).astype(BF)


def exchange(values):
    return lax.all_to_all(values, "req", split_axis=0, concat_axis=0, tiled=True)


def per_device(
    hidden, norm_gain, w_query, w_keyval, w_out, kv_cache, lengths, parents, accepted, slot_of
):
    held = hidden.shape[0]
    rows = hidden.reshape(held * TREE, WIDTH)
    parity = lax.axis_index("tp").astype(jnp.int32).reshape(1)
    packed = pack_rows(rows, parity)
    gathered = lax.all_gather(packed, "tp", axis=0, tiled=False)

    destination = slot_of // held
    peer_index = jnp.arange(held, dtype=jnp.int32)
    matches = (destination[None, :] == peer_index[:, None]).astype(jnp.int32)
    send_order = jnp.sum(matches * peer_index[None, :], axis=1)
    key_send, value_send = order_cache(kv_cache, send_order)
    key_received = exchange(key_send)

    tables = prepare_tables(parents, lengths)
    gain = norm_gain[:, None]
    wq = (jnp.dot(w_query, spread_heads(GROUP), preferred_element_type=F32) * gain).astype(BF)
    wkv = lax.dot_general(
        w_keyval, spread_heads(2), (((0,), (0,)), ((), ())), preferred_element_type=F32
    )
    wkv = (wkv * gain).astype(BF)

    key_received, value_send = lax.optimization_barrier((key_received, value_send))
    partial, value_send = verify_layer(
        gathered,
        wq,
        wkv,
        w_out,
        kv_cache,
        tables,
        lengths,
        accepted.reshape(-1),
        destination,
        value_send,
        0,
    )
    summed = lax.psum_scatter(partial, "tp", scatter_dimension=0, tiled=True)
    value_received = exchange(value_send)
    new_cache = assemble_cache(key_received, value_received)
    out_rows = finish_rows(summed.reshape(-1, PACKED, LANES), rows, parity)
    return (out_rows.reshape(hidden.shape), new_cache)


def solution(mesh):
    in_specs = (
        P("req", None, "tp"),
        P(),
        P(None, "tp"),
        P("tp", None),
        P("tp", None),
        P("req", "tp", None),
        P("req"),
        P("req", None),
        P("req", None),
        P("req"),
    )
    out_specs = (P("req", None, "tp"), P("req", "tp", None))
    return jax.shard_map(
        per_device, mesh=mesh, in_specs=in_specs, out_specs=out_specs, check_vma=False
    )
```

```python
import math

import jax
import jax.numpy as jnp
from jax import lax
from jax.experimental import pallas as pl
from jax.experimental.pallas import tpu as pltpu
from jax.sharding import PartitionSpec as P

H = 32
KVH = 8
HD = 80
D = 2560
TREE = 24
CACHE = 512
DEPTH = 4
N_TP = 8
GROUP = H // KVH
LANES = 128
REQ_BLOCK = 8
ROWS = REQ_BLOCK * TREE
HALF = ROWS // 2
PACKED = 2 * ROWS + HALF
WIDTH = D // N_TP
NEG = -1e30
EXTRA = 16
EARLY = 112
LATE = 2 * HD - EARLY
CHUNKS = 2
BF = jnp.bfloat16
F32 = jnp.float32
VMEM_LIMIT = 56 * 1024 * 1024


def lane_index(shape):
    return lax.broadcasted_iota(jnp.int32, shape, len(shape) - 1)


def swap_halves(tile):
    return pltpu.roll(tile, 64, 1)


def pack_kernel(parity, x_ref, o_ref):
    x = x_ref[...].astype(F32)
    t0 = x[:, 0:128]
    t1 = x[:, 128:256]
    t2 = jnp.concatenate([x[:, 256:320], jnp.zeros((ROWS, 64), F32)], axis=1)
    low = lane_index((ROWS, LANES)) < 64
    low_half = lane_index((HALF, LANES)) < 64
    even = jnp.bitwise_and(parity[0], 1) == 0

    @pl.when(even)
    def _():
        o_ref[0, 0:ROWS] = t0.astype(BF)
        o_ref[0, ROWS : 2 * ROWS] = t1.astype(BF)
        o_ref[0, 2 * ROWS : PACKED] = jnp.where(
            low_half, t2[:HALF], swap_halves(t2[HALF:])
        ).astype(BF)

    @pl.when(jnp.logical_not(even))
    def _():
        s0, s1, s2 = swap_halves(t0), swap_halves(t1), swap_halves(t2)
        o_ref[0, 0:ROWS] = jnp.where(low, s0, s1).astype(BF)
        o_ref[0, ROWS : 2 * ROWS] = jnp.where(low, s1, s2).astype(BF)
        o_ref[0, 2 * ROWS : PACKED] = jnp.where(low_half, t0[:HALF], s0[HALF:]).astype(BF)


def pack_rows(rows, parity, blocks, first_block):
    return pl.pallas_call(
        pack_kernel,
        out_shape=jax.ShapeDtypeStruct((blocks, PACKED, LANES), BF),
        grid_spec=pltpu.PrefetchScalarGridSpec(
            num_scalar_prefetch=1,
            grid=(blocks,),
            in_specs=[pl.BlockSpec((ROWS, WIDTH), lambda b, p: (first_block + b, 0))],
            out_specs=pl.BlockSpec((1, PACKED, LANES), lambda b, p: (b, 0, 0)),
        ),
        name="pack_rows",
    )(parity, rows)


def finish_kernel(parity, s_ref, x_ref, o_ref):
    m0 = s_ref[0, 0:ROWS].astype(F32)
    m1 = s_ref[0, ROWS : 2 * ROWS].astype(F32)
    packed_tail = s_ref[0, 2 * ROWS : PACKED].astype(F32)
    tail = jnp.concatenate([packed_tail, swap_halves(packed_tail)], axis=0)
    low = lane_index((ROWS, LANES)) < 64
    even = jnp.bitwise_and(parity[0], 1) == 0

    @pl.when(even)
    def _():
        total = jnp.concatenate([m0, m1, tail], axis=1)[:, :WIDTH]
        o_ref[...] = (x_ref[...].astype(F32) + total).astype(BF)

    @pl.when(jnp.logical_not(even))
    def _():
        s0, s1 = swap_halves(m0), swap_halves(m1)
        total = jnp.concatenate(
            [jnp.where(low, tail, s0), jnp.where(low, s0, s1), s1], axis=1
        )[:, :WIDTH]
        o_ref[...] = (x_ref[...].astype(F32) + total).astype(BF)


def finish_rows(summed, rows, parity, first_block, done):
    blocks = summed.shape[0]
    kernel = finish_kernel
    operands = (parity, summed, rows)
    in_specs = [
        pl.BlockSpec((1, PACKED, LANES), lambda b, p: (b, 0, 0)),
        pl.BlockSpec((ROWS, WIDTH), lambda b, p: (first_block + b, 0)),
    ]
    aliases = {}
    if done is not None:

        def kernel(parity, s_ref, x_ref, done_ref, o_ref):
            finish_kernel(parity, s_ref, x_ref, o_ref)

        operands += (done,)
        in_specs.append(pl.BlockSpec(memory_space=pl.ANY))
        aliases = {3: 0}
    return pl.pallas_call(
        kernel,
        out_shape=jax.ShapeDtypeStruct(rows.shape, BF),
        grid_spec=pltpu.PrefetchScalarGridSpec(
            num_scalar_prefetch=1,
            grid=(blocks,),
            in_specs=in_specs,
            out_specs=pl.BlockSpec((ROWS, WIDTH), lambda b, p: (first_block + b, 0)),
        ),
        input_output_aliases=aliases,
        name="finish_rows",
    )(*operands)


def prep_kernel(parents_ref, cos_ref, sin_ref, step_ref, bias_out, cos_out, sin_out):
    requests = parents_ref.shape[0]
    lane = lane_index((requests, LANES))
    step_cos = step_ref[0:1, :]
    step_sin = step_ref[1:2, :]
    sign = step_ref[2:3, :]
    parents = parents_ref[...]
    marks = jnp.where(lane == 0, 1.0, 0.0)
    cosines, sines = cos_ref[...], sin_ref[...]
    older = (marks, cosines, sines)
    newer = older
    for t in range(TREE):
        if t > 0:
            near = jnp.broadcast_to(parents[:, t : t + 1], (requests, LANES)) == t - 1
            marks, cosines, sines = (jnp.where(near, a, b) for a, b in zip(newer, older))
            marks = jnp.where(lane == t, 1.0, marks)
            if t > 0:
                cosines, sines = (
                    cosines * step_cos - sines * step_sin,
                    sines * step_cos + cosines * step_sin,
                )
            older, newer = newer, (marks, cosines, sines)
        bias_out[:, t, :] = jnp.where(marks > 0.5, 0.0, NEG)
        cos_out[:, t, :] = cosines
        sin_out[:, t, :] = sines * sign


def prepare_tables(parents, lengths):
    requests = parents.shape[0]
    lane = jnp.arange(LANES)
    pair = jnp.where(lane < HD // 2, lane, lane - HD // 2)
    frequency = 10000.0 ** (-2.0 * pair.astype(F32) / HD)
    angles = lengths.astype(F32)[:, None] * frequency[None, :]
    sign = jnp.where(lane < HD // 2, -1.0, jnp.where(lane < HD, 1.0, 0.0))
    steps = jnp.stack([jnp.cos(frequency), jnp.sin(frequency), sign] + [sign] * 5)
    table = jax.ShapeDtypeStruct((requests, TREE, LANES), F32)
    return pl.pallas_call(
        prep_kernel, out_shape=(table, table, table), name="prepare_tables"
    )(parents, jnp.cos(angles), jnp.sin(angles), steps)


def order_kernel(order, cache_ref, early_ref, late_ref, buffer, load_sems, early_sems, late_sems):
    loads, stores = [], []
    for d in range(cache_ref.shape[0]):
        loads.append(
            pltpu.make_async_copy(cache_ref.at[order[d]], buffer.at[d], load_sems.at[d])
        )
        loads[-1].start()
    for d, load in enumerate(loads):
        load.wait()
        stores.append(
            pltpu.make_async_copy(buffer.at[d, pl.ds(0, EARLY)], early_ref.at[d], early_sems.at[d])
        )
        stores.append(
            pltpu.make_async_copy(
                buffer.at[d, pl.ds(EARLY, LATE)], late_ref.at[d, pl.ds(0, LATE)], late_sems.at[d]
            )
        )
        stores[-2].start()
        stores[-1].start()
    for store in stores:
        store.wait()


def order_cache(kv_cache, send_order):
    held = kv_cache.shape[0]
    return pl.pallas_call(
        order_kernel,
        out_shape=(
            jax.ShapeDtypeStruct((held, EARLY, CACHE), BF),
            jax.ShapeDtypeStruct((held, LATE + EXTRA, CACHE), BF),
        ),
        grid_spec=pltpu.PrefetchScalarGridSpec(
            num_scalar_prefetch=1,
            grid=(1,),
            in_specs=[pl.BlockSpec(memory_space=pl.ANY)],
            out_specs=(pl.BlockSpec(memory_space=pl.ANY), pl.BlockSpec(memory_space=pl.ANY)),
            scratch_shapes=[
                pltpu.VMEM(kv_cache.shape, BF),
                pltpu.SemaphoreType.DMA((held,)),
                pltpu.SemaphoreType.DMA((held,)),
                pltpu.SemaphoreType.DMA((held,)),
            ],
        ),
        compiler_params=pltpu.CompilerParams(vmem_limit_bytes=VMEM_LIMIT),
        name="order_cache",
    )(send_order, kv_cache)


def layer_kernel(
    lengths,
    accepted,
    destination,
    x_ref,
    wq_ref,
    wkv_ref,
    wo_ref,
    cache_ref,
    bias_ref,
    cos_ref,
    sin_ref,
    send_in,
    out_ref,
    send_out,
    xs,
    qkv,
    ctx,
    wo,
    extra,
    sems,
    *,
    first_block,
):
    b = pl.program_id(0)

    @pl.when(b == 0)
    def _():
        wo[...] = jnp.zeros_like(wo)
        for h in range(GROUP):
            wo[h * LANES : h * LANES + HD] = wo_ref[h * HD : (h + 1) * HD]
        ctx[...] = jnp.zeros_like(ctx)
        extra[...] = jnp.zeros_like(extra)

    low_half = lane_index((HALF, LANES)) < 64
    squares = jnp.zeros((ROWS, LANES), F32)
    for j in range(N_TP // 2):
        base = j * 5 * LANES
        for device, at in ((2 * j, base), (2 * j + 1, base + 3 * LANES)):
            for part in range(2):
                piece = x_ref[device, 0, part * ROWS : (part + 1) * ROWS]
                xs[:, at + part * LANES : at + (part + 1) * LANES] = piece
                wide = piece.astype(F32)
                squares = squares + wide * wide
        even_tail = x_ref[2 * j, 0, 2 * ROWS : PACKED].astype(F32)
        odd_tail = x_ref[2 * j + 1, 0, 2 * ROWS : PACKED].astype(F32)
        tail = jnp.concatenate(
            [
                jnp.where(low_half, even_tail, swap_halves(odd_tail)),
                jnp.where(low_half, swap_halves(even_tail), odd_tail),
            ],
            axis=0,
        )
        xs[:, base + 2 * LANES : base + 3 * LANES] = tail.astype(BF)
        squares = squares + tail * tail
    scale = lax.rsqrt(jnp.sum(squares, axis=1, keepdims=True) * (1.0 / D) + 1e-05)
    flat = xs[...]
    query = jnp.dot(flat, wq_ref[...], preferred_element_type=F32) * scale
    keyval = jnp.dot(flat, wkv_ref[...], preferred_element_type=F32) * scale
    cosines = cos_ref[...].reshape(ROWS, LANES)
    sines = sin_ref[...].reshape(ROWS, LANES)
    first = lane_index((ROWS, LANES)) < HD // 2

    def rotate(tile):
        other = jnp.where(
            first, pltpu.roll(tile, LANES - HD // 2, 1), pltpu.roll(tile, HD // 2, 1)
        )
        return tile * cosines + other * sines

    for h in range(GROUP):
        qkv[:, h * LANES : (h + 1) * LANES] = rotate(query[:, h * LANES : (h + 1) * LANES])
    qkv[:, GROUP * LANES : (GROUP + 1) * LANES] = rotate(keyval[:, :LANES])
    qkv[:, (GROUP + 1) * LANES :] = keyval[:, LANES:]

    factor = math.log2(math.e) / math.sqrt(HD)
    column = lane_index((GROUP * TREE, CACHE))
    extra_row = lax.broadcasted_iota(jnp.int32, (EXTRA, LANES), 0)
    extra_lane = lane_index((EXTRA, LANES))
    pick_row = lax.broadcasted_iota(jnp.int32, (EXTRA, TREE), 0)
    pick_column = lane_index((EXTRA, TREE))
    copies = []
    for i in range(REQ_BLOCK):
        r = (first_block + b) * REQ_BLOCK + i
        length = lengths[r]
        rows = slice(i * TREE, (i + 1) * TREE)
        q = jnp.concatenate(
            [qkv[rows, h * LANES : (h + 1) * LANES] for h in range(GROUP)], axis=0
        ).astype(BF)
        k = qkv[rows, GROUP * LANES : (GROUP + 1) * LANES].astype(BF)
        v = qkv[rows, (GROUP + 1) * LANES :].astype(BF)
        cached = jnp.dot(q[:, :HD], cache_ref[i, 0:HD], preferred_element_type=F32)
        cached = jnp.where(column < length, cached * factor, NEG)
        fresh = lax.dot_general(q, k, (((1,), (1,)), ((), ())), preferred_element_type=F32)
        bias = bias_ref[i][:, :TREE]
        fresh = fresh * factor + jnp.concatenate([bias] * GROUP, axis=0)
        top = jnp.maximum(
            jnp.max(cached, axis=1, keepdims=True), jnp.max(fresh, axis=1, keepdims=True)
        )
        cached = jnp.exp2(cached - top)
        fresh = jnp.exp2(fresh - top)
        total = jnp.sum(cached, axis=1, keepdims=True) + jnp.sum(fresh, axis=1, keepdims=True)
        mixed = lax.dot_general(
            cached.astype(BF),
            cache_ref[i, HD : 2 * HD],
            (((1,), (1,)), ((), ())),
            preferred_element_type=F32,
        ) + jnp.dot(fresh.astype(BF), v[:, :HD], preferred_element_type=F32)
        mixed = mixed / total
        for h in range(GROUP):
            ctx[rows, h * LANES : h * LANES + HD] = mixed[h * TREE : (h + 1) * TREE]

        wanted = jnp.full((EXTRA, TREE), -1, jnp.int32)
        for m in range(DEPTH):
            wanted = jnp.where(pick_row == m, accepted[r * DEPTH + m], wanted)
        pick = jnp.where(pick_column == wanted, 1.0, 0.0).astype(BF)
        new_keys = jnp.dot(pick, k, preferred_element_type=F32)
        new_values = jnp.dot(pick, v, preferred_element_type=F32)
        coarse = (length // 16).astype(F32)
        fine = (length % 16).astype(F32)
        shifted = pltpu.roll(new_values, HD, 1)
        new_keys = jnp.where(extra_lane < HD, new_keys, shifted)
        extra[i, :, 0:LANES] = jnp.where(
            extra_row == 8, coarse, jnp.where(extra_row == 9, fine, new_keys)
        ).astype(BF)
        extra[i, :, LANES : 2 * LANES] = jnp.where(
            extra_lane < 2 * HD - LANES, shifted, 0.0
        ).astype(BF)
        copies.append(
            pltpu.make_async_copy(
                extra.at[i], send_out.at[destination[r], pl.ds(LATE, EXTRA)], sems.at[i]
            )
        )
        copies[-1].start()

    partial = jnp.dot(ctx[...].astype(BF), wo[...], preferred_element_type=F32)
    for j in range(N_TP // 2):
        base = j * 5 * LANES
        for device, at in ((2 * j, base), (2 * j + 1, base + 3 * LANES)):
            for part in range(2):
                out_ref[device, 0, part * ROWS : (part + 1) * ROWS] = partial[
                    :, at + part * LANES : at + (part + 1) * LANES
                ].astype(BF)
        tail = partial[:, base + 2 * LANES : base + 3 * LANES]
        out_ref[2 * j, 0, 2 * ROWS : PACKED] = jnp.where(
            low_half, tail[:HALF], swap_halves(tail[HALF:])
        ).astype(BF)
        out_ref[2 * j + 1, 0, 2 * ROWS : PACKED] = jnp.where(
            low_half, swap_halves(tail[:HALF]), tail[HALF:]
        ).astype(BF)
    for copy in copies:
        copy.wait()


def verify_layer(
    gathered, wq, wkv, w_out, kv_cache, tables, lengths, accepted, destination, send, first_block
):
    blocks = gathered.shape[1]
    full = lambda b, *_: (0, 0)
    packed = pl.BlockSpec((N_TP, 1, PACKED, LANES), lambda b, *_: (0, b, 0, 0))
    table = pl.BlockSpec((REQ_BLOCK, TREE, LANES), lambda b, *_: (first_block + b, 0, 0))
    anywhere = pl.BlockSpec(memory_space=pl.ANY)

    def body(*refs):
        layer_kernel(*refs, first_block=first_block)

    return pl.pallas_call(
        body,
        out_shape=(
            jax.ShapeDtypeStruct((N_TP, blocks, PACKED, LANES), BF),
            jax.ShapeDtypeStruct(send.shape, BF),
        ),
        grid_spec=pltpu.PrefetchScalarGridSpec(
            num_scalar_prefetch=3,
            grid=(blocks,),
            in_specs=[
                packed,
                pl.BlockSpec(wq.shape, full),
                pl.BlockSpec(wkv.shape, full),
                pl.BlockSpec(w_out.shape, full),
                pl.BlockSpec(
                    (REQ_BLOCK, 2 * HD, CACHE), lambda b, *_: (first_block + b, 0, 0)
                ),
                table,
                table,
                table,
                anywhere,
            ],
            out_specs=(packed, anywhere),
            scratch_shapes=[
                pltpu.VMEM((ROWS, D), BF),
                pltpu.VMEM((ROWS, (GROUP + 2) * LANES), F32),
                pltpu.VMEM((ROWS, GROUP * LANES), F32),
                pltpu.VMEM((GROUP * LANES, D), BF),
                pltpu.VMEM((REQ_BLOCK, EXTRA, CACHE), BF),
                pltpu.SemaphoreType.DMA((REQ_BLOCK,)),
            ],
        ),
        input_output_aliases={11: 1},
        compiler_params=pltpu.CompilerParams(vmem_limit_bytes=VMEM_LIMIT),
        name="verify_layer",
    )(
        lengths,
        accepted,
        destination,
        gathered,
        wq,
        wkv,
        w_out,
        kv_cache,
        *tables,
        send,
    )


def assemble_kernel(early_ref, late_ref, o_ref):
    place_row = lax.broadcasted_iota(jnp.int32, (EXTRA, CACHE), 0)
    place_column = lane_index((EXTRA, CACHE))
    for i in range(early_ref.shape[0]):
        extra = late_ref[i, LATE : LATE + EXTRA, : 2 * LANES]
        wide = extra[:, :LANES].astype(F32)
        length = (wide[8:9] * 16.0 + wide[9:10]).astype(jnp.int32)
        length = jnp.concatenate([length] * (CACHE // LANES), axis=1)
        offset = place_column - length
        place = jnp.where(
            jnp.logical_and(offset == place_row, place_row < DEPTH), 1.0, 0.0
        ).astype(BF)
        live = jnp.where(offset[0:1] < 0, 1.0, 0.0).astype(BF)
        new = lax.dot_general(
            extra, place, (((0,), (0,)), ((), ())), preferred_element_type=F32
        ).astype(BF)
        o_ref[i, 0:EARLY] = early_ref[i] * live + new[0:EARLY]
        o_ref[i, EARLY : 2 * HD] = late_ref[i, 0:LATE] * live + new[EARLY : 2 * HD]


def assemble_cache(early, late):
    held = early.shape[0]
    step = 4
    return pl.pallas_call(
        assemble_kernel,
        out_shape=jax.ShapeDtypeStruct((held, 2 * HD, CACHE), BF),
        grid=(held // step,),
        in_specs=[
            pl.BlockSpec((step, EARLY, CACHE), lambda s: (s, 0, 0)),
            pl.BlockSpec((step, LATE + EXTRA, CACHE), lambda s: (s, 0, 0)),
        ],
        out_specs=pl.BlockSpec((step, 2 * HD, CACHE), lambda s: (s, 0, 0)),
        name="assemble_cache",
    )(early, late)


def spread_heads(heads):
    source = jnp.arange(heads * HD)[:, None]
    target = jnp.arange(heads * LANES)[None, :]
    return (source // HD * LANES + source % HD == target).astype(BF)


def exchange(values):
    return lax.all_to_all(values, "req", split_axis=0, concat_axis=0, tiled=True)


def per_device(
    hidden, norm_gain, w_query, w_keyval, w_out, kv_cache, lengths, parents, accepted, slot_of
):
    held = hidden.shape[0]
    rows = hidden.reshape(held * TREE, WIDTH)
    parity = lax.axis_index("tp").astype(jnp.int32).reshape(1)
    blocks = held // REQ_BLOCK // CHUNKS
    gathered = []
    for c in range(CHUNKS):
        packed = pack_rows(rows, parity, blocks, c * blocks)
        gathered.append(lax.all_gather(packed, "tp", axis=0, tiled=False))

    destination = slot_of // held
    peer_index = jnp.arange(held, dtype=jnp.int32)
    matches = (destination[None, :] == peer_index[:, None]).astype(jnp.int32)
    send_order = jnp.sum(matches * peer_index[None, :], axis=1)
    early, late = order_cache(kv_cache, send_order)
    early = exchange(early)

    tables = prepare_tables(parents, lengths)
    gain = norm_gain[:, None]
    wq = (jnp.dot(w_query, spread_heads(GROUP), preferred_element_type=F32) * gain).astype(BF)
    wkv = lax.dot_general(
        w_keyval, spread_heads(2), (((0,), (0,)), ((), ())), preferred_element_type=F32
    )
    wkv = (wkv * gain).astype(BF)

    summed = []
    for c in range(CHUNKS):
        if c == CHUNKS - 1:
            early, late = lax.optimization_barrier((early, late))
        partial, late = verify_layer(
            gathered[c],
            wq,
            wkv,
            w_out,
            kv_cache,
            tables,
            lengths,
            accepted.reshape(-1),
            destination,
            late,
            c * blocks,
        )
        summed.append(lax.psum_scatter(partial, "tp", scatter_dimension=0, tiled=True))
    late = exchange(late)
    new_cache = assemble_cache(early, late)
    out_rows = None
    for c in range(CHUNKS):
        out_rows = finish_rows(
            summed[c].reshape(-1, PACKED, LANES), rows, parity, c * blocks, out_rows
        )
    return (out_rows.reshape(hidden.shape), new_cache)


def solution(mesh):
    in_specs = (
        P("req", None, "tp"),
        P(),
        P(None, "tp"),
        P("tp", None),
        P("tp", None),
        P("req", "tp", None),
        P("req"),
        P("req", None),
        P("req", None),
        P("req"),
    )
    out_specs = (P("req", None, "tp"), P("req", "tp", None))
    return jax.shard_map(
        per_device, mesh=mesh, in_specs=in_specs, out_specs=out_specs, check_vma=False
    )
```

```python
import math

import jax
import jax.numpy as jnp
from jax import lax
from jax.experimental import pallas as pl
from jax.experimental.pallas import tpu as pltpu
from jax.sharding import PartitionSpec as P

H = 32
KVH = 8
HD = 80
D = 2560
TREE = 24
CACHE = 512
DEPTH = 4
N_TP = 8
GROUP = H // KVH
LANES = 128
REQ_BLOCK = 8
ROWS = REQ_BLOCK * TREE
HALF = ROWS // 2
PACKED = 2 * ROWS + HALF
WIDTH = D // N_TP
NEG = -1e30
EXTRA = 16
HALF_BLOCKS = 2
BF = jnp.bfloat16
F32 = jnp.float32
VMEM_LIMIT = 56 * 1024 * 1024


def lane_index(shape):
    return lax.broadcasted_iota(jnp.int32, shape, len(shape) - 1)


def swap_halves(tile):
    return pltpu.roll(tile, 64, 1)


def pack_kernel(parity, x_ref, o_ref):
    x = x_ref[...].astype(F32)
    t0 = x[:, 0:128]
    t1 = x[:, 128:256]
    t2 = jnp.concatenate([x[:, 256:320], jnp.zeros((ROWS, 64), F32)], axis=1)
    low = lane_index((ROWS, LANES)) < 64
    low_half = lane_index((HALF, LANES)) < 64
    even = jnp.bitwise_and(parity[0], 1) == 0

    @pl.when(even)
    def _():
        o_ref[0, 0:ROWS] = t0.astype(BF)
        o_ref[0, ROWS : 2 * ROWS] = t1.astype(BF)
        o_ref[0, 2 * ROWS : PACKED] = jnp.where(
            low_half, t2[:HALF], swap_halves(t2[HALF:])
        ).astype(BF)

    @pl.when(jnp.logical_not(even))
    def _():
        s0, s1, s2 = swap_halves(t0), swap_halves(t1), swap_halves(t2)
        o_ref[0, 0:ROWS] = jnp.where(low, s0, s1).astype(BF)
        o_ref[0, ROWS : 2 * ROWS] = jnp.where(low, s1, s2).astype(BF)
        o_ref[0, 2 * ROWS : PACKED] = jnp.where(low_half, t0[:HALF], s0[HALF:]).astype(BF)


def pack_rows(rows, parity):
    blocks = rows.shape[0] // ROWS
    return pl.pallas_call(
        pack_kernel,
        out_shape=jax.ShapeDtypeStruct((blocks, PACKED, LANES), BF),
        grid_spec=pltpu.PrefetchScalarGridSpec(
            num_scalar_prefetch=1,
            grid=(blocks,),
            in_specs=[pl.BlockSpec((ROWS, WIDTH), lambda b, p: (b, 0))],
            out_specs=pl.BlockSpec((1, PACKED, LANES), lambda b, p: (b, 0, 0)),
        ),
        name="pack_rows",
    )(parity, rows)


def finish_kernel(parity, own_ref, up_ref, down_ref, x_ref, o_ref):
    packed = (
        own_ref[0].astype(F32) + up_ref[0].astype(F32) + down_ref[0].astype(F32)
    )
    m0 = packed[0:ROWS]
    m1 = packed[ROWS : 2 * ROWS]
    packed_tail = packed[2 * ROWS : PACKED]
    tail = jnp.concatenate([packed_tail, swap_halves(packed_tail)], axis=0)
    low = lane_index((ROWS, LANES)) < 64
    even = jnp.bitwise_and(parity[0], 1) == 0

    @pl.when(even)
    def _():
        total = jnp.concatenate([m0, m1, tail], axis=1)[:, :WIDTH]
        o_ref[...] = (x_ref[...].astype(F32) + total).astype(BF)

    @pl.when(jnp.logical_not(even))
    def _():
        s0, s1 = swap_halves(m0), swap_halves(m1)
        total = jnp.concatenate(
            [jnp.where(low, tail, s0), jnp.where(low, s0, s1), s1], axis=1
        )[:, :WIDTH]
        o_ref[...] = (x_ref[...].astype(F32) + total).astype(BF)


def finish_rows(own, up, down, rows, parity):
    blocks = rows.shape[0] // ROWS
    packed = pl.BlockSpec((1, PACKED, LANES), lambda b, p: (b, 0, 0))
    flat = pl.BlockSpec((ROWS, WIDTH), lambda b, p: (b, 0))
    return pl.pallas_call(
        finish_kernel,
        out_shape=jax.ShapeDtypeStruct(rows.shape, BF),
        grid_spec=pltpu.PrefetchScalarGridSpec(
            num_scalar_prefetch=1,
            grid=(blocks,),
            in_specs=[packed, packed, packed, flat],
            out_specs=flat,
        ),
        name="finish_rows",
    )(parity, own, up, down, rows)


def arrange_kernel(me, wq_ref, wkv_ref, wo_ref, w_ref, o_ref):
    o_ref[...] = jnp.zeros_like(o_ref)
    query = GROUP * LANES
    low = lane_index((GROUP * HD, LANES)) < 64
    for j in range(N_TP // 2):
        base = j * 5 * LANES
        tails = []
        for k, at, tail_at in (
            (2 * j, base, base + 256),
            (2 * j + 1, base + 384, base + 320),
        ):
            device = jnp.bitwise_and(me[0] + k, N_TP - 1)
            odd = jnp.bitwise_and(device, 1)
            main_from = pl.multiple_of(device * WIDTH + 64 * odd, 64)
            tail_from = pl.multiple_of(device * WIDTH + 256 * (1 - odd), 64)
            w_ref[at : at + 256, :query] = wq_ref[pl.ds(main_from, 256), :]
            w_ref[at : at + 256, query:] = wkv_ref[pl.ds(main_from, 256), :]
            w_ref[tail_at : tail_at + 64, :query] = wq_ref[pl.ds(tail_from, 64), :]
            w_ref[tail_at : tail_at + 64, query:] = wkv_ref[pl.ds(tail_from, 64), :]
            tile = device // 2 * 5
            for part in range(2):
                column = pl.multiple_of((tile + 3 * odd + part) * LANES, LANES)
                piece = wo_ref[:, pl.ds(column, LANES)]
                for h in range(GROUP):
                    o_ref[
                        h * LANES : h * LANES + HD,
                        at + part * LANES : at + (part + 1) * LANES,
                    ] = piece[h * HD : (h + 1) * HD]
            column = pl.multiple_of((tile + 2) * LANES, LANES)
            tail = wo_ref[:, pl.ds(column, LANES)].astype(F32)
            wrong = odd == (1 - k % 2)
            tails.append(jnp.where(wrong, swap_halves(tail), tail))
        joined = jnp.where(low, tails[0], tails[1]).astype(BF)
        for h in range(GROUP):
            o_ref[h * LANES : h * LANES + HD, base + 256 : base + 384] = joined[
                h * HD : (h + 1) * HD
            ]


def arrange_weights(wq, wkv, w_out, me):
    return pl.pallas_call(
        arrange_kernel,
        out_shape=(
            jax.ShapeDtypeStruct((D, (GROUP + 2) * LANES), BF),
            jax.ShapeDtypeStruct((GROUP * LANES, D), BF),
        ),
        in_specs=[pl.BlockSpec(memory_space=pltpu.SMEM)]
        + [pl.BlockSpec(memory_space=pltpu.VMEM)] * 3,
        out_specs=(
            pl.BlockSpec(memory_space=pltpu.VMEM),
            pl.BlockSpec(memory_space=pltpu.VMEM),
        ),
        compiler_params=pltpu.CompilerParams(vmem_limit_bytes=VMEM_LIMIT),
        name="arrange_weights",
    )(me, wq, wkv, w_out)


def prep_kernel(parents_ref, cos_ref, sin_ref, step_ref, bias_out, cos_out, sin_out):
    requests = parents_ref.shape[0]
    lane = lane_index((requests, LANES))
    step_cos = step_ref[0:1, :]
    step_sin = step_ref[1:2, :]
    sign = step_ref[2:3, :]
    parents = parents_ref[...]
    marks = jnp.where(lane == 0, 1.0, 0.0)
    cosines, sines = cos_ref[...], sin_ref[...]
    older = (marks, cosines, sines)
    newer = older
    for t in range(TREE):
        if t > 0:
            near = jnp.broadcast_to(parents[:, t : t + 1], (requests, LANES)) == t - 1
            marks, cosines, sines = (jnp.where(near, a, b) for a, b in zip(newer, older))
            marks = jnp.where(lane == t, 1.0, marks)
            if t > 0:
                cosines, sines = (
                    cosines * step_cos - sines * step_sin,
                    sines * step_cos + cosines * step_sin,
                )
            older, newer = newer, (marks, cosines, sines)
        bias_out[:, t, :] = jnp.where(marks > 0.5, 0.0, NEG)
        cos_out[:, t, :] = cosines
        sin_out[:, t, :] = sines * sign


def prepare_tables(parents, lengths):
    requests = parents.shape[0]
    lane = jnp.arange(LANES)
    pair = jnp.where(lane < HD // 2, lane, lane - HD // 2)
    frequency = 10000.0 ** (-2.0 * pair.astype(F32) / HD)
    angles = lengths.astype(F32)[:, None] * frequency[None, :]
    sign = jnp.where(lane < HD // 2, -1.0, jnp.where(lane < HD, 1.0, 0.0))
    steps = jnp.stack([jnp.cos(frequency), jnp.sin(frequency), sign] + [sign] * 5)
    table = jax.ShapeDtypeStruct((requests, TREE, LANES), F32)
    return pl.pallas_call(
        prep_kernel, out_shape=(table, table, table), name="prepare_tables"
    )(parents, jnp.cos(angles), jnp.sin(angles), steps)


def order_kernel(order, cache_ref, out_ref, buffer, load_sems, store_sems):
    loads, stores = [], []
    for d in range(cache_ref.shape[0]):
        loads.append(
            pltpu.make_async_copy(cache_ref.at[order[d]], buffer.at[d], load_sems.at[d])
        )
        loads[-1].start()
    for d, load in enumerate(loads):
        load.wait()
        stores.append(pltpu.make_async_copy(buffer.at[d], out_ref.at[d], store_sems.at[d]))
        stores[-1].start()
    for store in stores:
        store.wait()


def order_cache(kv_cache, send_order):
    held = kv_cache.shape[0]
    return pl.pallas_call(
        order_kernel,
        out_shape=jax.ShapeDtypeStruct(kv_cache.shape, BF),
        grid_spec=pltpu.PrefetchScalarGridSpec(
            num_scalar_prefetch=1,
            grid=(1,),
            in_specs=[pl.BlockSpec(memory_space=pl.ANY)],
            out_specs=pl.BlockSpec(memory_space=pl.ANY),
            scratch_shapes=[
                pltpu.VMEM(kv_cache.shape, BF),
                pltpu.SemaphoreType.DMA((held,)),
                pltpu.SemaphoreType.DMA((held,)),
            ],
        ),
        compiler_params=pltpu.CompilerParams(vmem_limit_bytes=VMEM_LIMIT),
        name="order_cache",
    )(send_order, kv_cache)


def layer_kernel(lengths, accepted, destination, *refs):
    x_refs = refs[: N_TP + 1]
    w_ref, wo_ref, cache_ref, bias_ref, cos_ref, sin_ref = refs[N_TP + 1 : N_TP + 7]
    out_refs = refs[N_TP + 7 : 2 * N_TP + 7]
    extra_out, xs, qkv, ctx, extra, sems = refs[2 * N_TP + 7 :]
    b = pl.program_id(0)

    @pl.when(b == 0)
    def _():
        ctx[...] = jnp.zeros_like(ctx)
        extra[...] = jnp.zeros_like(extra)

    def received(k, first, last):
        piece = x_refs[k][0, first:last]
        if k == N_TP // 2:
            piece = jnp.where(b < HALF_BLOCKS, piece, x_refs[N_TP][0, first:last])
        return piece

    low_half = lane_index((HALF, LANES)) < 64
    squares = jnp.zeros((ROWS, LANES), F32)
    for j in range(N_TP // 2):
        base = j * 5 * LANES
        for device, at in ((2 * j, base), (2 * j + 1, base + 3 * LANES)):
            for part in range(2):
                piece = received(device, part * ROWS, (part + 1) * ROWS)
                xs[:, at + part * LANES : at + (part + 1) * LANES] = piece
                wide = piece.astype(F32)
                squares = squares + wide * wide
        even_tail = received(2 * j, 2 * ROWS, PACKED).astype(F32)
        odd_tail = received(2 * j + 1, 2 * ROWS, PACKED).astype(F32)
        tail = jnp.concatenate(
            [
                jnp.where(low_half, even_tail, swap_halves(odd_tail)),
                jnp.where(low_half, swap_halves(even_tail), odd_tail),
            ],
            axis=0,
        )
        xs[:, base + 2 * LANES : base + 3 * LANES] = tail.astype(BF)
        squares = squares + tail * tail
    scale = lax.rsqrt(jnp.sum(squares, axis=1, keepdims=True) * (1.0 / D) + 1e-05)
    flat = xs[...]
    projected = jnp.dot(flat, w_ref[...], preferred_element_type=F32) * scale
    cosines = cos_ref[...].reshape(ROWS, LANES)
    sines = sin_ref[...].reshape(ROWS, LANES)
    first = lane_index((ROWS, LANES)) < HD // 2

    def rotate(tile):
        other = jnp.where(
            first, pltpu.roll(tile, LANES - HD // 2, 1), pltpu.roll(tile, HD // 2, 1)
        )
        return tile * cosines + other * sines

    for h in range(GROUP + 1):
        head = slice(h * LANES, (h + 1) * LANES)
        qkv[:, head] = rotate(projected[:, head])
    qkv[:, (GROUP + 1) * LANES :] = projected[:, (GROUP + 1) * LANES :]

    factor = math.log2(math.e) / math.sqrt(HD)
    column = lane_index((GROUP * TREE, CACHE))
    extra_row = lax.broadcasted_iota(jnp.int32, (EXTRA, LANES), 0)
    extra_lane = lane_index((EXTRA, LANES))
    pick_row = lax.broadcasted_iota(jnp.int32, (EXTRA, TREE), 0)
    pick_column = lane_index((EXTRA, TREE))
    copies = []
    for i in range(REQ_BLOCK):
        r = b * REQ_BLOCK + i
        length = lengths[r]
        rows = slice(i * TREE, (i + 1) * TREE)
        q = jnp.concatenate(
            [qkv[rows, h * LANES : (h + 1) * LANES] for h in range(GROUP)], axis=0
        ).astype(BF)
        k = qkv[rows, GROUP * LANES : (GROUP + 1) * LANES].astype(BF)
        v = qkv[rows, (GROUP + 1) * LANES :].astype(BF)
        cached = jnp.dot(q[:, :HD], cache_ref[i, 0:HD], preferred_element_type=F32)
        cached = jnp.where(column < length, cached * factor, NEG)
        fresh = lax.dot_general(q, k, (((1,), (1,)), ((), ())), preferred_element_type=F32)
        bias = bias_ref[i][:, :TREE]
        fresh = fresh * factor + jnp.concatenate([bias] * GROUP, axis=0)
        top = jnp.maximum(
            jnp.max(cached, axis=1, keepdims=True), jnp.max(fresh, axis=1, keepdims=True)
        )
        cached = jnp.exp2(cached - top)
        fresh = jnp.exp2(fresh - top)
        total = jnp.sum(cached, axis=1, keepdims=True) + jnp.sum(fresh, axis=1, keepdims=True)
        mixed = lax.dot_general(
            cached.astype(BF),
            cache_ref[i, HD : 2 * HD],
            (((1,), (1,)), ((), ())),
            preferred_element_type=F32,
        ) + jnp.dot(fresh.astype(BF), v[:, :HD], preferred_element_type=F32)
        mixed = mixed / total
        for h in range(GROUP):
            ctx[rows, h * LANES : h * LANES + HD] = mixed[h * TREE : (h + 1) * TREE]

        wanted = jnp.full((EXTRA, TREE), -1, jnp.int32)
        for m in range(DEPTH):
            wanted = jnp.where(pick_row == m, accepted[r * DEPTH + m], wanted)
        pick = jnp.where(pick_column == wanted, 1.0, 0.0).astype(BF)
        new_keys = jnp.dot(pick, k, preferred_element_type=F32)
        new_values = jnp.dot(pick, v, preferred_element_type=F32)
        coarse = (length // 16).astype(F32)
        fine = (length % 16).astype(F32)
        shifted = pltpu.roll(new_values, HD, 1)
        new_keys = jnp.where(extra_lane < HD, new_keys, shifted)
        extra[i, :, 0:LANES] = jnp.where(
            extra_row == 8, coarse, jnp.where(extra_row == 9, fine, new_keys)
        ).astype(BF)
        extra[i, :, LANES : 2 * LANES] = jnp.where(
            extra_lane < 2 * HD - LANES, shifted, 0.0
        ).astype(BF)
        copies.append(
            pltpu.make_async_copy(
                extra.at[i], extra_out.at[destination[r]], sems.at[i]
            )
        )
        copies[-1].start()

    partial = jnp.dot(ctx[...].astype(BF), wo_ref[...], preferred_element_type=F32)
    for j in range(N_TP // 2):
        base = j * 5 * LANES
        for device, at in ((2 * j, base), (2 * j + 1, base + 3 * LANES)):
            for part in range(2):
                out_refs[device][0, part * ROWS : (part + 1) * ROWS] = partial[
                    :, at + part * LANES : at + (part + 1) * LANES
                ].astype(BF)
        tail = partial[:, base + 2 * LANES : base + 3 * LANES]
        out_refs[2 * j][0, 2 * ROWS : PACKED] = jnp.where(
            low_half, tail[:HALF], swap_halves(tail[HALF:])
        ).astype(BF)
        out_refs[2 * j + 1][0, 2 * ROWS : PACKED] = jnp.where(
            low_half, swap_halves(tail[:HALF]), tail[HALF:]
        ).astype(BF)
    for copy in copies:
        copy.wait()


def verify_layer(parts, w, wo, kv_cache, tables, lengths, accepted, destination):
    held = kv_cache.shape[0]
    blocks = held // REQ_BLOCK
    full = lambda b, *_: (0, 0)
    packed = pl.BlockSpec((1, PACKED, LANES), lambda b, *_: (b, 0, 0))
    table = pl.BlockSpec((REQ_BLOCK, TREE, LANES), lambda b, *_: (b, 0, 0))
    in_specs = [packed] * (N_TP + 1)
    in_specs[N_TP // 2] = pl.BlockSpec(
        (1, PACKED, LANES), lambda b, *_: (jnp.minimum(b, HALF_BLOCKS - 1), 0, 0)
    )
    in_specs[N_TP] = pl.BlockSpec(
        (1, PACKED, LANES), lambda b, *_: (jnp.maximum(b - HALF_BLOCKS, 0), 0, 0)
    )
    return pl.pallas_call(
        layer_kernel,
        out_shape=[jax.ShapeDtypeStruct((blocks, PACKED, LANES), BF)] * N_TP
        + [jax.ShapeDtypeStruct((held, EXTRA, 2 * LANES), BF)],
        grid_spec=pltpu.PrefetchScalarGridSpec(
            num_scalar_prefetch=3,
            grid=(blocks,),
            in_specs=in_specs
            + [
                pl.BlockSpec(w.shape, full),
                pl.BlockSpec(wo.shape, full),
                pl.BlockSpec((REQ_BLOCK, 2 * HD, CACHE), lambda b, *_: (b, 0, 0)),
                table,
                table,
                table,
            ],
            out_specs=[packed] * N_TP + [pl.BlockSpec(memory_space=pl.ANY)],
            scratch_shapes=[
                pltpu.VMEM((ROWS, D), BF),
                pltpu.VMEM((ROWS, (GROUP + 2) * LANES), F32),
                pltpu.VMEM((ROWS, GROUP * LANES), F32),
                pltpu.VMEM((REQ_BLOCK, EXTRA, 2 * LANES), BF),
                pltpu.SemaphoreType.DMA((REQ_BLOCK,)),
            ],
        ),
        compiler_params=pltpu.CompilerParams(vmem_limit_bytes=VMEM_LIMIT),
        cost_estimate=pl.CostEstimate(
            flops=30_000_000_000, transcendentals=0, bytes_accessed=10_000_000
        ),
        name="verify_layer",
    )(lengths, accepted, destination, *parts, w, wo, kv_cache, *tables)


def assemble_kernel(cache_ref, extra_ref, o_ref):
    place_row = lax.broadcasted_iota(jnp.int32, (EXTRA, CACHE), 0)
    place_column = lane_index((EXTRA, CACHE))
    for i in range(cache_ref.shape[0]):
        extra = extra_ref[i]
        wide = extra[:, :LANES].astype(F32)
        length = (wide[8:9] * 16.0 + wide[9:10]).astype(jnp.int32)
        length = jnp.concatenate([length] * (CACHE // LANES), axis=1)
        offset = place_column - length
        place = jnp.where(
            jnp.logical_and(offset == place_row, place_row < DEPTH), 1.0, 0.0
        ).astype(BF)
        live = jnp.where(offset[0:1] < 0, 1.0, 0.0).astype(BF)
        new = lax.dot_general(
            extra, place, (((0,), (0,)), ((), ())), preferred_element_type=F32
        ).astype(BF)
        o_ref[i] = cache_ref[i] * live + new[: 2 * HD]


def assemble_cache(cached, extra):
    step = 4
    cache_spec = pl.BlockSpec((step,) + cached.shape[1:], lambda s: (s, 0, 0))
    extra_spec = pl.BlockSpec((step,) + extra.shape[1:], lambda s: (s, 0, 0))
    return pl.pallas_call(
        assemble_kernel,
        out_shape=jax.ShapeDtypeStruct(cached.shape, BF),
        grid=(cached.shape[0] // step,),
        in_specs=[cache_spec, extra_spec],
        out_specs=cache_spec,
        name="assemble_cache",
    )(cached, extra)


def spread_heads(heads):
    source = jnp.arange(heads * HD)[:, None]
    target = jnp.arange(heads * LANES)[None, :]
    return (source // HD * LANES + source % HD == target).astype(BF)


def exchange(values):
    return lax.all_to_all(values, "req", split_axis=0, concat_axis=0, tiled=True)


def go_up(values):
    return lax.ppermute(values, "tp", [(i, (i + 1) % N_TP) for i in range(N_TP)])


def go_down(values):
    return lax.ppermute(values, "tp", [(i, (i - 1) % N_TP) for i in range(N_TP)])


def add_up(a, b):
    return (a.astype(F32) + b.astype(F32)).astype(BF)


def gather_ring(packed):
    parts = [packed] * (N_TP + 1)
    from_below = from_above = packed
    for step in range(1, N_TP // 2):
        from_below = go_up(from_below)
        from_above = go_down(from_above)
        parts[N_TP - step] = from_below
        parts[step] = from_above
    parts[N_TP // 2] = go_up(from_below[:HALF_BLOCKS])
    parts[N_TP] = go_down(from_above[HALF_BLOCKS:])
    return parts


def scatter_ring(targets):
    half = N_TP // 2
    up = go_up(targets[half][:HALF_BLOCKS])
    down = go_down(targets[half][HALF_BLOCKS:])
    for step in range(1, half):
        above, below = targets[half - step], targets[half + step]
        if step == 1:
            above = jnp.concatenate([add_up(above[:HALF_BLOCKS], up), above[HALF_BLOCKS:]])
            below = jnp.concatenate([below[:HALF_BLOCKS], add_up(below[HALF_BLOCKS:], down)])
        else:
            above, below = add_up(above, up), add_up(below, down)
        up = go_up(above)
        down = go_down(below)
    return up, down


def per_device(
    hidden, norm_gain, w_query, w_keyval, w_out, kv_cache, lengths, parents, accepted, slot_of
):
    held = hidden.shape[0]
    rows = hidden.reshape(held * TREE, WIDTH)
    me = lax.axis_index("tp").astype(jnp.int32).reshape(1)
    parts = gather_ring(pack_rows(rows, me))

    destination = slot_of // held
    peer_index = jnp.arange(held, dtype=jnp.int32)
    matches = (destination[None, :] == peer_index[:, None]).astype(jnp.int32)
    send_order = jnp.sum(matches * peer_index[None, :], axis=1)
    cached = exchange(order_cache(kv_cache, send_order))

    tables = prepare_tables(parents, lengths)
    gain = norm_gain[:, None]
    wq = (jnp.dot(w_query, spread_heads(GROUP), preferred_element_type=F32) * gain).astype(BF)
    wkv = lax.dot_general(
        w_keyval, spread_heads(2), (((0,), (0,)), ((), ())), preferred_element_type=F32
    )
    wkv = (wkv * gain).astype(BF)
    w, wo = arrange_weights(wq, wkv, w_out, me)

    *targets, extra = verify_layer(
        parts, w, wo, kv_cache, tables, lengths, accepted.reshape(-1), destination
    )
    cached, extra = lax.optimization_barrier((cached, extra))
    new_cache = assemble_cache(cached, exchange(extra))
    up, down = scatter_ring(targets)
    out_rows = finish_rows(targets[0], up, down, rows, me)
    return (out_rows.reshape(hidden.shape), new_cache)


def solution(mesh):
    in_specs = (
        P("req", None, "tp"),
        P(),
        P(None, "tp"),
        P("tp", None),
        P("tp", None),
        P("req", "tp", None),
        P("req"),
        P("req", None),
        P("req", None),
        P("req"),
    )
    out_specs = (P("req", None, "tp"), P("req", "tp", None))
    return jax.shard_map(
        per_device, mesh=mesh, in_specs=in_specs, out_specs=out_specs, check_vma=False
    )
```

```python
import math

import jax
import jax.numpy as jnp
from jax import lax
from jax.experimental import pallas as pl
from jax.experimental.pallas import tpu as pltpu
from jax.sharding import PartitionSpec as P

H = 32
KVH = 8
HD = 80
D = 2560
TREE = 24
CACHE = 512
DEPTH = 4
N_TP = 8
GROUP = H // KVH
LANES = 128
REQ_BLOCK = 8
ROWS = REQ_BLOCK * TREE
HALF = ROWS // 2
PACKED = 2 * ROWS + HALF
WIDTH = D // N_TP
NEG = -1e30
EXTRA = 16
HALF_BLOCKS = 2
BF = jnp.bfloat16
F32 = jnp.float32
VMEM_LIMIT = 56 * 1024 * 1024


def lane_index(shape):
    return lax.broadcasted_iota(jnp.int32, shape, len(shape) - 1)


def swap_halves(tile):
    return pltpu.roll(tile, 64, 1)


def pack_kernel(parity, x_ref, o_ref):
    for i in range(HALF_BLOCKS):
        pack_block(parity, x_ref.at[pl.ds(i * ROWS, ROWS)], o_ref.at[pl.ds(i, 1)])


def pack_block(parity, x_ref, o_ref):
    x = x_ref[...].astype(F32)
    t0 = x[:, 0:128]
    t1 = x[:, 128:256]
    t2 = jnp.concatenate([x[:, 256:320], jnp.zeros((ROWS, 64), F32)], axis=1)
    low = lane_index((ROWS, LANES)) < 64
    low_half = lane_index((HALF, LANES)) < 64
    even = jnp.bitwise_and(parity[0], 1) == 0

    @pl.when(even)
    def _():
        o_ref[0, 0:ROWS] = t0.astype(BF)
        o_ref[0, ROWS : 2 * ROWS] = t1.astype(BF)
        o_ref[0, 2 * ROWS : PACKED] = jnp.where(
            low_half, t2[:HALF], swap_halves(t2[HALF:])
        ).astype(BF)

    @pl.when(jnp.logical_not(even))
    def _():
        s0, s1, s2 = swap_halves(t0), swap_halves(t1), swap_halves(t2)
        o_ref[0, 0:ROWS] = jnp.where(low, s0, s1).astype(BF)
        o_ref[0, ROWS : 2 * ROWS] = jnp.where(low, s1, s2).astype(BF)
        o_ref[0, 2 * ROWS : PACKED] = jnp.where(low_half, t0[:HALF], s0[HALF:]).astype(BF)


def pack_rows(rows, parity):
    blocks = rows.shape[0] // ROWS
    return pl.pallas_call(
        pack_kernel,
        out_shape=jax.ShapeDtypeStruct((blocks, PACKED, LANES), BF),
        grid_spec=pltpu.PrefetchScalarGridSpec(
            num_scalar_prefetch=1,
            grid=(blocks // HALF_BLOCKS,),
            in_specs=[pl.BlockSpec((HALF_BLOCKS * ROWS, WIDTH), lambda b, p: (b, 0))],
            out_specs=pl.BlockSpec((HALF_BLOCKS, PACKED, LANES), lambda b, p: (b, 0, 0)),
        ),
        name="pack_rows",
    )(parity, rows)


def finish_kernel(parity, own_ref, up_ref, down_ref, x_ref, o_ref):
    for i in range(HALF_BLOCKS):
        block = pl.ds(i, 1)
        flat = pl.ds(i * ROWS, ROWS)
        finish_block(
            parity,
            own_ref.at[block],
            up_ref.at[block],
            down_ref.at[block],
            x_ref.at[flat],
            o_ref.at[flat],
        )


def finish_block(parity, own_ref, up_ref, down_ref, x_ref, o_ref):
    packed = (
        own_ref[0].astype(F32) + up_ref[0].astype(F32) + down_ref[0].astype(F32)
    )
    m0 = packed[0:ROWS]
    m1 = packed[ROWS : 2 * ROWS]
    packed_tail = packed[2 * ROWS : PACKED]
    tail = jnp.concatenate([packed_tail, swap_halves(packed_tail)], axis=0)
    low = lane_index((ROWS, LANES)) < 64
    even = jnp.bitwise_and(parity[0], 1) == 0

    @pl.when(even)
    def _():
        total = jnp.concatenate([m0, m1, tail], axis=1)[:, :WIDTH]
        o_ref[...] = (x_ref[...].astype(F32) + total).astype(BF)

    @pl.when(jnp.logical_not(even))
    def _():
        s0, s1 = swap_halves(m0), swap_halves(m1)
        total = jnp.concatenate(
            [jnp.where(low, tail, s0), jnp.where(low, s0, s1), s1], axis=1
        )[:, :WIDTH]
        o_ref[...] = (x_ref[...].astype(F32) + total).astype(BF)


def finish_rows(own, up, down, rows, parity):
    blocks = rows.shape[0] // ROWS
    packed = pl.BlockSpec((HALF_BLOCKS, PACKED, LANES), lambda b, p: (b, 0, 0))
    flat = pl.BlockSpec((HALF_BLOCKS * ROWS, WIDTH), lambda b, p: (b, 0))
    return pl.pallas_call(
        finish_kernel,
        out_shape=jax.ShapeDtypeStruct(rows.shape, BF),
        grid_spec=pltpu.PrefetchScalarGridSpec(
            num_scalar_prefetch=1,
            grid=(blocks // HALF_BLOCKS,),
            in_specs=[packed, packed, packed, flat],
            out_specs=flat,
        ),
        name="finish_rows",
    )(parity, own, up, down, rows)


def arrange_kernel(me, wq_ref, wkv_ref, wo_ref, w_ref, o_ref):
    o_ref[...] = jnp.zeros_like(o_ref)
    query = GROUP * LANES
    low = lane_index((GROUP * HD, LANES)) < 64
    for j in range(N_TP // 2):
        base = j * 5 * LANES
        tails = []
        for k, at, tail_at in (
            (2 * j, base, base + 256),
            (2 * j + 1, base + 384, base + 320),
        ):
            device = jnp.bitwise_and(me[0] + k, N_TP - 1)
            odd = jnp.bitwise_and(device, 1)
            main_from = pl.multiple_of(device * WIDTH + 64 * odd, 64)
            tail_from = pl.multiple_of(device * WIDTH + 256 * (1 - odd), 64)
            w_ref[at : at + 256, :query] = wq_ref[pl.ds(main_from, 256), :]
            w_ref[at : at + 256, query:] = wkv_ref[pl.ds(main_from, 256), :]
            w_ref[tail_at : tail_at + 64, :query] = wq_ref[pl.ds(tail_from, 64), :]
            w_ref[tail_at : tail_at + 64, query:] = wkv_ref[pl.ds(tail_from, 64), :]
            tile = device // 2 * 5
            for part in range(2):
                column = pl.multiple_of((tile + 3 * odd + part) * LANES, LANES)
                piece = wo_ref[:, pl.ds(column, LANES)]
                for h in range(GROUP):
                    o_ref[
                        h * LANES : h * LANES + HD,
                        at + part * LANES : at + (part + 1) * LANES,
                    ] = piece[h * HD : (h + 1) * HD]
            column = pl.multiple_of((tile + 2) * LANES, LANES)
            tail = wo_ref[:, pl.ds(column, LANES)].astype(F32)
            wrong = odd == (1 - k % 2)
            tails.append(jnp.where(wrong, swap_halves(tail), tail))
        joined = jnp.where(low, tails[0], tails[1]).astype(BF)
        for h in range(GROUP):
            o_ref[h * LANES : h * LANES + HD, base + 256 : base + 384] = joined[
                h * HD : (h + 1) * HD
            ]


def arrange_weights(wq, wkv, w_out, me):
    return pl.pallas_call(
        arrange_kernel,
        out_shape=(
            jax.ShapeDtypeStruct((D, (GROUP + 2) * LANES), BF),
            jax.ShapeDtypeStruct((GROUP * LANES, D), BF),
        ),
        in_specs=[pl.BlockSpec(memory_space=pltpu.SMEM)]
        + [pl.BlockSpec(memory_space=pltpu.VMEM)] * 3,
        out_specs=(
            pl.BlockSpec(memory_space=pltpu.VMEM),
            pl.BlockSpec(memory_space=pltpu.VMEM),
        ),
        compiler_params=pltpu.CompilerParams(vmem_limit_bytes=VMEM_LIMIT),
        name="arrange_weights",
    )(me, wq, wkv, w_out)


def prep_kernel(parents_ref, cos_ref, sin_ref, step_ref, bias_out, cos_out, sin_out):
    requests = parents_ref.shape[0]
    lane = lane_index((requests, LANES))
    step_cos = step_ref[0:1, :]
    step_sin = step_ref[1:2, :]
    sign = step_ref[2:3, :]
    parents = parents_ref[...]
    marks = jnp.where(lane == 0, 1.0, 0.0)
    cosines, sines = cos_ref[...], sin_ref[...]
    older = (marks, cosines, sines)
    newer = older
    for t in range(TREE):
        if t > 0:
            near = jnp.broadcast_to(parents[:, t : t + 1], (requests, LANES)) == t - 1
            marks, cosines, sines = (jnp.where(near, a, b) for a, b in zip(newer, older))
            marks = jnp.where(lane == t, 1.0, marks)
            if t > 0:
                cosines, sines = (
                    cosines * step_cos - sines * step_sin,
                    sines * step_cos + cosines * step_sin,
                )
            older, newer = newer, (marks, cosines, sines)
        bias_out[:, t, :] = jnp.where(marks > 0.5, 0.0, NEG)
        cos_out[:, t, :] = cosines
        sin_out[:, t, :] = sines * sign


def prepare_tables(parents, lengths):
    requests = parents.shape[0]
    lane = jnp.arange(LANES)
    pair = jnp.where(lane < HD // 2, lane, lane - HD // 2)
    frequency = 10000.0 ** (-2.0 * pair.astype(F32) / HD)
    angles = lengths.astype(F32)[:, None] * frequency[None, :]
    sign = jnp.where(lane < HD // 2, -1.0, jnp.where(lane < HD, 1.0, 0.0))
    steps = jnp.stack([jnp.cos(frequency), jnp.sin(frequency), sign] + [sign] * 5)
    table = jax.ShapeDtypeStruct((requests, TREE, LANES), F32)
    return pl.pallas_call(
        prep_kernel, out_shape=(table, table, table), name="prepare_tables"
    )(parents, jnp.cos(angles), jnp.sin(angles), steps)


def order_kernel(order, cache_ref, out_ref, buffer, load_sems, store_sems):
    loads, stores = [], []
    for d in range(cache_ref.shape[0]):
        loads.append(
            pltpu.make_async_copy(cache_ref.at[order[d]], buffer.at[d], load_sems.at[d])
        )
        loads[-1].start()
    for d, load in enumerate(loads):
        load.wait()
        stores.append(pltpu.make_async_copy(buffer.at[d], out_ref.at[d], store_sems.at[d]))
        stores[-1].start()
    for store in stores:
        store.wait()


def order_cache(kv_cache, send_order):
    held = kv_cache.shape[0]
    return pl.pallas_call(
        order_kernel,
        out_shape=jax.ShapeDtypeStruct(kv_cache.shape, BF),
        grid_spec=pltpu.PrefetchScalarGridSpec(
            num_scalar_prefetch=1,
            grid=(1,),
            in_specs=[pl.BlockSpec(memory_space=pl.ANY)],
            out_specs=pl.BlockSpec(memory_space=pl.ANY),
            scratch_shapes=[
                pltpu.VMEM(kv_cache.shape, BF),
                pltpu.SemaphoreType.DMA((held,)),
                pltpu.SemaphoreType.DMA((held,)),
            ],
        ),
        compiler_params=pltpu.CompilerParams(vmem_limit_bytes=VMEM_LIMIT),
        name="order_cache",
    )(send_order, kv_cache)


def layer_kernel(lengths, accepted, destination, *refs):
    x_refs = refs[: N_TP + 1]
    w_ref, wo_ref, cache_ref, bias_ref, cos_ref, sin_ref = refs[N_TP + 1 : N_TP + 7]
    out_refs = refs[N_TP + 7 : 2 * N_TP + 8]
    extra_out, xs, qkv, ctx, extra, sems = refs[2 * N_TP + 8 :]
    b = pl.program_id(0)

    @pl.when(b == 0)
    def _():
        ctx[...] = jnp.zeros_like(ctx)
        extra[...] = jnp.zeros_like(extra)

    def received(k, first, last):
        piece = x_refs[k][0, first:last]
        if k == N_TP // 2:
            piece = jnp.where(b < HALF_BLOCKS, piece, x_refs[N_TP][0, first:last])
        return piece

    def deliver(k, first, last, values):
        values = values.astype(BF)
        if k != N_TP // 2:
            out_refs[k][0, first:last] = values
            return

        @pl.when(b < HALF_BLOCKS)
        def _():
            out_refs[k][0, first:last] = values

        @pl.when(b >= HALF_BLOCKS)
        def _():
            out_refs[N_TP][0, first:last] = values

    low_half = lane_index((HALF, LANES)) < 64
    squares = jnp.zeros((ROWS, LANES), F32)
    for j in range(N_TP // 2):
        base = j * 5 * LANES
        for device, at in ((2 * j, base), (2 * j + 1, base + 3 * LANES)):
            for part in range(2):
                piece = received(device, part * ROWS, (part + 1) * ROWS)
                xs[:, at + part * LANES : at + (part + 1) * LANES] = piece
                wide = piece.astype(F32)
                squares = squares + wide * wide
        even_tail = received(2 * j, 2 * ROWS, PACKED).astype(F32)
        odd_tail = received(2 * j + 1, 2 * ROWS, PACKED).astype(F32)
        tail = jnp.concatenate(
            [
                jnp.where(low_half, even_tail, swap_halves(odd_tail)),
                jnp.where(low_half, swap_halves(even_tail), odd_tail),
            ],
            axis=0,
        )
        xs[:, base + 2 * LANES : base + 3 * LANES] = tail.astype(BF)
        squares = squares + tail * tail
    scale = lax.rsqrt(jnp.sum(squares, axis=1, keepdims=True) * (1.0 / D) + 1e-05)
    flat = xs[...]
    projected = jnp.dot(flat, w_ref[...], preferred_element_type=F32) * scale
    cosines = cos_ref[...].reshape(ROWS, LANES)
    sines = sin_ref[...].reshape(ROWS, LANES)
    first = lane_index((ROWS, LANES)) < HD // 2

    def rotate(tile):
        other = jnp.where(
            first, pltpu.roll(tile, LANES - HD // 2, 1), pltpu.roll(tile, HD // 2, 1)
        )
        return tile * cosines + other * sines

    for h in range(GROUP + 1):
        head = slice(h * LANES, (h + 1) * LANES)
        qkv[:, head] = rotate(projected[:, head])
    qkv[:, (GROUP + 1) * LANES :] = projected[:, (GROUP + 1) * LANES :]

    factor = math.log2(math.e) / math.sqrt(HD)
    column = lane_index((GROUP * TREE, CACHE))
    extra_row = lax.broadcasted_iota(jnp.int32, (EXTRA, LANES), 0)
    extra_lane = lane_index((EXTRA, LANES))
    pick_row = lax.broadcasted_iota(jnp.int32, (EXTRA, TREE), 0)
    pick_column = lane_index((EXTRA, TREE))
    copies = []
    for i in range(REQ_BLOCK):
        r = b * REQ_BLOCK + i
        length = lengths[r]
        rows = slice(i * TREE, (i + 1) * TREE)
        q = jnp.concatenate(
            [qkv[rows, h * LANES : (h + 1) * LANES] for h in range(GROUP)], axis=0
        ).astype(BF)
        k = qkv[rows, GROUP * LANES : (GROUP + 1) * LANES].astype(BF)
        v = qkv[rows, (GROUP + 1) * LANES :].astype(BF)
        cached = jnp.dot(q[:, :HD], cache_ref[i, 0:HD], preferred_element_type=F32)
        cached = jnp.where(column < length, cached * factor, NEG)
        fresh = lax.dot_general(q, k, (((1,), (1,)), ((), ())), preferred_element_type=F32)
        bias = bias_ref[i][:, :TREE]
        fresh = fresh * factor + jnp.concatenate([bias] * GROUP, axis=0)
        top = jnp.maximum(
            jnp.max(cached, axis=1, keepdims=True), jnp.max(fresh, axis=1, keepdims=True)
        )
        cached = jnp.exp2(cached - top)
        fresh = jnp.exp2(fresh - top)
        total = jnp.sum(cached, axis=1, keepdims=True) + jnp.sum(fresh, axis=1, keepdims=True)
        mixed = lax.dot_general(
            cached.astype(BF),
            cache_ref[i, HD : 2 * HD],
            (((1,), (1,)), ((), ())),
            preferred_element_type=F32,
        ) + jnp.dot(fresh.astype(BF), v[:, :HD], preferred_element_type=F32)
        mixed = mixed / total
        for h in range(GROUP):
            ctx[rows, h * LANES : h * LANES + HD] = mixed[h * TREE : (h + 1) * TREE]

        wanted = jnp.full((EXTRA, TREE), -1, jnp.int32)
        for m in range(DEPTH):
            wanted = jnp.where(pick_row == m, accepted[r * DEPTH + m], wanted)
        pick = jnp.where(pick_column == wanted, 1.0, 0.0).astype(BF)
        new_keys = jnp.dot(pick, k, preferred_element_type=F32)
        new_values = jnp.dot(pick, v, preferred_element_type=F32)
        coarse = (length // 16).astype(F32)
        fine = (length % 16).astype(F32)
        shifted = pltpu.roll(new_values, HD, 1)
        new_keys = jnp.where(extra_lane < HD, new_keys, shifted)
        extra[i, :, 0:LANES] = jnp.where(
            extra_row == 8, coarse, jnp.where(extra_row == 9, fine, new_keys)
        ).astype(BF)
        extra[i, :, LANES : 2 * LANES] = jnp.where(
            extra_lane < 2 * HD - LANES, shifted, 0.0
        ).astype(BF)
        copies.append(
            pltpu.make_async_copy(
                extra.at[i], extra_out.at[destination[r]], sems.at[i]
            )
        )
        copies[-1].start()

    partial = jnp.dot(ctx[...].astype(BF), wo_ref[...], preferred_element_type=F32)
    for j in range(N_TP // 2):
        base = j * 5 * LANES
        for k, at in ((2 * j, base), (2 * j + 1, base + 3 * LANES)):
            for part in range(2):
                tile = partial[:, at + part * LANES : at + (part + 1) * LANES]
                deliver(k, part * ROWS, (part + 1) * ROWS, tile)
        tail = partial[:, base + 2 * LANES : base + 3 * LANES]
        top, bottom = tail[:HALF], tail[HALF:]
        deliver(2 * j, 2 * ROWS, PACKED, jnp.where(low_half, top, swap_halves(bottom)))
        deliver(2 * j + 1, 2 * ROWS, PACKED, jnp.where(low_half, swap_halves(top), bottom))
    for copy in copies:
        copy.wait()


def verify_layer(parts, w, wo, kv_cache, tables, lengths, accepted, destination):
    held = kv_cache.shape[0]
    blocks = held // REQ_BLOCK
    full = lambda b, *_: (0, 0)
    packed = pl.BlockSpec((1, PACKED, LANES), lambda b, *_: (b, 0, 0))
    table = pl.BlockSpec((REQ_BLOCK, TREE, LANES), lambda b, *_: (b, 0, 0))
    in_specs = [packed] * (N_TP + 1)
    in_specs[N_TP // 2] = pl.BlockSpec(
        (1, PACKED, LANES), lambda b, *_: (jnp.minimum(b, HALF_BLOCKS - 1), 0, 0)
    )
    in_specs[N_TP] = pl.BlockSpec(
        (1, PACKED, LANES), lambda b, *_: (jnp.maximum(b - HALF_BLOCKS, 0), 0, 0)
    )
    return pl.pallas_call(
        layer_kernel,
        out_shape=[
            jax.ShapeDtypeStruct(
                (HALF_BLOCKS if k % (N_TP // 2) == 0 and k > 0 else blocks, PACKED, LANES), BF
            )
            for k in range(N_TP + 1)
        ]
        + [jax.ShapeDtypeStruct((held, EXTRA, 2 * LANES), BF)],
        grid_spec=pltpu.PrefetchScalarGridSpec(
            num_scalar_prefetch=3,
            grid=(blocks,),
            in_specs=in_specs
            + [
                pl.BlockSpec(w.shape, full),
                pl.BlockSpec(wo.shape, full),
                pl.BlockSpec((REQ_BLOCK, 2 * HD, CACHE), lambda b, *_: (b, 0, 0)),
                table,
                table,
                table,
            ],
            out_specs=in_specs + [pl.BlockSpec(memory_space=pl.ANY)],
            scratch_shapes=[
                pltpu.VMEM((ROWS, D), BF),
                pltpu.VMEM((ROWS, (GROUP + 2) * LANES), F32),
                pltpu.VMEM((ROWS, GROUP * LANES), F32),
                pltpu.VMEM((REQ_BLOCK, EXTRA, 2 * LANES), BF),
                pltpu.SemaphoreType.DMA((REQ_BLOCK,)),
            ],
        ),
        compiler_params=pltpu.CompilerParams(vmem_limit_bytes=VMEM_LIMIT),
        cost_estimate=pl.CostEstimate(
            flops=30_000_000_000, transcendentals=0, bytes_accessed=10_000_000
        ),
        name="verify_layer",
    )(lengths, accepted, destination, *parts, w, wo, kv_cache, *tables)


def assemble_kernel(cache_ref, extra_ref, o_ref):
    place_row = lax.broadcasted_iota(jnp.int32, (EXTRA, CACHE), 0)
    place_column = lane_index((EXTRA, CACHE))
    for i in range(cache_ref.shape[0]):
        extra = extra_ref[i]
        wide = extra[:, :LANES].astype(F32)
        length = (wide[8:9] * 16.0 + wide[9:10]).astype(jnp.int32)
        length = jnp.concatenate([length] * (CACHE // LANES), axis=1)
        offset = place_column - length
        place = jnp.where(
            jnp.logical_and(offset == place_row, place_row < DEPTH), 1.0, 0.0
        ).astype(BF)
        live = jnp.where(offset[0:1] < 0, 1.0, 0.0).astype(BF)
        new = lax.dot_general(
            extra, place, (((0,), (0,)), ((), ())), preferred_element_type=F32
        ).astype(BF)
        o_ref[i] = cache_ref[i] * live + new[: 2 * HD]


def assemble_cache(cached, extra):
    step = 4
    cache_spec = pl.BlockSpec((step,) + cached.shape[1:], lambda s: (s, 0, 0))
    extra_spec = pl.BlockSpec((step,) + extra.shape[1:], lambda s: (s, 0, 0))
    return pl.pallas_call(
        assemble_kernel,
        out_shape=jax.ShapeDtypeStruct(cached.shape, BF),
        grid=(cached.shape[0] // step,),
        in_specs=[cache_spec, extra_spec],
        out_specs=cache_spec,
        name="assemble_cache",
    )(cached, extra)


def spread_heads(heads):
    source = jnp.arange(heads * HD)[:, None]
    target = jnp.arange(heads * LANES)[None, :]
    return (source // HD * LANES + source % HD == target).astype(BF)


def exchange(values):
    return lax.all_to_all(values, "req", split_axis=0, concat_axis=0, tiled=True)


def go_up(values):
    return lax.ppermute(values, "tp", [(i, (i + 1) % N_TP) for i in range(N_TP)])


def go_down(values):
    return lax.ppermute(values, "tp", [(i, (i - 1) % N_TP) for i in range(N_TP)])


def add_up(a, b):
    return (a.astype(F32) + b.astype(F32)).astype(BF)


def gather_ring(packed, weights, tables):
    parts = [packed] * (N_TP + 1)
    from_below = go_up(packed)
    from_above = go_down(packed)
    for step in range(1, N_TP // 2):
        parts[N_TP - step] = from_below
        parts[step] = from_above
        if step == 2:
            from_below, from_above, weights = lax.optimization_barrier(
                (from_below, from_above, weights)
            )
        if step == 3:
            from_below, from_above, tables = lax.optimization_barrier(
                (from_below, from_above, tables)
            )
            from_below = from_below[:HALF_BLOCKS]
            from_above = from_above[HALF_BLOCKS:]
        from_below = go_up(from_below)
        from_above = go_down(from_above)
    parts[N_TP // 2] = from_below
    parts[N_TP] = from_above
    return parts, weights, tables


def add_blocks(values, more, first):
    picked = values[first : first + HALF_BLOCKS]
    return lax.dynamic_update_slice(values, add_up(picked, more), (first, 0, 0))


def scatter_ring(targets, cached, extra):
    half = N_TP // 2
    up = go_up(targets[half])
    down = go_down(targets[N_TP])
    for step in range(1, half):
        above, below = targets[half - step], targets[half + step]
        if step == 1:
            above = add_blocks(above, up, 0)
            below = add_blocks(below, down, HALF_BLOCKS)
        else:
            above, below = add_up(above, up), add_up(below, down)
        if step == 2:
            above, below, cached, extra = lax.optimization_barrier(
                (above, below, cached, extra)
            )
            extra = exchange(extra)
        if step == 3:
            above, below, extra = lax.optimization_barrier((above, below, extra))
            new_cache = assemble_cache(cached, extra)
        up = go_up(above)
        down = go_down(below)
    up, down, new_cache = lax.optimization_barrier((up, down, new_cache))
    return up, down, new_cache


def per_device(
    hidden, norm_gain, w_query, w_keyval, w_out, kv_cache, lengths, parents, accepted, slot_of
):
    held = hidden.shape[0]
    rows = hidden.reshape(held * TREE, WIDTH)
    me = lax.axis_index("tp").astype(jnp.int32).reshape(1)
    packed = pack_rows(rows, me)

    destination = slot_of // held
    peer_index = jnp.arange(held, dtype=jnp.int32)
    matches = (destination[None, :] == peer_index[:, None]).astype(jnp.int32)
    send_order = jnp.sum(matches * peer_index[None, :], axis=1)
    cached = exchange(order_cache(kv_cache, send_order))

    tables = prepare_tables(parents, lengths)
    gain = norm_gain[:, None]
    wq = (jnp.dot(w_query, spread_heads(GROUP), preferred_element_type=F32) * gain).astype(BF)
    wkv = lax.dot_general(
        w_keyval, spread_heads(2), (((0,), (0,)), ((), ())), preferred_element_type=F32
    )
    wkv = (wkv * gain).astype(BF)
    weights = arrange_weights(wq, wkv, w_out, me)
    parts, weights, (tables, picks) = gather_ring(
        packed, weights, (tables, accepted.reshape(-1))
    )

    *targets, extra = verify_layer(
        parts, *weights, kv_cache, tables, lengths, picks, destination
    )
    up, down, new_cache = scatter_ring(targets, cached, extra)
    out_rows = finish_rows(targets[0], up, down, rows, me)
    return (out_rows.reshape(hidden.shape), new_cache)


def solution(mesh):
    in_specs = (
        P("req", None, "tp"),
        P(),
        P(None, "tp"),
        P("tp", None),
        P("tp", None),
        P("req", "tp", None),
        P("req"),
        P("req", None),
        P("req", None),
        P("req"),
    )
    out_specs = (P("req", None, "tp"), P("req", "tp", None))
    return jax.shard_map(
        per_device, mesh=mesh, in_specs=in_specs, out_specs=out_specs, check_vma=False
    )
```

```python
import math

import jax
import jax.numpy as jnp
from jax import lax
from jax.experimental import pallas as pl
from jax.experimental.pallas import tpu as pltpu
from jax.sharding import PartitionSpec as P

H = 32
KVH = 8
HD = 80
D = 2560
TREE = 24
CACHE = 512
DEPTH = 4
N_TP = 8
GROUP = H // KVH
LANES = 128
REQ_BLOCK = 8
ROWS = REQ_BLOCK * TREE
HALF = ROWS // 2
PACKED = 2 * ROWS + HALF
WIDTH = D // N_TP
NEG = -1e30
EXTRA = 8
HALF_BLOCKS = 2
BF = jnp.bfloat16
F32 = jnp.float32
VMEM_LIMIT = 56 * 1024 * 1024


def lane_index(shape):
    return lax.broadcasted_iota(jnp.int32, shape, len(shape) - 1)


def swap_halves(tile):
    return pltpu.roll(tile, 64, 1)


def pack_kernel(parity, x_ref, o_ref):
    for i in range(HALF_BLOCKS):
        pack_block(parity, x_ref.at[pl.ds(i * ROWS, ROWS)], o_ref.at[pl.ds(i, 1)])


def pack_block(parity, x_ref, o_ref):
    x = x_ref[...].astype(F32)
    t0 = x[:, 0:128]
    t1 = x[:, 128:256]
    t2 = jnp.concatenate([x[:, 256:320], jnp.zeros((ROWS, 64), F32)], axis=1)
    low = lane_index((ROWS, LANES)) < 64
    low_half = lane_index((HALF, LANES)) < 64
    even = jnp.bitwise_and(parity[0], 1) == 0

    @pl.when(even)
    def _():
        o_ref[0, 0:ROWS] = t0.astype(BF)
        o_ref[0, ROWS : 2 * ROWS] = t1.astype(BF)
        o_ref[0, 2 * ROWS : PACKED] = jnp.where(
            low_half, t2[:HALF], swap_halves(t2[HALF:])
        ).astype(BF)

    @pl.when(jnp.logical_not(even))
    def _():
        s0, s1, s2 = swap_halves(t0), swap_halves(t1), swap_halves(t2)
        o_ref[0, 0:ROWS] = jnp.where(low, s0, s1).astype(BF)
        o_ref[0, ROWS : 2 * ROWS] = jnp.where(low, s1, s2).astype(BF)
        o_ref[0, 2 * ROWS : PACKED] = jnp.where(low_half, t0[:HALF], s0[HALF:]).astype(BF)


def pack_rows(rows, parity):
    blocks = rows.shape[0] // ROWS
    return pl.pallas_call(
        pack_kernel,
        out_shape=jax.ShapeDtypeStruct((blocks, PACKED, LANES), BF),
        grid_spec=pltpu.PrefetchScalarGridSpec(
            num_scalar_prefetch=1,
            grid=(blocks // HALF_BLOCKS,),
            in_specs=[pl.BlockSpec((HALF_BLOCKS * ROWS, WIDTH), lambda b, p: (b, 0))],
            out_specs=pl.BlockSpec((HALF_BLOCKS, PACKED, LANES), lambda b, p: (b, 0, 0)),
        ),
        name="pack_rows",
    )(parity, rows)


def finish_kernel(parity, own_ref, up_ref, down_ref, x_ref, o_ref):
    for i in range(HALF_BLOCKS):
        block = pl.ds(i, 1)
        flat = pl.ds(i * ROWS, ROWS)
        finish_block(
            parity,
            own_ref.at[block],
            up_ref.at[block],
            down_ref.at[block],
            x_ref.at[flat],
            o_ref.at[flat],
        )


def finish_block(parity, own_ref, up_ref, down_ref, x_ref, o_ref):
    packed = (
        own_ref[0].astype(F32) + up_ref[0].astype(F32) + down_ref[0].astype(F32)
    )
    m0 = packed[0:ROWS]
    m1 = packed[ROWS : 2 * ROWS]
    packed_tail = packed[2 * ROWS : PACKED]
    tail = jnp.concatenate([packed_tail, swap_halves(packed_tail)], axis=0)
    low = lane_index((ROWS, LANES)) < 64
    even = jnp.bitwise_and(parity[0], 1) == 0

    @pl.when(even)
    def _():
        total = jnp.concatenate([m0, m1, tail], axis=1)[:, :WIDTH]
        o_ref[...] = (x_ref[...].astype(F32) + total).astype(BF)

    @pl.when(jnp.logical_not(even))
    def _():
        s0, s1 = swap_halves(m0), swap_halves(m1)
        total = jnp.concatenate(
            [jnp.where(low, tail, s0), jnp.where(low, s0, s1), s1], axis=1
        )[:, :WIDTH]
        o_ref[...] = (x_ref[...].astype(F32) + total).astype(BF)


def finish_rows(own, up, down, rows, parity):
    blocks = rows.shape[0] // ROWS
    packed = pl.BlockSpec((HALF_BLOCKS, PACKED, LANES), lambda b, p: (b, 0, 0))
    flat = pl.BlockSpec((HALF_BLOCKS * ROWS, WIDTH), lambda b, p: (b, 0))
    return pl.pallas_call(
        finish_kernel,
        out_shape=jax.ShapeDtypeStruct(rows.shape, BF),
        grid_spec=pltpu.PrefetchScalarGridSpec(
            num_scalar_prefetch=1,
            grid=(blocks // HALF_BLOCKS,),
            in_specs=[packed, packed, packed, flat],
            out_specs=flat,
        ),
        name="finish_rows",
    )(parity, own, up, down, rows)


def arrange_kernel(me, wq_ref, wkv_ref, wo_ref, w_ref, o_ref):
    o_ref[...] = jnp.zeros_like(o_ref)
    query = GROUP * LANES
    low = lane_index((GROUP * HD, LANES)) < 64
    for j in range(N_TP // 2):
        base = j * 5 * LANES
        tails = []
        for k, at, tail_at in (
            (2 * j, base, base + 256),
            (2 * j + 1, base + 384, base + 320),
        ):
            device = jnp.bitwise_and(me[0] + k, N_TP - 1)
            odd = jnp.bitwise_and(device, 1)
            main_from = pl.multiple_of(device * WIDTH + 64 * odd, 64)
            tail_from = pl.multiple_of(device * WIDTH + 256 * (1 - odd), 64)
            w_ref[at : at + 256, :query] = wq_ref[pl.ds(main_from, 256), :]
            w_ref[at : at + 256, query:] = wkv_ref[pl.ds(main_from, 256), :]
            w_ref[tail_at : tail_at + 64, :query] = wq_ref[pl.ds(tail_from, 64), :]
            w_ref[tail_at : tail_at + 64, query:] = wkv_ref[pl.ds(tail_from, 64), :]
            tile = device // 2 * 5
            for part in range(2):
                column = pl.multiple_of((tile + 3 * odd + part) * LANES, LANES)
                piece = wo_ref[:, pl.ds(column, LANES)]
                for h in range(GROUP):
                    o_ref[
                        h * LANES : h * LANES + HD,
                        at + part * LANES : at + (part + 1) * LANES,
                    ] = piece[h * HD : (h + 1) * HD]
            column = pl.multiple_of((tile + 2) * LANES, LANES)
            tail = wo_ref[:, pl.ds(column, LANES)].astype(F32)
            wrong = odd == (1 - k % 2)
            tails.append(jnp.where(wrong, swap_halves(tail), tail))
        joined = jnp.where(low, tails[0], tails[1]).astype(BF)
        for h in range(GROUP):
            o_ref[h * LANES : h * LANES + HD, base + 256 : base + 384] = joined[
                h * HD : (h + 1) * HD
            ]


def arrange_weights(wq, wkv, w_out, me):
    return pl.pallas_call(
        arrange_kernel,
        out_shape=(
            jax.ShapeDtypeStruct((D, (GROUP + 2) * LANES), BF),
            jax.ShapeDtypeStruct((GROUP * LANES, D), BF),
        ),
        in_specs=[pl.BlockSpec(memory_space=pltpu.SMEM)]
        + [pl.BlockSpec(memory_space=pltpu.VMEM)] * 3,
        out_specs=(
            pl.BlockSpec(memory_space=pltpu.VMEM),
            pl.BlockSpec(memory_space=pltpu.VMEM),
        ),
        compiler_params=pltpu.CompilerParams(vmem_limit_bytes=VMEM_LIMIT),
        name="arrange_weights",
    )(me, wq, wkv, w_out)


def prep_kernel(parents_ref, cos_ref, sin_ref, step_ref, bias_out, cos_out, sin_out):
    requests = parents_ref.shape[0]
    lane = lane_index((requests, LANES))
    step_cos = step_ref[0:1, :]
    step_sin = step_ref[1:2, :]
    sign = step_ref[2:3, :]
    parents = parents_ref[...]
    marks = jnp.where(lane == 0, 1.0, 0.0)
    cosines, sines = cos_ref[...], sin_ref[...]
    older = (marks, cosines, sines)
    newer = older
    for t in range(TREE):
        if t > 0:
            near = jnp.broadcast_to(parents[:, t : t + 1], (requests, LANES)) == t - 1
            marks, cosines, sines = (jnp.where(near, a, b) for a, b in zip(newer, older))
            marks = jnp.where(lane == t, 1.0, marks)
            if t > 0:
                cosines, sines = (
                    cosines * step_cos - sines * step_sin,
                    sines * step_cos + cosines * step_sin,
                )
            older, newer = newer, (marks, cosines, sines)
        bias_out[:, t, :] = jnp.where(marks > 0.5, 0.0, NEG)
        cos_out[:, t, :] = cosines
        sin_out[:, t, :] = sines * sign


def prepare_tables(parents, lengths):
    requests = parents.shape[0]
    lane = jnp.arange(LANES)
    pair = jnp.where(lane < HD // 2, lane, lane - HD // 2)
    frequency = 10000.0 ** (-2.0 * pair.astype(F32) / HD)
    angles = lengths.astype(F32)[:, None] * frequency[None, :]
    sign = jnp.where(lane < HD // 2, -1.0, jnp.where(lane < HD, 1.0, 0.0))
    steps = jnp.stack([jnp.cos(frequency), jnp.sin(frequency), sign] + [sign] * 5)
    table = jax.ShapeDtypeStruct((requests, TREE, LANES), F32)
    return pl.pallas_call(
        prep_kernel, out_shape=(table, table, table), name="prepare_tables"
    )(parents, jnp.cos(angles), jnp.sin(angles), steps)


def order_kernel(order, cache_ref, out_ref, buffer, load_sems, store_sems):
    loads, stores = [], []
    for d in range(cache_ref.shape[0]):
        loads.append(
            pltpu.make_async_copy(cache_ref.at[order[d]], buffer.at[d], load_sems.at[d])
        )
        loads[-1].start()
    for d, load in enumerate(loads):
        load.wait()
        stores.append(pltpu.make_async_copy(buffer.at[d], out_ref.at[d], store_sems.at[d]))
        stores[-1].start()
    for store in stores:
        store.wait()


def order_cache(kv_cache, send_order):
    held = kv_cache.shape[0]
    return pl.pallas_call(
        order_kernel,
        out_shape=jax.ShapeDtypeStruct(kv_cache.shape, BF),
        grid_spec=pltpu.PrefetchScalarGridSpec(
            num_scalar_prefetch=1,
            grid=(1,),
            in_specs=[pl.BlockSpec(memory_space=pl.ANY)],
            out_specs=pl.BlockSpec(memory_space=pl.ANY),
            scratch_shapes=[
                pltpu.VMEM(kv_cache.shape, BF),
                pltpu.SemaphoreType.DMA((held,)),
                pltpu.SemaphoreType.DMA((held,)),
            ],
        ),
        compiler_params=pltpu.CompilerParams(vmem_limit_bytes=VMEM_LIMIT),
        name="order_cache",
    )(send_order, kv_cache)


def layer_kernel(lengths, accepted, destination, *refs):
    x_refs = refs[: N_TP + 1]
    w_ref, wo_ref, cache_ref, bias_ref, cos_ref, sin_ref = refs[N_TP + 1 : N_TP + 7]
    out_refs = refs[N_TP + 7 : 2 * N_TP + 8]
    extra_out, xs, qkv, ctx, extra, sems = refs[2 * N_TP + 8 :]
    b = pl.program_id(0)

    @pl.when(b == 0)
    def _():
        ctx[...] = jnp.zeros_like(ctx)

    def received(k, first, last):
        piece = x_refs[k][0, first:last]
        if k == N_TP // 2:
            piece = jnp.where(b < HALF_BLOCKS, piece, x_refs[N_TP][0, first:last])
        return piece

    def deliver(k, first, last, values):
        values = values.astype(BF)
        if k != N_TP // 2:
            out_refs[k][0, first:last] = values
            return

        @pl.when(b < HALF_BLOCKS)
        def _():
            out_refs[k][0, first:last] = values

        @pl.when(b >= HALF_BLOCKS)
        def _():
            out_refs[N_TP][0, first:last] = values

    low_half = lane_index((HALF, LANES)) < 64
    squares = jnp.zeros((ROWS, LANES), F32)
    for j in range(N_TP // 2):
        base = j * 5 * LANES
        for device, at in ((2 * j, base), (2 * j + 1, base + 3 * LANES)):
            for part in range(2):
                piece = received(device, part * ROWS, (part + 1) * ROWS)
                xs[:, at + part * LANES : at + (part + 1) * LANES] = piece
                wide = piece.astype(F32)
                squares = squares + wide * wide
        even_tail = received(2 * j, 2 * ROWS, PACKED).astype(F32)
        odd_tail = received(2 * j + 1, 2 * ROWS, PACKED).astype(F32)
        tail = jnp.concatenate(
            [
                jnp.where(low_half, even_tail, swap_halves(odd_tail)),
                jnp.where(low_half, swap_halves(even_tail), odd_tail),
            ],
            axis=0,
        )
        xs[:, base + 2 * LANES : base + 3 * LANES] = tail.astype(BF)
        squares = squares + tail * tail
    scale = lax.rsqrt(jnp.sum(squares, axis=1, keepdims=True) * (1.0 / D) + 1e-05)
    flat = xs[...]
    projected = jnp.dot(flat, w_ref[...], preferred_element_type=F32) * scale
    cosines = cos_ref[...].reshape(ROWS, LANES)
    sines = sin_ref[...].reshape(ROWS, LANES)
    first = lane_index((ROWS, LANES)) < HD // 2

    def rotate(tile):
        other = jnp.where(
            first, pltpu.roll(tile, LANES - HD // 2, 1), pltpu.roll(tile, HD // 2, 1)
        )
        return tile * cosines + other * sines

    for h in range(GROUP + 1):
        head = slice(h * LANES, (h + 1) * LANES)
        qkv[:, head] = rotate(projected[:, head])
    qkv[:, (GROUP + 1) * LANES :] = projected[:, (GROUP + 1) * LANES :]

    factor = math.log2(math.e) / math.sqrt(HD)
    column = lane_index((GROUP * TREE, CACHE))
    extra_row = lax.broadcasted_iota(jnp.int32, (EXTRA, LANES), 0)
    extra_lane = lane_index((EXTRA, LANES))
    pick_row = lax.broadcasted_iota(jnp.int32, (EXTRA, TREE), 0)
    pick_column = lane_index((EXTRA, TREE))
    copies = []
    for i in range(REQ_BLOCK):
        r = b * REQ_BLOCK + i
        length = lengths[r]
        rows = slice(i * TREE, (i + 1) * TREE)
        q = jnp.concatenate(
            [qkv[rows, h * LANES : (h + 1) * LANES] for h in range(GROUP)], axis=0
        ).astype(BF)
        fresh_rows = qkv[rows, GROUP * LANES :].astype(BF)
        k = fresh_rows[:, :LANES]
        v = fresh_rows[:, LANES:]
        cached = jnp.dot(q[:, :HD], cache_ref[i, 0:HD], preferred_element_type=F32)
        cached = jnp.where(column < length, cached * factor, NEG)
        fresh = lax.dot_general(q, k, (((1,), (1,)), ((), ())), preferred_element_type=F32)
        bias = bias_ref[i][:, :TREE]
        fresh = fresh * factor + jnp.concatenate([bias] * GROUP, axis=0)
        top = jnp.maximum(
            jnp.max(cached, axis=1, keepdims=True), jnp.max(fresh, axis=1, keepdims=True)
        )
        cached = jnp.exp2(cached - top)
        fresh = jnp.exp2(fresh - top)
        total = jnp.sum(cached, axis=1, keepdims=True) + jnp.sum(fresh, axis=1, keepdims=True)
        mixed = lax.dot_general(
            cached.astype(BF),
            cache_ref[i, HD : 2 * HD],
            (((1,), (1,)), ((), ())),
            preferred_element_type=F32,
        ) + jnp.dot(fresh.astype(BF), v[:, :HD], preferred_element_type=F32)
        mixed = mixed / total
        for h in range(GROUP):
            ctx[rows, h * LANES : h * LANES + HD] = mixed[h * TREE : (h + 1) * TREE]

        wanted = jnp.full((EXTRA, TREE), -1, jnp.int32)
        for m in range(DEPTH):
            here = jnp.bitwise_and(pick_row, DEPTH - 1) == m
            wanted = jnp.where(here, accepted[r * DEPTH + m], wanted)
        pick = jnp.where(pick_column == wanted, 1.0, 0.0).astype(BF)
        new = jnp.dot(pick, fresh_rows, preferred_element_type=F32)
        shifted = pltpu.roll(new[:, LANES:], HD, 1)
        tile = jnp.where(
            extra_row < DEPTH,
            jnp.where(extra_lane < HD, new[:, :LANES], shifted),
            jnp.where(extra_lane < 2 * HD - LANES, shifted, 0.0),
        )
        coarse = (length // 16).astype(F32)
        fine = (length % 16).astype(F32)
        marker = jnp.where(extra_row == DEPTH, coarse, fine)
        marked = jnp.logical_and(
            extra_lane >= 64,
            jnp.logical_or(extra_row == DEPTH, extra_row == DEPTH + 1),
        )
        extra[i] = jnp.where(marked, marker, tile).astype(BF)
        copies.append(
            pltpu.make_async_copy(
                extra.at[i], extra_out.at[destination[r]], sems.at[i]
            )
        )
        copies[-1].start()

    partial = jnp.dot(ctx[...].astype(BF), wo_ref[...], preferred_element_type=F32)
    for j in range(N_TP // 2):
        base = j * 5 * LANES
        for k, at in ((2 * j, base), (2 * j + 1, base + 3 * LANES)):
            for part in range(2):
                tile = partial[:, at + part * LANES : at + (part + 1) * LANES]
                deliver(k, part * ROWS, (part + 1) * ROWS, tile)
        tail = partial[:, base + 2 * LANES : base + 3 * LANES]
        top, bottom = tail[:HALF], tail[HALF:]
        deliver(2 * j, 2 * ROWS, PACKED, jnp.where(low_half, top, swap_halves(bottom)))
        deliver(2 * j + 1, 2 * ROWS, PACKED, jnp.where(low_half, swap_halves(top), bottom))
    for copy in copies:
        copy.wait()


def verify_layer(parts, w, wo, kv_cache, tables, lengths, accepted, destination):
    held = kv_cache.shape[0]
    blocks = held // REQ_BLOCK
    full = lambda b, *_: (0, 0)
    packed = pl.BlockSpec((1, PACKED, LANES), lambda b, *_: (b, 0, 0))
    table = pl.BlockSpec((REQ_BLOCK, TREE, LANES), lambda b, *_: (b, 0, 0))
    in_specs = [packed] * (N_TP + 1)
    in_specs[N_TP // 2] = pl.BlockSpec(
        (1, PACKED, LANES), lambda b, *_: (jnp.minimum(b, HALF_BLOCKS - 1), 0, 0)
    )
    in_specs[N_TP] = pl.BlockSpec(
        (1, PACKED, LANES), lambda b, *_: (jnp.maximum(b - HALF_BLOCKS, 0), 0, 0)
    )
    return pl.pallas_call(
        layer_kernel,
        out_shape=[
            jax.ShapeDtypeStruct(
                (HALF_BLOCKS if k % (N_TP // 2) == 0 and k > 0 else blocks, PACKED, LANES), BF
            )
            for k in range(N_TP + 1)
        ]
        + [jax.ShapeDtypeStruct((held, EXTRA, LANES), BF)],
        grid_spec=pltpu.PrefetchScalarGridSpec(
            num_scalar_prefetch=3,
            grid=(blocks,),
            in_specs=in_specs
            + [
                pl.BlockSpec(w.shape, full),
                pl.BlockSpec(wo.shape, full),
                pl.BlockSpec((REQ_BLOCK, 2 * HD, CACHE), lambda b, *_: (b, 0, 0)),
                table,
                table,
                table,
            ],
            out_specs=in_specs + [pl.BlockSpec(memory_space=pl.ANY)],
            scratch_shapes=[
                pltpu.VMEM((ROWS, D), BF),
                pltpu.VMEM((ROWS, (GROUP + 2) * LANES), F32),
                pltpu.VMEM((ROWS, GROUP * LANES), F32),
                pltpu.VMEM((REQ_BLOCK, EXTRA, LANES), BF),
                pltpu.SemaphoreType.DMA((REQ_BLOCK,)),
            ],
        ),
        compiler_params=pltpu.CompilerParams(vmem_limit_bytes=VMEM_LIMIT),
        cost_estimate=pl.CostEstimate(
            flops=1_000_000_000, transcendentals=0, bytes_accessed=10_000_000
        ),
        name="verify_layer",
    )(lengths, accepted, destination, *parts, w, wo, kv_cache, *tables)


def assemble_kernel(me, cache_ref, extra_ref, o_ref):
    place_row = lax.broadcasted_iota(jnp.int32, (EXTRA, CACHE), 0)
    place_column = lane_index((EXTRA, CACHE))
    upper = lane_index((1, LANES)) >= 64
    for i in range(cache_ref.shape[0]):
        extra = extra_ref[i, 0]
        wide = extra.astype(F32)
        length = wide[DEPTH : DEPTH + 1] * 16.0 + wide[DEPTH + 1 : DEPTH + 2]
        length = jnp.where(upper, length, swap_halves(length)).astype(jnp.int32)
        length = jnp.concatenate([length] * (CACHE // LANES), axis=1)
        offset = place_column - length
        first = jnp.logical_and(offset == place_row, place_row < DEPTH)
        second = jnp.logical_and(offset == place_row - DEPTH, place_row >= DEPTH)
        live = jnp.where(offset[0:1] < 0, 1.0, 0.0).astype(BF)
        contract = (((0,), (0,)), ((), ()))
        new = lax.dot_general(
            extra, jnp.where(first, 1.0, 0.0).astype(BF), contract, preferred_element_type=F32
        )
        rest = lax.dot_general(
            extra, jnp.where(second, 1.0, 0.0).astype(BF), contract, preferred_element_type=F32
        )[: 2 * HD - LANES]
        o_ref[i, :LANES] = cache_ref[i, :LANES] * live + new.astype(BF)
        o_ref[i, LANES:] = cache_ref[i, LANES:] * live + rest.astype(BF)


def assemble_cache(cached, extra, me):
    step = 4
    cache_spec = pl.BlockSpec((step,) + cached.shape[1:], lambda s, me: (s, 0, 0))
    extra_spec = pl.BlockSpec((step, 1, EXTRA, LANES), lambda s, me: (s, me[0], 0, 0))
    return pl.pallas_call(
        assemble_kernel,
        out_shape=jax.ShapeDtypeStruct(cached.shape, BF),
        grid_spec=pltpu.PrefetchScalarGridSpec(
            num_scalar_prefetch=1,
            grid=(cached.shape[0] // step,),
            in_specs=[cache_spec, extra_spec],
            out_specs=cache_spec,
        ),
        name="assemble_cache",
    )(me, cached, extra)


def spread_heads(heads):
    source = jnp.arange(heads * HD)[:, None]
    target = jnp.arange(heads * LANES)[None, :]
    return (source // HD * LANES + source % HD == target).astype(BF)


def exchange(values):
    return lax.all_to_all(values, "req", split_axis=0, concat_axis=0, tiled=True)


def go_up(values):
    return lax.ppermute(values, "tp", [(i, (i + 1) % N_TP) for i in range(N_TP)])


def go_down(values):
    return lax.ppermute(values, "tp", [(i, (i - 1) % N_TP) for i in range(N_TP)])


def add_up(a, b):
    return (a.astype(F32) + b.astype(F32)).astype(BF)


def add_blocks(values, more, first):
    picked = values[first : first + HALF_BLOCKS]
    return lax.dynamic_update_slice(values, add_up(picked, more), (first, 0, 0))


def scatter_ring(targets, cached, extra):
    half = N_TP // 2
    up = go_up(targets[half])
    down = go_down(targets[N_TP])
    extra = lax.all_gather(extra, "req", axis=0, tiled=False)
    for step in range(1, half):
        above, below = targets[half - step], targets[half + step]
        if step == 1:
            above = add_blocks(above, up, 0)
            below = add_blocks(below, down, HALF_BLOCKS)
        else:
            above, below = add_up(above, up), add_up(below, down)
        if step == 3:
            above, below, cached, extra = lax.optimization_barrier(
                (above, below, cached, extra)
            )
            me = lax.axis_index("req").astype(jnp.int32).reshape(1)
            new_cache = assemble_cache(cached, extra, me)
        up = go_up(above)
        down = go_down(below)
    up, down, new_cache = lax.optimization_barrier((up, down, new_cache))
    return up, down, new_cache


def per_device(
    hidden, norm_gain, w_query, w_keyval, w_out, kv_cache, lengths, parents, accepted, slot_of
):
    held = hidden.shape[0]
    rows = hidden.reshape(held * TREE, WIDTH)
    me = lax.axis_index("tp").astype(jnp.int32).reshape(1)
    barrier = lax.optimization_barrier

    parts = [pack_rows(rows, me)] * (N_TP + 1)
    destination = slot_of // held
    peer_index = jnp.arange(held, dtype=jnp.int32)
    matches = (destination[None, :] == peer_index[:, None]).astype(jnp.int32)
    send_order = jnp.sum(matches * peer_index[None, :], axis=1)
    ordered = order_cache(kv_cache, send_order)
    below, above = go_up(parts[0]), go_down(parts[0])

    below, above, w_keyval, ordered = barrier((below, above, w_keyval, ordered))
    parts[7], parts[1] = below, above
    gain = norm_gain[:, None]
    wkv = lax.dot_general(
        w_keyval, spread_heads(2), (((0,), (0,)), ((), ())), preferred_element_type=F32
    )
    wkv = (wkv * gain).astype(BF)
    ordered, wkv = barrier((ordered, wkv))
    cached = exchange(ordered)
    below, above = go_up(below), go_down(above)

    below, above, w_query, wkv = barrier((below, above, w_query, wkv))
    parts[6], parts[2] = below, above
    wq = (jnp.dot(w_query, spread_heads(GROUP), preferred_element_type=F32) * gain).astype(BF)
    weights = arrange_weights(wq, wkv, w_out, me)
    below, above = go_up(below), go_down(above)

    below, above, weights, parents = barrier((below, above, weights, parents))
    parts[5], parts[3] = below, above
    tables = prepare_tables(parents, lengths)
    parts[4] = go_up(below[:HALF_BLOCKS])
    parts[8] = go_down(above[HALF_BLOCKS:])
    picks = accepted.reshape(-1)

    *targets, extra = verify_layer(
        parts, *weights, kv_cache, tables, lengths, picks, destination
    )
    up, down, new_cache = scatter_ring(targets, cached, extra)
    out_rows = finish_rows(targets[0], up, down, rows, me)
    return (out_rows.reshape(hidden.shape), new_cache)


def solution(mesh):
    in_specs = (
        P("req", None, "tp"),
        P(),
        P(None, "tp"),
        P("tp", None),
        P("tp", None),
        P("req", "tp", None),
        P("req"),
        P("req", None),
        P("req", None),
        P("req"),
    )
    out_specs = (P("req", None, "tp"), P("req", "tp", None))
    return jax.shard_map(
        per_device, mesh=mesh, in_specs=in_specs, out_specs=out_specs, check_vma=False
    )
```

```python
import math

import jax
import jax.numpy as jnp
from jax import lax
from jax.experimental import pallas as pl
from jax.experimental.pallas import tpu as pltpu
from jax.sharding import PartitionSpec as P

H = 32
KVH = 8
HD = 80
D = 2560
TREE = 24
CACHE = 512
DEPTH = 4
N_TP = 8
GROUP = H // KVH
LANES = 128
REQ_BLOCK = 8
ROWS = REQ_BLOCK * TREE
HALF = ROWS // 2
PACKED = 2 * ROWS + HALF
WIDTH = D // N_TP
NEG = -1e30
EXTRA = 8
HALF_BLOCKS = 2
BF = jnp.bfloat16
F32 = jnp.float32
VMEM_LIMIT = 56 * 1024 * 1024


def lane_index(shape):
    return lax.broadcasted_iota(jnp.int32, shape, len(shape) - 1)


def swap_halves(tile):
    return pltpu.roll(tile, 64, 1)


def pack_kernel(parity, x_ref, o_ref):
    for i in range(HALF_BLOCKS):
        pack_block(parity, x_ref.at[pl.ds(i * ROWS, ROWS)], o_ref.at[pl.ds(i, 1)])


def pack_block(parity, x_ref, o_ref):
    x = x_ref[...].astype(F32)
    t0 = x[:, 0:128]
    t1 = x[:, 128:256]
    t2 = jnp.concatenate([x[:, 256:320], jnp.zeros((ROWS, 64), F32)], axis=1)
    low = lane_index((ROWS, LANES)) < 64
    low_half = lane_index((HALF, LANES)) < 64
    even = jnp.bitwise_and(parity[0], 1) == 0

    @pl.when(even)
    def _():
        o_ref[0, 0:ROWS] = t0.astype(BF)
        o_ref[0, ROWS : 2 * ROWS] = t1.astype(BF)
        o_ref[0, 2 * ROWS : PACKED] = jnp.where(
            low_half, t2[:HALF], swap_halves(t2[HALF:])
        ).astype(BF)

    @pl.when(jnp.logical_not(even))
    def _():
        s0, s1, s2 = swap_halves(t0), swap_halves(t1), swap_halves(t2)
        o_ref[0, 0:ROWS] = jnp.where(low, s0, s1).astype(BF)
        o_ref[0, ROWS : 2 * ROWS] = jnp.where(low, s1, s2).astype(BF)
        o_ref[0, 2 * ROWS : PACKED] = jnp.where(low_half, t0[:HALF], s0[HALF:]).astype(BF)


def pack_rows(rows, parity):
    blocks = rows.shape[0] // ROWS
    return pl.pallas_call(
        pack_kernel,
        out_shape=jax.ShapeDtypeStruct((blocks, PACKED, LANES), BF),
        grid_spec=pltpu.PrefetchScalarGridSpec(
            num_scalar_prefetch=1,
            grid=(blocks // HALF_BLOCKS,),
            in_specs=[pl.BlockSpec((HALF_BLOCKS * ROWS, WIDTH), lambda b, p: (b, 0))],
            out_specs=pl.BlockSpec((HALF_BLOCKS, PACKED, LANES), lambda b, p: (b, 0, 0)),
        ),
        name="pack_rows",
    )(parity, rows)


def finish_kernel(parity, own_ref, up_ref, down_ref, x_ref, o_ref):
    for i in range(HALF_BLOCKS):
        block = pl.ds(i, 1)
        flat = pl.ds(i * ROWS, ROWS)
        finish_block(
            parity,
            own_ref.at[block],
            up_ref.at[block],
            down_ref.at[block],
            x_ref.at[flat],
            o_ref.at[flat],
        )


def finish_block(parity, own_ref, up_ref, down_ref, x_ref, o_ref):
    packed = (
        own_ref[0].astype(F32) + up_ref[0].astype(F32) + down_ref[0].astype(F32)
    )
    m0 = packed[0:ROWS]
    m1 = packed[ROWS : 2 * ROWS]
    packed_tail = packed[2 * ROWS : PACKED]
    tail = jnp.concatenate([packed_tail, swap_halves(packed_tail)], axis=0)
    low = lane_index((ROWS, LANES)) < 64
    even = jnp.bitwise_and(parity[0], 1) == 0

    @pl.when(even)
    def _():
        total = jnp.concatenate([m0, m1, tail], axis=1)[:, :WIDTH]
        o_ref[...] = (x_ref[...].astype(F32) + total).astype(BF)

    @pl.when(jnp.logical_not(even))
    def _():
        s0, s1 = swap_halves(m0), swap_halves(m1)
        total = jnp.concatenate(
            [jnp.where(low, tail, s0), jnp.where(low, s0, s1), s1], axis=1
        )[:, :WIDTH]
        o_ref[...] = (x_ref[...].astype(F32) + total).astype(BF)


def finish_rows(own, up, down, rows, parity):
    blocks = rows.shape[0] // ROWS
    packed = pl.BlockSpec((HALF_BLOCKS, PACKED, LANES), lambda b, p: (b, 0, 0))
    flat = pl.BlockSpec((HALF_BLOCKS * ROWS, WIDTH), lambda b, p: (b, 0))
    return pl.pallas_call(
        finish_kernel,
        out_shape=jax.ShapeDtypeStruct(rows.shape, BF),
        grid_spec=pltpu.PrefetchScalarGridSpec(
            num_scalar_prefetch=1,
            grid=(blocks // HALF_BLOCKS,),
            in_specs=[packed, packed, packed, flat],
            out_specs=flat,
        ),
        name="finish_rows",
    )(parity, own, up, down, rows)


def arrange_kernel(me, wq_ref, wkv_ref, wo_ref, w_ref, o_ref):
    o_ref[...] = jnp.zeros_like(o_ref)
    query = GROUP * LANES
    low = lane_index((GROUP * HD, LANES)) < 64
    for j in range(N_TP // 2):
        base = j * 5 * LANES
        tails = []
        for k, at, tail_at in (
            (2 * j, base, base + 256),
            (2 * j + 1, base + 384, base + 320),
        ):
            device = jnp.bitwise_and(me[0] + k, N_TP - 1)
            odd = jnp.bitwise_and(device, 1)
            main_from = pl.multiple_of(device * WIDTH + 64 * odd, 64)
            tail_from = pl.multiple_of(device * WIDTH + 256 * (1 - odd), 64)
            w_ref[at : at + 256, :query] = wq_ref[pl.ds(main_from, 256), :]
            w_ref[at : at + 256, query:] = wkv_ref[pl.ds(main_from, 256), :]
            w_ref[tail_at : tail_at + 64, :query] = wq_ref[pl.ds(tail_from, 64), :]
            w_ref[tail_at : tail_at + 64, query:] = wkv_ref[pl.ds(tail_from, 64), :]
            tile = device // 2 * 5
            for part in range(2):
                column = pl.multiple_of((tile + 3 * odd + part) * LANES, LANES)
                piece = wo_ref[:, pl.ds(column, LANES)]
                for h in range(GROUP):
                    o_ref[
                        h * LANES : h * LANES + HD,
                        at + part * LANES : at + (part + 1) * LANES,
                    ] = piece[h * HD : (h + 1) * HD]
            column = pl.multiple_of((tile + 2) * LANES, LANES)
            tail = wo_ref[:, pl.ds(column, LANES)].astype(F32)
            wrong = odd == (1 - k % 2)
            tails.append(jnp.where(wrong, swap_halves(tail), tail))
        joined = jnp.where(low, tails[0], tails[1]).astype(BF)
        for h in range(GROUP):
            o_ref[h * LANES : h * LANES + HD, base + 256 : base + 384] = joined[
                h * HD : (h + 1) * HD
            ]


def arrange_weights(wq, wkv, w_out, me):
    return pl.pallas_call(
        arrange_kernel,
        out_shape=(
            jax.ShapeDtypeStruct((D, (GROUP + 2) * LANES), BF),
            jax.ShapeDtypeStruct((GROUP * LANES, D), BF),
        ),
        in_specs=[pl.BlockSpec(memory_space=pltpu.SMEM)]
        + [pl.BlockSpec(memory_space=pltpu.VMEM)] * 3,
        out_specs=(
            pl.BlockSpec(memory_space=pltpu.VMEM),
            pl.BlockSpec(memory_space=pltpu.VMEM),
        ),
        compiler_params=pltpu.CompilerParams(vmem_limit_bytes=VMEM_LIMIT),
        name="arrange_weights",
    )(me, wq, wkv, w_out)


def prep_kernel(parents_ref, cos_ref, sin_ref, step_ref, bias_out, cos_out, sin_out):
    requests = parents_ref.shape[0]
    lane = lane_index((requests, LANES))
    step_cos = step_ref[0:1, :]
    step_sin = step_ref[1:2, :]
    sign = step_ref[2:3, :]
    parents = parents_ref[...]
    marks = jnp.where(lane == 0, 1.0, 0.0)
    cosines, sines = cos_ref[...], sin_ref[...]
    older = (marks, cosines, sines)
    newer = older
    for t in range(TREE):
        if t > 0:
            near = jnp.broadcast_to(parents[:, t : t + 1], (requests, LANES)) == t - 1
            marks, cosines, sines = (jnp.where(near, a, b) for a, b in zip(newer, older))
            marks = jnp.where(lane == t, 1.0, marks)
            if t > 0:
                cosines, sines = (
                    cosines * step_cos - sines * step_sin,
                    sines * step_cos + cosines * step_sin,
                )
            older, newer = newer, (marks, cosines, sines)
        bias_out[:, t, :] = jnp.where(marks > 0.5, 0.0, NEG)
        cos_out[:, t, :] = cosines
        sin_out[:, t, :] = sines * sign


def prepare_tables(parents, lengths):
    requests = parents.shape[0]
    lane = jnp.arange(LANES)
    pair = jnp.where(lane < HD // 2, lane, lane - HD // 2)
    frequency = 10000.0 ** (-2.0 * pair.astype(F32) / HD)
    angles = lengths.astype(F32)[:, None] * frequency[None, :]
    sign = jnp.where(lane < HD // 2, -1.0, jnp.where(lane < HD, 1.0, 0.0))
    steps = jnp.stack([jnp.cos(frequency), jnp.sin(frequency), sign] + [sign] * 5)
    table = jax.ShapeDtypeStruct((requests, TREE, LANES), F32)
    return pl.pallas_call(
        prep_kernel, out_shape=(table, table, table), name="prepare_tables"
    )(parents, jnp.cos(angles), jnp.sin(angles), steps)


def order_kernel(order, cache_ref, out_ref, buffer, load_sems, store_sems):
    loads, stores = [], []
    for d in range(cache_ref.shape[0]):
        loads.append(
            pltpu.make_async_copy(cache_ref.at[order[d]], buffer.at[d], load_sems.at[d])
        )
        loads[-1].start()
    for d, load in enumerate(loads):
        load.wait()
        stores.append(pltpu.make_async_copy(buffer.at[d], out_ref.at[d], store_sems.at[d]))
        stores[-1].start()
    for store in stores:
        store.wait()


def order_cache(kv_cache, send_order):
    held = kv_cache.shape[0]
    return pl.pallas_call(
        order_kernel,
        out_shape=jax.ShapeDtypeStruct(kv_cache.shape, BF),
        grid_spec=pltpu.PrefetchScalarGridSpec(
            num_scalar_prefetch=1,
            grid=(1,),
            in_specs=[pl.BlockSpec(memory_space=pl.ANY)],
            out_specs=pl.BlockSpec(memory_space=pl.ANY),
            scratch_shapes=[
                pltpu.VMEM(kv_cache.shape, BF),
                pltpu.SemaphoreType.DMA((held,)),
                pltpu.SemaphoreType.DMA((held,)),
            ],
        ),
        compiler_params=pltpu.CompilerParams(vmem_limit_bytes=VMEM_LIMIT),
        name="order_cache",
    )(send_order, kv_cache)


def project_kernel(lengths, accepted, destination, *refs):
    x_refs = refs[: N_TP + 1]
    w_ref, cos_ref, sin_ref, qkv, extra_out, xs, extra, sems = refs[N_TP + 1 :]
    b = pl.program_id(0)

    def received(k, first, last):
        piece = x_refs[k][0, first:last]
        if k == N_TP // 2:
            piece = jnp.where(b < HALF_BLOCKS, piece, x_refs[N_TP][0, first:last])
        return piece

    low_half = lane_index((HALF, LANES)) < 64
    squares = jnp.zeros((ROWS, LANES), F32)
    for j in range(N_TP // 2):
        base = j * 5 * LANES
        for device, at in ((2 * j, base), (2 * j + 1, base + 3 * LANES)):
            for part in range(2):
                piece = received(device, part * ROWS, (part + 1) * ROWS)
                xs[:, at + part * LANES : at + (part + 1) * LANES] = piece
                wide = piece.astype(F32)
                squares = squares + wide * wide
        even_tail = received(2 * j, 2 * ROWS, PACKED).astype(F32)
        odd_tail = received(2 * j + 1, 2 * ROWS, PACKED).astype(F32)
        tail = jnp.concatenate(
            [
                jnp.where(low_half, even_tail, swap_halves(odd_tail)),
                jnp.where(low_half, swap_halves(even_tail), odd_tail),
            ],
            axis=0,
        )
        xs[:, base + 2 * LANES : base + 3 * LANES] = tail.astype(BF)
        squares = squares + tail * tail
    scale = lax.rsqrt(jnp.sum(squares, axis=1, keepdims=True) * (1.0 / D) + 1e-05)
    flat = xs[...]
    projected = jnp.dot(flat, w_ref[...], preferred_element_type=F32) * scale
    cosines = cos_ref[...].reshape(ROWS, LANES)
    sines = sin_ref[...].reshape(ROWS, LANES)
    first = lane_index((ROWS, LANES)) < HD // 2

    def rotate(tile):
        other = jnp.where(
            first, pltpu.roll(tile, LANES - HD // 2, 1), pltpu.roll(tile, HD // 2, 1)
        )
        return tile * cosines + other * sines

    for h in range(GROUP + 1):
        head = slice(h * LANES, (h + 1) * LANES)
        qkv[:, head] = rotate(projected[:, head])
    qkv[:, (GROUP + 1) * LANES :] = projected[:, (GROUP + 1) * LANES :]

    extra_row = lax.broadcasted_iota(jnp.int32, (EXTRA, LANES), 0)
    extra_lane = lane_index((EXTRA, LANES))
    pick_row = lax.broadcasted_iota(jnp.int32, (EXTRA, TREE), 0)
    pick_column = lane_index((EXTRA, TREE))
    copies = []
    for i in range(REQ_BLOCK):
        r = b * REQ_BLOCK + i
        length = lengths[r]
        fresh_rows = qkv[i * TREE : (i + 1) * TREE, GROUP * LANES :].astype(BF)
        wanted = jnp.full((EXTRA, TREE), -1, jnp.int32)
        for m in range(DEPTH):
            here = jnp.bitwise_and(pick_row, DEPTH - 1) == m
            wanted = jnp.where(here, accepted[r * DEPTH + m], wanted)
        pick = jnp.where(pick_column == wanted, 1.0, 0.0).astype(BF)
        new = jnp.dot(pick, fresh_rows, preferred_element_type=F32)
        shifted = pltpu.roll(new[:, LANES:], HD, 1)
        tile = jnp.where(
            extra_row < DEPTH,
            jnp.where(extra_lane < HD, new[:, :LANES], shifted),
            jnp.where(extra_lane < 2 * HD - LANES, shifted, 0.0),
        )
        coarse = (length // 16).astype(F32)
        fine = (length % 16).astype(F32)
        marker = jnp.where(extra_row == DEPTH, coarse, fine)
        marked = jnp.logical_and(
            extra_lane >= 64,
            jnp.logical_or(extra_row == DEPTH, extra_row == DEPTH + 1),
        )
        extra[i] = jnp.where(marked, marker, tile).astype(BF)
        copies.append(
            pltpu.make_async_copy(
                extra.at[i], extra_out.at[destination[r]], sems.at[i]
            )
        )
        copies[-1].start()
    for copy in copies:
        copy.wait()


def attend_kernel(lengths, qkv, wo_ref, cache_ref, bias_ref, *refs):
    out_refs = refs[: N_TP + 1]
    ctx = refs[N_TP + 1]
    b = pl.program_id(0)

    @pl.when(b == 0)
    def _():
        ctx[...] = jnp.zeros_like(ctx)

    def deliver(k, first, last, values):
        values = values.astype(BF)
        if k != N_TP // 2:
            out_refs[k][0, first:last] = values
            return

        @pl.when(b < HALF_BLOCKS)
        def _():
            out_refs[k][0, first:last] = values

        @pl.when(b >= HALF_BLOCKS)
        def _():
            out_refs[N_TP][0, first:last] = values

    low_half = lane_index((HALF, LANES)) < 64
    factor = math.log2(math.e) / math.sqrt(HD)
    column = lane_index((GROUP * TREE, CACHE))
    for i in range(REQ_BLOCK):
        r = b * REQ_BLOCK + i
        length = lengths[r]
        rows = slice(i * TREE, (i + 1) * TREE)
        q = jnp.concatenate(
            [qkv[rows, h * LANES : (h + 1) * LANES] for h in range(GROUP)], axis=0
        ).astype(BF)
        fresh_rows = qkv[rows, GROUP * LANES :].astype(BF)
        k = fresh_rows[:, :LANES]
        v = fresh_rows[:, LANES:]
        cached = jnp.dot(q[:, :HD], cache_ref[i, 0:HD], preferred_element_type=F32)
        cached = jnp.where(column < length, cached * factor, NEG)
        fresh = lax.dot_general(q, k, (((1,), (1,)), ((), ())), preferred_element_type=F32)
        bias = bias_ref[i][:, :TREE]
        fresh = fresh * factor + jnp.concatenate([bias] * GROUP, axis=0)
        top = jnp.maximum(
            jnp.max(cached, axis=1, keepdims=True), jnp.max(fresh, axis=1, keepdims=True)
        )
        cached = jnp.exp2(cached - top)
        fresh = jnp.exp2(fresh - top)
        total = jnp.sum(cached, axis=1, keepdims=True) + jnp.sum(fresh, axis=1, keepdims=True)
        mixed = lax.dot_general(
            cached.astype(BF),
            cache_ref[i, HD : 2 * HD],
            (((1,), (1,)), ((), ())),
            preferred_element_type=F32,
        ) + jnp.dot(fresh.astype(BF), v[:, :HD], preferred_element_type=F32)
        mixed = mixed / total
        for h in range(GROUP):
            ctx[rows, h * LANES : h * LANES + HD] = mixed[h * TREE : (h + 1) * TREE]

    partial = jnp.dot(ctx[...].astype(BF), wo_ref[...], preferred_element_type=F32)
    for j in range(N_TP // 2):
        base = j * 5 * LANES
        for k, at in ((2 * j, base), (2 * j + 1, base + 3 * LANES)):
            for part in range(2):
                tile = partial[:, at + part * LANES : at + (part + 1) * LANES]
                deliver(k, part * ROWS, (part + 1) * ROWS, tile)
        tail = partial[:, base + 2 * LANES : base + 3 * LANES]
        top, bottom = tail[:HALF], tail[HALF:]
        deliver(2 * j, 2 * ROWS, PACKED, jnp.where(low_half, top, swap_halves(bottom)))
        deliver(2 * j + 1, 2 * ROWS, PACKED, jnp.where(low_half, swap_halves(top), bottom))


def project_rows(parts, w, cosines, sines, lengths, accepted, destination):
    held = lengths.shape[0]
    blocks = held // REQ_BLOCK
    packed = pl.BlockSpec((1, PACKED, LANES), lambda b, *_: (b, 0, 0))
    table = pl.BlockSpec((REQ_BLOCK, TREE, LANES), lambda b, *_: (b, 0, 0))
    x_specs = [packed] * (N_TP + 1)
    x_specs[N_TP // 2] = pl.BlockSpec(
        (1, PACKED, LANES), lambda b, *_: (jnp.minimum(b, HALF_BLOCKS - 1), 0, 0)
    )
    x_specs[N_TP] = pl.BlockSpec(
        (1, PACKED, LANES), lambda b, *_: (jnp.maximum(b - HALF_BLOCKS, 0), 0, 0)
    )
    width = w.shape[1]
    return pl.pallas_call(
        project_kernel,
        out_shape=(
            jax.ShapeDtypeStruct((held * TREE, width), F32),
            jax.ShapeDtypeStruct((held, EXTRA, LANES), BF),
        ),
        grid_spec=pltpu.PrefetchScalarGridSpec(
            num_scalar_prefetch=3,
            grid=(blocks,),
            in_specs=x_specs + [pl.BlockSpec(w.shape, lambda b, *_: (0, 0)), table, table],
            out_specs=(
                pl.BlockSpec((ROWS, width), lambda b, *_: (b, 0)),
                pl.BlockSpec(memory_space=pl.ANY),
            ),
            scratch_shapes=[
                pltpu.VMEM((ROWS, D), BF),
                pltpu.VMEM((REQ_BLOCK, EXTRA, LANES), BF),
                pltpu.SemaphoreType.DMA((REQ_BLOCK,)),
            ],
        ),
        compiler_params=pltpu.CompilerParams(vmem_limit_bytes=VMEM_LIMIT),
        cost_estimate=pl.CostEstimate(
            flops=1_000_000_000, transcendentals=0, bytes_accessed=10_000_000
        ),
        name="project_rows",
    )(lengths, accepted, destination, *parts, w, cosines, sines)


def attend_cache(qkv, wo, kv_cache, bias, lengths):
    held = kv_cache.shape[0]
    blocks = held // REQ_BLOCK
    packed = pl.BlockSpec((1, PACKED, LANES), lambda b, *_: (b, 0, 0))
    out_specs = [packed] * (N_TP + 1)
    out_specs[N_TP // 2] = pl.BlockSpec(
        (1, PACKED, LANES), lambda b, *_: (jnp.minimum(b, HALF_BLOCKS - 1), 0, 0)
    )
    out_specs[N_TP] = pl.BlockSpec(
        (1, PACKED, LANES), lambda b, *_: (jnp.maximum(b - HALF_BLOCKS, 0), 0, 0)
    )
    out_blocks = [blocks] * (N_TP + 1)
    out_blocks[N_TP // 2] = out_blocks[N_TP] = HALF_BLOCKS
    return pl.pallas_call(
        attend_kernel,
        out_shape=[jax.ShapeDtypeStruct((n, PACKED, LANES), BF) for n in out_blocks],
        grid_spec=pltpu.PrefetchScalarGridSpec(
            num_scalar_prefetch=1,
            grid=(blocks,),
            in_specs=[
                pl.BlockSpec((ROWS, qkv.shape[1]), lambda b, *_: (b, 0)),
                pl.BlockSpec(wo.shape, lambda b, *_: (0, 0)),
                pl.BlockSpec((REQ_BLOCK, 2 * HD, CACHE), lambda b, *_: (b, 0, 0)),
                pl.BlockSpec((REQ_BLOCK, TREE, LANES), lambda b, *_: (b, 0, 0)),
            ],
            out_specs=out_specs,
            scratch_shapes=[pltpu.VMEM((ROWS, GROUP * LANES), F32)],
        ),
        compiler_params=pltpu.CompilerParams(vmem_limit_bytes=VMEM_LIMIT),
        cost_estimate=pl.CostEstimate(
            flops=1_000_000_000, transcendentals=0, bytes_accessed=10_000_000
        ),
        name="attend_cache",
    )(lengths, qkv, wo, kv_cache, bias)


def assemble_kernel(me, cache_ref, extra_ref, o_ref):
    place_row = lax.broadcasted_iota(jnp.int32, (EXTRA, CACHE), 0)
    place_column = lane_index((EXTRA, CACHE))
    upper = lane_index((1, LANES)) >= 64
    for i in range(cache_ref.shape[0]):
        extra = extra_ref[i, 0]
        wide = extra.astype(F32)
        length = wide[DEPTH : DEPTH + 1] * 16.0 + wide[DEPTH + 1 : DEPTH + 2]
        length = jnp.where(upper, length, swap_halves(length)).astype(jnp.int32)
        length = jnp.concatenate([length] * (CACHE // LANES), axis=1)
        offset = place_column - length
        first = jnp.logical_and(offset == place_row, place_row < DEPTH)
        second = jnp.logical_and(offset == place_row - DEPTH, place_row >= DEPTH)
        live = jnp.where(offset[0:1] < 0, 1.0, 0.0).astype(BF)
        contract = (((0,), (0,)), ((), ()))
        new = lax.dot_general(
            extra, jnp.where(first, 1.0, 0.0).astype(BF), contract, preferred_element_type=F32
        )
        rest = lax.dot_general(
            extra, jnp.where(second, 1.0, 0.0).astype(BF), contract, preferred_element_type=F32
        )[: 2 * HD - LANES]
        o_ref[i, :LANES] = cache_ref[i, :LANES] * live + new.astype(BF)
        o_ref[i, LANES:] = cache_ref[i, LANES:] * live + rest.astype(BF)


def assemble_cache(cached, extra, me):
    step = 4
    cache_spec = pl.BlockSpec((step,) + cached.shape[1:], lambda s, me: (s, 0, 0))
    extra_spec = pl.BlockSpec((step, 1, EXTRA, LANES), lambda s, me: (s, me[0], 0, 0))
    return pl.pallas_call(
        assemble_kernel,
        out_shape=jax.ShapeDtypeStruct(cached.shape, BF),
        grid_spec=pltpu.PrefetchScalarGridSpec(
            num_scalar_prefetch=1,
            grid=(cached.shape[0] // step,),
            in_specs=[cache_spec, extra_spec],
            out_specs=cache_spec,
        ),
        name="assemble_cache",
    )(me, cached, extra)


def spread_heads(heads):
    source = jnp.arange(heads * HD)[:, None]
    target = jnp.arange(heads * LANES)[None, :]
    return (source // HD * LANES + source % HD == target).astype(BF)


def exchange(values):
    return lax.all_to_all(values, "req", split_axis=0, concat_axis=0, tiled=True)


def go_up(values):
    return lax.ppermute(values, "tp", [(i, (i + 1) % N_TP) for i in range(N_TP)])


def go_down(values):
    return lax.ppermute(values, "tp", [(i, (i - 1) % N_TP) for i in range(N_TP)])


def add_up(a, b):
    return (a.astype(F32) + b.astype(F32)).astype(BF)


def add_blocks(values, more, first):
    picked = values[first : first + HALF_BLOCKS]
    return lax.dynamic_update_slice(values, add_up(picked, more), (first, 0, 0))


def scatter_ring(targets, cached, extra):
    half = N_TP // 2
    up = go_up(targets[half])
    down = go_down(targets[N_TP])
    for step in range(1, half):
        above, below = targets[half - step], targets[half + step]
        if step == 1:
            above = add_blocks(above, up, 0)
            below = add_blocks(below, down, HALF_BLOCKS)
        else:
            above, below = add_up(above, up), add_up(below, down)
        if step == 3:
            above, below, cached, extra = lax.optimization_barrier(
                (above, below, cached, extra)
            )
            me = lax.axis_index("req").astype(jnp.int32).reshape(1)
            new_cache = assemble_cache(cached, extra, me)
        up = go_up(above)
        down = go_down(below)
    up, down, new_cache = lax.optimization_barrier((up, down, new_cache))
    return up, down, new_cache


def per_device(
    hidden, norm_gain, w_query, w_keyval, w_out, kv_cache, lengths, parents, accepted, slot_of
):
    held = hidden.shape[0]
    rows = hidden.reshape(held * TREE, WIDTH)
    me = lax.axis_index("tp").astype(jnp.int32).reshape(1)
    barrier = lax.optimization_barrier

    parts = [pack_rows(rows, me)] * (N_TP + 1)
    destination = slot_of // held
    peer_index = jnp.arange(held, dtype=jnp.int32)
    matches = (destination[None, :] == peer_index[:, None]).astype(jnp.int32)
    send_order = jnp.sum(matches * peer_index[None, :], axis=1)
    ordered = order_cache(kv_cache, send_order)
    below, above = go_up(parts[0]), go_down(parts[0])

    below, above, w_keyval, ordered = barrier((below, above, w_keyval, ordered))
    parts[7], parts[1] = below, above
    gain = norm_gain[:, None]
    wkv = lax.dot_general(
        w_keyval, spread_heads(2), (((0,), (0,)), ((), ())), preferred_element_type=F32
    )
    wkv = (wkv * gain).astype(BF)
    ordered, wkv = barrier((ordered, wkv))
    cached = exchange(ordered)
    below, above = go_up(below), go_down(above)

    below, above, w_query, wkv = barrier((below, above, w_query, wkv))
    parts[6], parts[2] = below, above
    wq = (jnp.dot(w_query, spread_heads(GROUP), preferred_element_type=F32) * gain).astype(BF)
    weights = arrange_weights(wq, wkv, w_out, me)
    below, above = go_up(below), go_down(above)

    below, above, weights, parents = barrier((below, above, weights, parents))
    parts[5], parts[3] = below, above
    tables = prepare_tables(parents, lengths)
    parts[4] = go_up(below[:HALF_BLOCKS])
    parts[8] = go_down(above[HALF_BLOCKS:])
    picks = accepted.reshape(-1)

    bias, cosines, sines = tables
    w, wo = weights
    qkv, extra = project_rows(parts, w, cosines, sines, lengths, picks, destination)
    extra = lax.all_gather(extra, "req", axis=0, tiled=False)
    targets = attend_cache(qkv, wo, kv_cache, bias, lengths)
    up, down, new_cache = scatter_ring(targets, cached, extra)
    out_rows = finish_rows(targets[0], up, down, rows, me)
    return (out_rows.reshape(hidden.shape), new_cache)


def solution(mesh):
    in_specs = (
        P("req", None, "tp"),
        P(),
        P(None, "tp"),
        P("tp", None),
        P("tp", None),
        P("req", "tp", None),
        P("req"),
        P("req", None),
        P("req", None),
        P("req"),
    )
    out_specs = (P("req", None, "tp"), P("req", "tp", None))
    return jax.shard_map(
        per_device, mesh=mesh, in_specs=in_specs, out_specs=out_specs, check_vma=False
    )
```

```python
import math

import jax
import jax.numpy as jnp
from jax import lax
from jax.experimental import pallas as pl
from jax.experimental.pallas import tpu as pltpu
from jax.sharding import PartitionSpec as P

H = 32
KVH = 8
HD = 80
D = 2560
TREE = 24
CACHE = 512
DEPTH = 4
N_TP = 8
GROUP = H // KVH
LANES = 128
REQ_BLOCK = 8
ROWS = REQ_BLOCK * TREE
HALF = ROWS // 2
PACKED = 2 * ROWS + HALF
WIDTH = D // N_TP
NEG = -1e30
EXTRA = 8
HALF_BLOCKS = 2
BF = jnp.bfloat16
F32 = jnp.float32
VMEM_LIMIT = 56 * 1024 * 1024


def lane_index(shape):
    return lax.broadcasted_iota(jnp.int32, shape, len(shape) - 1)


def swap_halves(tile):
    return pltpu.roll(tile, 64, 1)


def pack_kernel(parity, x_ref, o_ref):
    for i in range(HALF_BLOCKS):
        pack_block(parity, x_ref.at[pl.ds(i * ROWS, ROWS)], o_ref.at[pl.ds(i, 1)])


def pack_block(parity, x_ref, o_ref):
    x = x_ref[...].astype(F32)
    t0 = x[:, 0:128]
    t1 = x[:, 128:256]
    t2 = jnp.concatenate([x[:, 256:320], jnp.zeros((ROWS, 64), F32)], axis=1)
    low = lane_index((ROWS, LANES)) < 64
    low_half = lane_index((HALF, LANES)) < 64
    even = jnp.bitwise_and(parity[0], 1) == 0

    @pl.when(even)
    def _():
        o_ref[0, 0:ROWS] = t0.astype(BF)
        o_ref[0, ROWS : 2 * ROWS] = t1.astype(BF)
        o_ref[0, 2 * ROWS : PACKED] = jnp.where(
            low_half, t2[:HALF], swap_halves(t2[HALF:])
        ).astype(BF)

    @pl.when(jnp.logical_not(even))
    def _():
        s0, s1, s2 = swap_halves(t0), swap_halves(t1), swap_halves(t2)
        o_ref[0, 0:ROWS] = jnp.where(low, s0, s1).astype(BF)
        o_ref[0, ROWS : 2 * ROWS] = jnp.where(low, s1, s2).astype(BF)
        o_ref[0, 2 * ROWS : PACKED] = jnp.where(low_half, t0[:HALF], s0[HALF:]).astype(BF)


def pack_rows(rows, parity):
    blocks = rows.shape[0] // ROWS
    return pl.pallas_call(
        pack_kernel,
        out_shape=jax.ShapeDtypeStruct((blocks, PACKED, LANES), BF),
        grid_spec=pltpu.PrefetchScalarGridSpec(
            num_scalar_prefetch=1,
            grid=(blocks // HALF_BLOCKS,),
            in_specs=[pl.BlockSpec((HALF_BLOCKS * ROWS, WIDTH), lambda b, p: (b, 0))],
            out_specs=pl.BlockSpec((HALF_BLOCKS, PACKED, LANES), lambda b, p: (b, 0, 0)),
        ),
        name="pack_rows",
    )(parity, rows)


def finish_kernel(parity, own_ref, up_ref, down_ref, x_ref, o_ref):
    for i in range(HALF_BLOCKS):
        block = pl.ds(i, 1)
        flat = pl.ds(i * ROWS, ROWS)
        finish_block(
            parity,
            own_ref.at[block],
            up_ref.at[block],
            down_ref.at[block],
            x_ref.at[flat],
            o_ref.at[flat],
        )


def finish_block(parity, own_ref, up_ref, down_ref, x_ref, o_ref):
    packed = (
        own_ref[0].astype(F32) + up_ref[0].astype(F32) + down_ref[0].astype(F32)
    )
    m0 = packed[0:ROWS]
    m1 = packed[ROWS : 2 * ROWS]
    packed_tail = packed[2 * ROWS : PACKED]
    tail = jnp.concatenate([packed_tail, swap_halves(packed_tail)], axis=0)
    low = lane_index((ROWS, LANES)) < 64
    even = jnp.bitwise_and(parity[0], 1) == 0

    @pl.when(even)
    def _():
        total = jnp.concatenate([m0, m1, tail], axis=1)[:, :WIDTH]
        o_ref[...] = (x_ref[...].astype(F32) + total).astype(BF)

    @pl.when(jnp.logical_not(even))
    def _():
        s0, s1 = swap_halves(m0), swap_halves(m1)
        total = jnp.concatenate(
            [jnp.where(low, tail, s0), jnp.where(low, s0, s1), s1], axis=1
        )[:, :WIDTH]
        o_ref[...] = (x_ref[...].astype(F32) + total).astype(BF)


def finish_rows(own, up, down, rows, parity):
    blocks = rows.shape[0] // ROWS
    packed = pl.BlockSpec((HALF_BLOCKS, PACKED, LANES), lambda b, p: (b, 0, 0))
    flat = pl.BlockSpec((HALF_BLOCKS * ROWS, WIDTH), lambda b, p: (b, 0))
    return pl.pallas_call(
        finish_kernel,
        out_shape=jax.ShapeDtypeStruct(rows.shape, BF),
        grid_spec=pltpu.PrefetchScalarGridSpec(
            num_scalar_prefetch=1,
            grid=(blocks // HALF_BLOCKS,),
            in_specs=[packed, packed, packed, flat],
            out_specs=flat,
        ),
        name="finish_rows",
    )(parity, own, up, down, rows)


def arrange_kernel(me, wq_ref, wkv_ref, wo_ref, w_ref, o_ref):
    o_ref[...] = jnp.zeros_like(o_ref)
    query = GROUP * LANES
    low = lane_index((GROUP * HD, LANES)) < 64
    for j in range(N_TP // 2):
        base = j * 5 * LANES
        tails = []
        for k, at, tail_at in (
            (2 * j, base, base + 256),
            (2 * j + 1, base + 384, base + 320),
        ):
            device = jnp.bitwise_and(me[0] + k, N_TP - 1)
            odd = jnp.bitwise_and(device, 1)
            main_from = pl.multiple_of(device * WIDTH + 64 * odd, 64)
            tail_from = pl.multiple_of(device * WIDTH + 256 * (1 - odd), 64)
            w_ref[at : at + 256, :query] = wq_ref[pl.ds(main_from, 256), :]
            w_ref[at : at + 256, query:] = wkv_ref[pl.ds(main_from, 256), :]
            w_ref[tail_at : tail_at + 64, :query] = wq_ref[pl.ds(tail_from, 64), :]
            w_ref[tail_at : tail_at + 64, query:] = wkv_ref[pl.ds(tail_from, 64), :]
            tile = device // 2 * 5
            for part in range(2):
                column = pl.multiple_of((tile + 3 * odd + part) * LANES, LANES)
                piece = wo_ref[:, pl.ds(column, LANES)]
                for h in range(GROUP):
                    o_ref[
                        h * LANES : h * LANES + HD,
                        at + part * LANES : at + (part + 1) * LANES,
                    ] = piece[h * HD : (h + 1) * HD]
            column = pl.multiple_of((tile + 2) * LANES, LANES)
            tail = wo_ref[:, pl.ds(column, LANES)].astype(F32)
            wrong = odd == (1 - k % 2)
            tails.append(jnp.where(wrong, swap_halves(tail), tail))
        joined = jnp.where(low, tails[0], tails[1]).astype(BF)
        for h in range(GROUP):
            o_ref[h * LANES : h * LANES + HD, base + 256 : base + 384] = joined[
                h * HD : (h + 1) * HD
            ]


def arrange_weights(wq, wkv, w_out, me):
    return pl.pallas_call(
        arrange_kernel,
        out_shape=(
            jax.ShapeDtypeStruct((D, (GROUP + 2) * LANES), BF),
            jax.ShapeDtypeStruct((GROUP * LANES, D), BF),
        ),
        in_specs=[pl.BlockSpec(memory_space=pltpu.SMEM)]
        + [pl.BlockSpec(memory_space=pltpu.VMEM)] * 3,
        out_specs=(
            pl.BlockSpec(memory_space=pltpu.VMEM),
            pl.BlockSpec(memory_space=pltpu.VMEM),
        ),
        compiler_params=pltpu.CompilerParams(vmem_limit_bytes=VMEM_LIMIT),
        name="arrange_weights",
    )(me, wq, wkv, w_out)


def prep_kernel(parents_ref, cos_ref, sin_ref, step_ref, bias_out, cos_out, sin_out):
    requests = parents_ref.shape[0]
    lane = lane_index((requests, LANES))
    step_cos = step_ref[0:1, :]
    step_sin = step_ref[1:2, :]
    sign = step_ref[2:3, :]
    parents = parents_ref[...]
    marks = jnp.where(lane == 0, 1.0, 0.0)
    cosines, sines = cos_ref[...], sin_ref[...]
    older = (marks, cosines, sines)
    newer = older
    for t in range(TREE):
        if t > 0:
            near = jnp.broadcast_to(parents[:, t : t + 1], (requests, LANES)) == t - 1
            marks, cosines, sines = (jnp.where(near, a, b) for a, b in zip(newer, older))
            marks = jnp.where(lane == t, 1.0, marks)
            if t > 0:
                cosines, sines = (
                    cosines * step_cos - sines * step_sin,
                    sines * step_cos + cosines * step_sin,
                )
            older, newer = newer, (marks, cosines, sines)
        bias_out[:, t, :] = jnp.where(marks > 0.5, 0.0, NEG)
        cos_out[:, t, :] = cosines
        sin_out[:, t, :] = sines * sign


def prepare_tables(parents, lengths):
    requests = parents.shape[0]
    lane = jnp.arange(LANES)
    pair = jnp.where(lane < HD // 2, lane, lane - HD // 2)
    frequency = 10000.0 ** (-2.0 * pair.astype(F32) / HD)
    angles = lengths.astype(F32)[:, None] * frequency[None, :]
    sign = jnp.where(lane < HD // 2, -1.0, jnp.where(lane < HD, 1.0, 0.0))
    steps = jnp.stack([jnp.cos(frequency), jnp.sin(frequency), sign] + [sign] * 5)
    table = jax.ShapeDtypeStruct((requests, TREE, LANES), F32)
    return pl.pallas_call(
        prep_kernel, out_shape=(table, table, table), name="prepare_tables"
    )(parents, jnp.cos(angles), jnp.sin(angles), steps)


def order_kernel(order, cache_ref, out_ref, buffer, load_sems, store_sems):
    loads, stores = [], []
    for d in range(cache_ref.shape[0]):
        loads.append(
            pltpu.make_async_copy(cache_ref.at[order[d]], buffer.at[d], load_sems.at[d])
        )
        loads[-1].start()
    for d, load in enumerate(loads):
        load.wait()
        stores.append(pltpu.make_async_copy(buffer.at[d], out_ref.at[d], store_sems.at[d]))
        stores[-1].start()
    for store in stores:
        store.wait()


def order_cache(kv_cache, send_order):
    held = kv_cache.shape[0]
    return pl.pallas_call(
        order_kernel,
        out_shape=jax.ShapeDtypeStruct(kv_cache.shape, BF),
        grid_spec=pltpu.PrefetchScalarGridSpec(
            num_scalar_prefetch=1,
            grid=(1,),
            in_specs=[pl.BlockSpec(memory_space=pl.ANY)],
            out_specs=pl.BlockSpec(memory_space=pl.ANY),
            scratch_shapes=[
                pltpu.VMEM(kv_cache.shape, BF),
                pltpu.SemaphoreType.DMA((held,)),
                pltpu.SemaphoreType.DMA((held,)),
            ],
        ),
        compiler_params=pltpu.CompilerParams(vmem_limit_bytes=VMEM_LIMIT),
        name="order_cache",
    )(send_order, kv_cache)


def layer_kernel(lengths, accepted, destination, *refs):
    x_refs = refs[: N_TP + 1]
    w_ref, wo_ref, cache_ref, bias_ref, cos_ref, sin_ref = refs[N_TP + 1 : N_TP + 7]
    out_refs = refs[N_TP + 7 : 2 * N_TP + 8]
    extra_out, xs, qkv, ctx, extra, sems = refs[2 * N_TP + 8 :]
    b = pl.program_id(0)

    @pl.when(b == 0)
    def _():
        ctx[...] = jnp.zeros_like(ctx)

    def received(k, first, last):
        piece = x_refs[k][0, first:last]
        if k == N_TP // 2:
            piece = jnp.where(b < HALF_BLOCKS, piece, x_refs[N_TP][0, first:last])
        return piece

    def deliver(k, first, last, values):
        values = values.astype(BF)
        if k != N_TP // 2:
            out_refs[k][0, first:last] = values
            return

        @pl.when(b < HALF_BLOCKS)
        def _():
            out_refs[k][0, first:last] = values

        @pl.when(b >= HALF_BLOCKS)
        def _():
            out_refs[N_TP][0, first:last] = values

    low_half = lane_index((HALF, LANES)) < 64
    squares = jnp.zeros((ROWS, LANES), F32)
    for j in range(N_TP // 2):
        base = j * 5 * LANES
        for device, at in ((2 * j, base), (2 * j + 1, base + 3 * LANES)):
            for part in range(2):
                piece = received(device, part * ROWS, (part + 1) * ROWS)
                xs[:, at + part * LANES : at + (part + 1) * LANES] = piece
                wide = piece.astype(F32)
                squares = squares + wide * wide
        even_tail = received(2 * j, 2 * ROWS, PACKED).astype(F32)
        odd_tail = received(2 * j + 1, 2 * ROWS, PACKED).astype(F32)
        tail = jnp.concatenate(
            [
                jnp.where(low_half, even_tail, swap_halves(odd_tail)),
                jnp.where(low_half, swap_halves(even_tail), odd_tail),
            ],
            axis=0,
        )
        xs[:, base + 2 * LANES : base + 3 * LANES] = tail.astype(BF)
        squares = squares + tail * tail
    scale = lax.rsqrt(jnp.sum(squares, axis=1, keepdims=True) * (1.0 / D) + 1e-05)
    flat = xs[...]
    projected = jnp.dot(flat, w_ref[...], preferred_element_type=F32) * scale
    cosines = cos_ref[...].reshape(ROWS, LANES)
    sines = sin_ref[...].reshape(ROWS, LANES)
    first = lane_index((ROWS, LANES)) < HD // 2

    def rotate(tile):
        other = jnp.where(
            first, pltpu.roll(tile, LANES - HD // 2, 1), pltpu.roll(tile, HD // 2, 1)
        )
        return tile * cosines + other * sines

    for h in range(GROUP + 1):
        head = slice(h * LANES, (h + 1) * LANES)
        qkv[:, head] = rotate(projected[:, head])
    qkv[:, (GROUP + 1) * LANES :] = projected[:, (GROUP + 1) * LANES :]

    factor = math.log2(math.e) / math.sqrt(HD)
    column = lane_index((GROUP * TREE, CACHE))
    extra_row = lax.broadcasted_iota(jnp.int32, (EXTRA, LANES), 0)
    extra_lane = lane_index((EXTRA, LANES))
    pick_row = lax.broadcasted_iota(jnp.int32, (EXTRA, TREE), 0)
    pick_column = lane_index((EXTRA, TREE))
    copies = []
    for i in range(REQ_BLOCK):
        r = b * REQ_BLOCK + i
        length = lengths[r]
        rows = slice(i * TREE, (i + 1) * TREE)
        q = jnp.concatenate(
            [qkv[rows, h * LANES : (h + 1) * LANES] for h in range(GROUP)], axis=0
        ).astype(BF)
        fresh_rows = qkv[rows, GROUP * LANES :].astype(BF)
        k = fresh_rows[:, :LANES]
        v = fresh_rows[:, LANES:]
        cached = jnp.dot(q[:, :HD], cache_ref[i, 0:HD], preferred_element_type=F32)
        cached = jnp.where(column < length, cached * factor, NEG)
        fresh = lax.dot_general(q, k, (((1,), (1,)), ((), ())), preferred_element_type=F32)
        bias = bias_ref[i][:, :TREE]
        fresh = fresh * factor + jnp.concatenate([bias] * GROUP, axis=0)
        top = jnp.maximum(
            jnp.max(cached, axis=1, keepdims=True), jnp.max(fresh, axis=1, keepdims=True)
        )
        cached = jnp.exp2(cached - top)
        fresh = jnp.exp2(fresh - top)
        total = jnp.sum(cached, axis=1, keepdims=True) + jnp.sum(fresh, axis=1, keepdims=True)
        mixed = lax.dot_general(
            cached.astype(BF),
            cache_ref[i, HD : 2 * HD],
            (((1,), (1,)), ((), ())),
            preferred_element_type=F32,
        ) + jnp.dot(fresh.astype(BF), v[:, :HD], preferred_element_type=F32)
        mixed = mixed / total
        for h in range(GROUP):
            ctx[rows, h * LANES : h * LANES + HD] = mixed[h * TREE : (h + 1) * TREE]

        wanted = jnp.full((EXTRA, TREE), -1, jnp.int32)
        for m in range(DEPTH):
            here = jnp.bitwise_and(pick_row, DEPTH - 1) == m
            wanted = jnp.where(here, accepted[r * DEPTH + m], wanted)
        pick = jnp.where(pick_column == wanted, 1.0, 0.0).astype(BF)
        new = jnp.dot(pick, fresh_rows, preferred_element_type=F32)
        shifted = pltpu.roll(new[:, LANES:], HD, 1)
        tile = jnp.where(
            extra_row < DEPTH,
            jnp.where(extra_lane < HD, new[:, :LANES], shifted),
            jnp.where(extra_lane < 2 * HD - LANES, shifted, 0.0),
        )
        coarse = (length // 16).astype(F32)
        fine = (length % 16).astype(F32)
        marker = jnp.where(extra_row == DEPTH, coarse, fine)
        marked = jnp.logical_and(
            extra_lane >= 64,
            jnp.logical_or(extra_row == DEPTH, extra_row == DEPTH + 1),
        )
        extra[i] = jnp.where(marked, marker, tile).astype(BF)
        copies.append(
            pltpu.make_async_copy(
                extra.at[i], extra_out.at[destination[r]], sems.at[i]
            )
        )
        copies[-1].start()

    partial = jnp.dot(ctx[...].astype(BF), wo_ref[...], preferred_element_type=F32)
    for j in range(N_TP // 2):
        base = j * 5 * LANES
        for k, at in ((2 * j, base), (2 * j + 1, base + 3 * LANES)):
            for part in range(2):
                tile = partial[:, at + part * LANES : at + (part + 1) * LANES]
                deliver(k, part * ROWS, (part + 1) * ROWS, tile)
        tail = partial[:, base + 2 * LANES : base + 3 * LANES]
        top, bottom = tail[:HALF], tail[HALF:]
        deliver(2 * j, 2 * ROWS, PACKED, jnp.where(low_half, top, swap_halves(bottom)))
        deliver(2 * j + 1, 2 * ROWS, PACKED, jnp.where(low_half, swap_halves(top), bottom))
    for copy in copies:
        copy.wait()


def verify_layer(parts, w, wo, kv_cache, tables, lengths, accepted, destination):
    held = kv_cache.shape[0]
    blocks = held // REQ_BLOCK
    full = lambda b, *_: (0, 0)
    packed = pl.BlockSpec((1, PACKED, LANES), lambda b, *_: (b, 0, 0))
    table = pl.BlockSpec((REQ_BLOCK, TREE, LANES), lambda b, *_: (b, 0, 0))
    in_specs = [packed] * (N_TP + 1)
    in_specs[N_TP // 2] = pl.BlockSpec(
        (1, PACKED, LANES), lambda b, *_: (jnp.minimum(b, HALF_BLOCKS - 1), 0, 0)
    )
    in_specs[N_TP] = pl.BlockSpec(
        (1, PACKED, LANES), lambda b, *_: (jnp.maximum(b - HALF_BLOCKS, 0), 0, 0)
    )
    return pl.pallas_call(
        layer_kernel,
        out_shape=[
            jax.ShapeDtypeStruct(
                (HALF_BLOCKS if k % (N_TP // 2) == 0 and k > 0 else blocks, PACKED, LANES), BF
            )
            for k in range(N_TP + 1)
        ]
        + [jax.ShapeDtypeStruct((held, EXTRA, LANES), BF)],
        grid_spec=pltpu.PrefetchScalarGridSpec(
            num_scalar_prefetch=3,
            grid=(blocks,),
            in_specs=in_specs
            + [
                pl.BlockSpec(w.shape, full),
                pl.BlockSpec(wo.shape, full),
                pl.BlockSpec((REQ_BLOCK, 2 * HD, CACHE), lambda b, *_: (b, 0, 0)),
                table,
                table,
                table,
            ],
            out_specs=in_specs + [pl.BlockSpec(memory_space=pl.ANY)],
            scratch_shapes=[
                pltpu.VMEM((ROWS, D), BF),
                pltpu.VMEM((ROWS, (GROUP + 2) * LANES), F32),
                pltpu.VMEM((ROWS, GROUP * LANES), F32),
                pltpu.VMEM((REQ_BLOCK, EXTRA, LANES), BF),
                pltpu.SemaphoreType.DMA((REQ_BLOCK,)),
            ],
        ),
        compiler_params=pltpu.CompilerParams(vmem_limit_bytes=VMEM_LIMIT),
        cost_estimate=pl.CostEstimate(
            flops=30_000_000_000, transcendentals=0, bytes_accessed=10_000_000
        ),
        name="verify_layer",
    )(lengths, accepted, destination, *parts, w, wo, kv_cache, *tables)


def assemble_kernel(cache_ref, extra_ref, o_ref):
    place_row = lax.broadcasted_iota(jnp.int32, (EXTRA, CACHE), 0)
    place_column = lane_index((EXTRA, CACHE))
    upper = lane_index((1, LANES)) >= 64
    for i in range(cache_ref.shape[0]):
        extra = extra_ref[i]
        wide = extra.astype(F32)
        length = wide[DEPTH : DEPTH + 1] * 16.0 + wide[DEPTH + 1 : DEPTH + 2]
        length = jnp.where(upper, length, swap_halves(length)).astype(jnp.int32)
        length = jnp.concatenate([length] * (CACHE // LANES), axis=1)
        offset = place_column - length
        first = jnp.logical_and(offset == place_row, place_row < DEPTH)
        second = jnp.logical_and(offset == place_row - DEPTH, place_row >= DEPTH)
        live = jnp.where(offset[0:1] < 0, 1.0, 0.0).astype(BF)
        contract = (((0,), (0,)), ((), ()))
        new = lax.dot_general(
            extra, jnp.where(first, 1.0, 0.0).astype(BF), contract, preferred_element_type=F32
        )
        rest = lax.dot_general(
            extra, jnp.where(second, 1.0, 0.0).astype(BF), contract, preferred_element_type=F32
        )[: 2 * HD - LANES]
        o_ref[i, :LANES] = cache_ref[i, :LANES] * live + new.astype(BF)
        o_ref[i, LANES:] = cache_ref[i, LANES:] * live + rest.astype(BF)


def assemble_cache(cached, extra):
    step = 4
    cache_spec = pl.BlockSpec((step,) + cached.shape[1:], lambda s: (s, 0, 0))
    extra_spec = pl.BlockSpec((step,) + extra.shape[1:], lambda s: (s, 0, 0))
    return pl.pallas_call(
        assemble_kernel,
        out_shape=jax.ShapeDtypeStruct(cached.shape, BF),
        grid=(cached.shape[0] // step,),
        in_specs=[cache_spec, extra_spec],
        out_specs=cache_spec,
        name="assemble_cache",
    )(cached, extra)


def spread_heads(heads):
    source = jnp.arange(heads * HD)[:, None]
    target = jnp.arange(heads * LANES)[None, :]
    return (source // HD * LANES + source % HD == target).astype(BF)


def exchange(values):
    return lax.all_to_all(values, "req", split_axis=0, concat_axis=0, tiled=True)


def go_up(values):
    return lax.ppermute(values, "tp", [(i, (i + 1) % N_TP) for i in range(N_TP)])


def go_down(values):
    return lax.ppermute(values, "tp", [(i, (i - 1) % N_TP) for i in range(N_TP)])


def add_up(a, b):
    return (a.astype(F32) + b.astype(F32)).astype(BF)


def add_blocks(values, more, first):
    picked = values[first : first + HALF_BLOCKS]
    return lax.dynamic_update_slice(values, add_up(picked, more), (first, 0, 0))


def scatter_ring(targets, cached, extra):
    half = N_TP // 2
    up = go_up(targets[half])
    down = go_down(targets[N_TP])
    for step in range(1, half):
        above, below = targets[half - step], targets[half + step]
        if step == 1:
            above = add_blocks(above, up, 0)
            below = add_blocks(below, down, HALF_BLOCKS)
        else:
            above, below = add_up(above, up), add_up(below, down)
        if step == 2:
            above, below, cached, extra = lax.optimization_barrier(
                (above, below, cached, extra)
            )
            extra = exchange(extra)
        if step == 3:
            above, below, extra = lax.optimization_barrier((above, below, extra))
            new_cache = assemble_cache(cached, extra)
        up = go_up(above)
        down = go_down(below)
    up, down, new_cache = lax.optimization_barrier((up, down, new_cache))
    return up, down, new_cache


def per_device(
    hidden, norm_gain, w_query, w_keyval, w_out, kv_cache, lengths, parents, accepted, slot_of
):
    held = hidden.shape[0]
    rows = hidden.reshape(held * TREE, WIDTH)
    me = lax.axis_index("tp").astype(jnp.int32).reshape(1)
    barrier = lax.optimization_barrier

    parts = [pack_rows(rows, me)] * (N_TP + 1)
    destination = slot_of // held
    peer_index = jnp.arange(held, dtype=jnp.int32)
    matches = (destination[None, :] == peer_index[:, None]).astype(jnp.int32)
    send_order = jnp.sum(matches * peer_index[None, :], axis=1)
    ordered = order_cache(kv_cache, send_order)
    below, above = go_up(parts[0]), go_down(parts[0])

    below, above, w_keyval, w_query, ordered = barrier(
        (below, above, w_keyval, w_query, ordered)
    )
    parts[7], parts[1] = below, above
    gain = norm_gain[:, None]
    wkv = lax.dot_general(
        w_keyval, spread_heads(2), (((0,), (0,)), ((), ())), preferred_element_type=F32
    )
    wkv = (wkv * gain).astype(BF)
    wq = (jnp.dot(w_query, spread_heads(GROUP), preferred_element_type=F32) * gain).astype(BF)
    ordered, wkv = barrier((ordered, wkv))
    cached = exchange(ordered)
    weights = arrange_weights(wq, wkv, w_out, me)
    below, above = go_up(below), go_down(above)

    below, above, weights = barrier((below, above, weights))
    parts[6], parts[2] = below, above
    below, above = go_up(below), go_down(above)

    below, above, parents = barrier((below, above, parents))
    parts[5], parts[3] = below, above
    tables = prepare_tables(parents, lengths)
    parts[4] = go_up(below[:HALF_BLOCKS])
    parts[8] = go_down(above[HALF_BLOCKS:])
    picks = accepted.reshape(-1)

    *targets, extra = verify_layer(
        parts, *weights, kv_cache, tables, lengths, picks, destination
    )
    up, down, new_cache = scatter_ring(targets, cached, extra)
    out_rows = finish_rows(targets[0], up, down, rows, me)
    return (out_rows.reshape(hidden.shape), new_cache)


def solution(mesh):
    in_specs = (
        P("req", None, "tp"),
        P(),
        P(None, "tp"),
        P("tp", None),
        P("tp", None),
        P("req", "tp", None),
        P("req"),
        P("req", None),
        P("req", None),
        P("req"),
    )
    out_specs = (P("req", None, "tp"), P("req", "tp", None))
    return jax.shard_map(
        per_device, mesh=mesh, in_specs=in_specs, out_specs=out_specs, check_vma=False
    )
```

```python
import math

import jax
import jax.numpy as jnp
from jax import lax
from jax.experimental import pallas as pl
from jax.experimental.pallas import tpu as pltpu
from jax.sharding import PartitionSpec as P

H = 32
KVH = 8
HD = 80
D = 2560
TREE = 24
CACHE = 512
DEPTH = 4
N_TP = 8
GROUP = H // KVH
LANES = 128
REQ_BLOCK = 8
ROWS = REQ_BLOCK * TREE
HALF = ROWS // 2
PACKED = 2 * ROWS + HALF
WIDTH = D // N_TP
NEG = -1e30
EXTRA = 8
HALF_BLOCKS = 2
BF = jnp.bfloat16
F32 = jnp.float32
VMEM_LIMIT = 56 * 1024 * 1024


def lane_index(shape):
    return lax.broadcasted_iota(jnp.int32, shape, len(shape) - 1)


def swap_halves(tile):
    return pltpu.roll(tile, 64, 1)


def pack_kernel(parity, x_ref, o_ref):
    for i in range(HALF_BLOCKS):
        pack_block(parity, x_ref.at[pl.ds(i * ROWS, ROWS)], o_ref.at[pl.ds(i, 1)])


def pack_block(parity, x_ref, o_ref):
    x = x_ref[...].astype(F32)
    t0 = x[:, 0:128]
    t1 = x[:, 128:256]
    t2 = jnp.concatenate([x[:, 256:320], jnp.zeros((ROWS, 64), F32)], axis=1)
    low = lane_index((ROWS, LANES)) < 64
    low_half = lane_index((HALF, LANES)) < 64
    even = jnp.bitwise_and(parity[0], 1) == 0

    @pl.when(even)
    def _():
        o_ref[0, 0:ROWS] = t0.astype(BF)
        o_ref[0, ROWS : 2 * ROWS] = t1.astype(BF)
        o_ref[0, 2 * ROWS : PACKED] = jnp.where(
            low_half, t2[:HALF], swap_halves(t2[HALF:])
        ).astype(BF)

    @pl.when(jnp.logical_not(even))
    def _():
        s0, s1, s2 = swap_halves(t0), swap_halves(t1), swap_halves(t2)
        o_ref[0, 0:ROWS] = jnp.where(low, s0, s1).astype(BF)
        o_ref[0, ROWS : 2 * ROWS] = jnp.where(low, s1, s2).astype(BF)
        o_ref[0, 2 * ROWS : PACKED] = jnp.where(low_half, t0[:HALF], s0[HALF:]).astype(BF)


def pack_rows(rows, parity):
    blocks = rows.shape[0] // ROWS
    return pl.pallas_call(
        pack_kernel,
        out_shape=jax.ShapeDtypeStruct((blocks, PACKED, LANES), BF),
        grid_spec=pltpu.PrefetchScalarGridSpec(
            num_scalar_prefetch=1,
            grid=(blocks // HALF_BLOCKS,),
            in_specs=[pl.BlockSpec((HALF_BLOCKS * ROWS, WIDTH), lambda b, p: (b, 0))],
            out_specs=pl.BlockSpec((HALF_BLOCKS, PACKED, LANES), lambda b, p: (b, 0, 0)),
        ),
        name="pack_rows",
    )(parity, rows)


def finish_kernel(parity, own_ref, up_ref, down_ref, x_ref, o_ref):
    for i in range(HALF_BLOCKS):
        block = pl.ds(i, 1)
        flat = pl.ds(i * ROWS, ROWS)
        finish_block(
            parity,
            own_ref.at[block],
            up_ref.at[block],
            down_ref.at[block],
            x_ref.at[flat],
            o_ref.at[flat],
        )


def finish_block(parity, own_ref, up_ref, down_ref, x_ref, o_ref):
    packed = (
        own_ref[0].astype(F32) + up_ref[0].astype(F32) + down_ref[0].astype(F32)
    )
    m0 = packed[0:ROWS]
    m1 = packed[ROWS : 2 * ROWS]
    packed_tail = packed[2 * ROWS : PACKED]
    tail = jnp.concatenate([packed_tail, swap_halves(packed_tail)], axis=0)
    low = lane_index((ROWS, LANES)) < 64
    even = jnp.bitwise_and(parity[0], 1) == 0

    @pl.when(even)
    def _():
        total = jnp.concatenate([m0, m1, tail], axis=1)[:, :WIDTH]
        o_ref[...] = (x_ref[...].astype(F32) + total).astype(BF)

    @pl.when(jnp.logical_not(even))
    def _():
        s0, s1 = swap_halves(m0), swap_halves(m1)
        total = jnp.concatenate(
            [jnp.where(low, tail, s0), jnp.where(low, s0, s1), s1], axis=1
        )[:, :WIDTH]
        o_ref[...] = (x_ref[...].astype(F32) + total).astype(BF)


def finish_rows(own, up, down, rows, parity):
    blocks = rows.shape[0] // ROWS
    packed = pl.BlockSpec((HALF_BLOCKS, PACKED, LANES), lambda b, p: (b, 0, 0))
    flat = pl.BlockSpec((HALF_BLOCKS * ROWS, WIDTH), lambda b, p: (b, 0))
    return pl.pallas_call(
        finish_kernel,
        out_shape=jax.ShapeDtypeStruct(rows.shape, BF),
        grid_spec=pltpu.PrefetchScalarGridSpec(
            num_scalar_prefetch=1,
            grid=(blocks // HALF_BLOCKS,),
            in_specs=[packed, packed, packed, flat],
            out_specs=flat,
        ),
        name="finish_rows",
    )(parity, own, up, down, rows)


def arrange_kernel(me, wq_ref, wkv_ref, wo_ref, w_ref, o_ref):
    o_ref[...] = jnp.zeros_like(o_ref)
    query = GROUP * LANES
    low = lane_index((GROUP * HD, LANES)) < 64
    for j in range(N_TP // 2):
        base = j * 5 * LANES
        tails = []
        for k, at, tail_at in (
            (2 * j, base, base + 256),
            (2 * j + 1, base + 384, base + 320),
        ):
            device = jnp.bitwise_and(me[0] + k, N_TP - 1)
            odd = jnp.bitwise_and(device, 1)
            main_from = pl.multiple_of(device * WIDTH + 64 * odd, 64)
            tail_from = pl.multiple_of(device * WIDTH + 256 * (1 - odd), 64)
            w_ref[at : at + 256, :query] = wq_ref[pl.ds(main_from, 256), :]
            w_ref[at : at + 256, query:] = wkv_ref[pl.ds(main_from, 256), :]
            w_ref[tail_at : tail_at + 64, :query] = wq_ref[pl.ds(tail_from, 64), :]
            w_ref[tail_at : tail_at + 64, query:] = wkv_ref[pl.ds(tail_from, 64), :]
            tile = device // 2 * 5
            for part in range(2):
                column = pl.multiple_of((tile + 3 * odd + part) * LANES, LANES)
                piece = wo_ref[:, pl.ds(column, LANES)]
                for h in range(GROUP):
                    o_ref[
                        h * LANES : h * LANES + HD,
                        at + part * LANES : at + (part + 1) * LANES,
                    ] = piece[h * HD : (h + 1) * HD]
            column = pl.multiple_of((tile + 2) * LANES, LANES)
            tail = wo_ref[:, pl.ds(column, LANES)].astype(F32)
            wrong = odd == (1 - k % 2)
            tails.append(jnp.where(wrong, swap_halves(tail), tail))
        joined = jnp.where(low, tails[0], tails[1]).astype(BF)
        for h in range(GROUP):
            o_ref[h * LANES : h * LANES + HD, base + 256 : base + 384] = joined[
                h * HD : (h + 1) * HD
            ]


def arrange_weights(wq, wkv, w_out, me):
    return pl.pallas_call(
        arrange_kernel,
        out_shape=(
            jax.ShapeDtypeStruct((D, (GROUP + 2) * LANES), BF),
            jax.ShapeDtypeStruct((GROUP * LANES, D), BF),
        ),
        in_specs=[pl.BlockSpec(memory_space=pltpu.SMEM)]
        + [pl.BlockSpec(memory_space=pltpu.VMEM)] * 3,
        out_specs=(
            pl.BlockSpec(memory_space=pltpu.VMEM),
            pl.BlockSpec(memory_space=pltpu.VMEM),
        ),
        compiler_params=pltpu.CompilerParams(vmem_limit_bytes=VMEM_LIMIT),
        name="arrange_weights",
    )(me, wq, wkv, w_out)


def prep_kernel(parents_ref, cos_ref, sin_ref, step_ref, bias_out, cos_out, sin_out):
    requests = parents_ref.shape[0]
    lane = lane_index((requests, LANES))
    step_cos = step_ref[0:1, :]
    step_sin = step_ref[1:2, :]
    sign = step_ref[2:3, :]
    parents = parents_ref[...]
    marks = jnp.where(lane == 0, 1.0, 0.0)
    cosines, sines = cos_ref[...], sin_ref[...]
    older = (marks, cosines, sines)
    newer = older
    for t in range(TREE):
        if t > 0:
            near = jnp.broadcast_to(parents[:, t : t + 1], (requests, LANES)) == t - 1
            marks, cosines, sines = (jnp.where(near, a, b) for a, b in zip(newer, older))
            marks = jnp.where(lane == t, 1.0, marks)
            if t > 0:
                cosines, sines = (
                    cosines * step_cos - sines * step_sin,
                    sines * step_cos + cosines * step_sin,
                )
            older, newer = newer, (marks, cosines, sines)
        bias_out[:, t, :] = jnp.where(marks > 0.5, 0.0, NEG)
        cos_out[:, t, :] = cosines
        sin_out[:, t, :] = sines * sign


def prepare_tables(parents, lengths):
    requests = parents.shape[0]
    lane = jnp.arange(LANES)
    pair = jnp.where(lane < HD // 2, lane, lane - HD // 2)
    frequency = 10000.0 ** (-2.0 * pair.astype(F32) / HD)
    angles = lengths.astype(F32)[:, None] * frequency[None, :]
    sign = jnp.where(lane < HD // 2, -1.0, jnp.where(lane < HD, 1.0, 0.0))
    steps = jnp.stack([jnp.cos(frequency), jnp.sin(frequency), sign] + [sign] * 5)
    table = jax.ShapeDtypeStruct((requests, TREE, LANES), F32)
    return pl.pallas_call(
        prep_kernel, out_shape=(table, table, table), name="prepare_tables"
    )(parents, jnp.cos(angles), jnp.sin(angles), steps)


def order_kernel(order, cache_ref, out_ref, buffer, load_sems, store_sems):
    loads, stores = [], []
    for d in range(cache_ref.shape[0]):
        loads.append(
            pltpu.make_async_copy(cache_ref.at[order[d]], buffer.at[d], load_sems.at[d])
        )
        loads[-1].start()
    for d, load in enumerate(loads):
        load.wait()
        stores.append(pltpu.make_async_copy(buffer.at[d], out_ref.at[d], store_sems.at[d]))
        stores[-1].start()
    for store in stores:
        store.wait()


def order_cache(kv_cache, send_order):
    held = kv_cache.shape[0]
    return pl.pallas_call(
        order_kernel,
        out_shape=jax.ShapeDtypeStruct(kv_cache.shape, BF),
        grid_spec=pltpu.PrefetchScalarGridSpec(
            num_scalar_prefetch=1,
            grid=(1,),
            in_specs=[pl.BlockSpec(memory_space=pl.ANY)],
            out_specs=pl.BlockSpec(memory_space=pl.ANY),
            scratch_shapes=[
                pltpu.VMEM(kv_cache.shape, BF),
                pltpu.SemaphoreType.DMA((held,)),
                pltpu.SemaphoreType.DMA((held,)),
            ],
        ),
        compiler_params=pltpu.CompilerParams(vmem_limit_bytes=VMEM_LIMIT),
        name="order_cache",
    )(send_order, kv_cache)


def layer_kernel(lengths, accepted, destination, *refs):
    x_refs = refs[: N_TP + 1]
    w_ref, wo_ref, cache_ref, bias_ref, cos_ref, sin_ref = refs[N_TP + 1 : N_TP + 7]
    out_refs = refs[N_TP + 7 : 2 * N_TP + 8]
    extra_out, xs, qkv, ctx, extra, sems = refs[2 * N_TP + 8 :]
    b = pl.program_id(0)

    @pl.when(b == 0)
    def _():
        ctx[...] = jnp.zeros_like(ctx)

    def received(k, first, last):
        piece = x_refs[k][0, first:last]
        if k == N_TP // 2:
            piece = jnp.where(b < HALF_BLOCKS, piece, x_refs[N_TP][0, first:last])
        return piece

    def deliver(k, first, last, values):
        values = values.astype(BF)
        if k != N_TP // 2:
            out_refs[k][0, first:last] = values
            return

        @pl.when(b < HALF_BLOCKS)
        def _():
            out_refs[k][0, first:last] = values

        @pl.when(b >= HALF_BLOCKS)
        def _():
            out_refs[N_TP][0, first:last] = values

    low_half = lane_index((HALF, LANES)) < 64
    squares = jnp.zeros((ROWS, LANES), F32)
    for j in range(N_TP // 2):
        base = j * 5 * LANES
        for device, at in ((2 * j, base), (2 * j + 1, base + 3 * LANES)):
            for part in range(2):
                piece = received(device, part * ROWS, (part + 1) * ROWS)
                xs[:, at + part * LANES : at + (part + 1) * LANES] = piece
                wide = piece.astype(F32)
                squares = squares + wide * wide
        even_tail = received(2 * j, 2 * ROWS, PACKED).astype(F32)
        odd_tail = received(2 * j + 1, 2 * ROWS, PACKED).astype(F32)
        tail = jnp.concatenate(
            [
                jnp.where(low_half, even_tail, swap_halves(odd_tail)),
                jnp.where(low_half, swap_halves(even_tail), odd_tail),
            ],
            axis=0,
        )
        xs[:, base + 2 * LANES : base + 3 * LANES] = tail.astype(BF)
        squares = squares + tail * tail
    scale = lax.rsqrt(jnp.sum(squares, axis=1, keepdims=True) * (1.0 / D) + 1e-05)
    flat = xs[...]
    projected = jnp.dot(flat, w_ref[...], preferred_element_type=F32) * scale
    cosines = cos_ref[...].reshape(ROWS, LANES)
    sines = sin_ref[...].reshape(ROWS, LANES)
    first = lane_index((ROWS, LANES)) < HD // 2

    def rotate(tile):
        other = jnp.where(
            first, pltpu.roll(tile, LANES - HD // 2, 1), pltpu.roll(tile, HD // 2, 1)
        )
        return tile * cosines + other * sines

    for h in range(GROUP + 1):
        head = slice(h * LANES, (h + 1) * LANES)
        qkv[:, head] = rotate(projected[:, head])
    qkv[:, (GROUP + 1) * LANES :] = projected[:, (GROUP + 1) * LANES :]

    factor = math.log2(math.e) / math.sqrt(HD)
    column = lane_index((GROUP * TREE, CACHE))
    extra_row = lax.broadcasted_iota(jnp.int32, (EXTRA, LANES), 0)
    extra_lane = lane_index((EXTRA, LANES))
    pick_row = lax.broadcasted_iota(jnp.int32, (EXTRA, TREE), 0)
    pick_column = lane_index((EXTRA, TREE))
    copies = []
    for i in range(REQ_BLOCK):
        r = b * REQ_BLOCK + i
        length = lengths[r]
        rows = slice(i * TREE, (i + 1) * TREE)
        q = jnp.concatenate(
            [qkv[rows, h * LANES : (h + 1) * LANES] for h in range(GROUP)], axis=0
        ).astype(BF)
        fresh_rows = qkv[rows, GROUP * LANES :].astype(BF)
        k = fresh_rows[:, :LANES]
        v = fresh_rows[:, LANES:]
        cached = jnp.dot(q[:, :HD], cache_ref[i, 0:HD], preferred_element_type=F32)
        cached = jnp.where(column < length, cached * factor, NEG)
        fresh = lax.dot_general(q, k, (((1,), (1,)), ((), ())), preferred_element_type=F32)
        bias = bias_ref[i][:, :TREE]
        fresh = fresh * factor + jnp.concatenate([bias] * GROUP, axis=0)
        top = jnp.maximum(
            jnp.max(cached, axis=1, keepdims=True), jnp.max(fresh, axis=1, keepdims=True)
        )
        cached = jnp.exp2(cached - top)
        fresh = jnp.exp2(fresh - top)
        total = jnp.sum(cached, axis=1, keepdims=True) + jnp.sum(fresh, axis=1, keepdims=True)
        mixed = lax.dot_general(
            cached.astype(BF),
            cache_ref[i, HD : 2 * HD],
            (((1,), (1,)), ((), ())),
            preferred_element_type=F32,
        ) + jnp.dot(fresh.astype(BF), v[:, :HD], preferred_element_type=F32)
        mixed = mixed / total
        for h in range(GROUP):
            ctx[rows, h * LANES : h * LANES + HD] = mixed[h * TREE : (h + 1) * TREE]

        wanted = jnp.full((EXTRA, TREE), -1, jnp.int32)
        for m in range(DEPTH):
            here = jnp.bitwise_and(pick_row, DEPTH - 1) == m
            wanted = jnp.where(here, accepted[r * DEPTH + m], wanted)
        pick = jnp.where(pick_column == wanted, 1.0, 0.0).astype(BF)
        new = jnp.dot(pick, fresh_rows, preferred_element_type=F32)
        shifted = pltpu.roll(new[:, LANES:], HD, 1)
        tile = jnp.where(
            extra_row < DEPTH,
            jnp.where(extra_lane < HD, new[:, :LANES], shifted),
            jnp.where(extra_lane < 2 * HD - LANES, shifted, 0.0),
        )
        coarse = (length // 16).astype(F32)
        fine = (length % 16).astype(F32)
        marker = jnp.where(extra_row == DEPTH, coarse, fine)
        marked = jnp.logical_and(
            extra_lane >= 64,
            jnp.logical_or(extra_row == DEPTH, extra_row == DEPTH + 1),
        )
        extra[i] = jnp.where(marked, marker, tile).astype(BF)
        copies.append(
            pltpu.make_async_copy(
                extra.at[i], extra_out.at[destination[r]], sems.at[i]
            )
        )
        copies[-1].start()

    partial = jnp.dot(ctx[...].astype(BF), wo_ref[...], preferred_element_type=F32)
    for j in range(N_TP // 2):
        base = j * 5 * LANES
        for k, at in ((2 * j, base), (2 * j + 1, base + 3 * LANES)):
            for part in range(2):
                tile = partial[:, at + part * LANES : at + (part + 1) * LANES]
                deliver(k, part * ROWS, (part + 1) * ROWS, tile)
        tail = partial[:, base + 2 * LANES : base + 3 * LANES]
        top, bottom = tail[:HALF], tail[HALF:]
        deliver(2 * j, 2 * ROWS, PACKED, jnp.where(low_half, top, swap_halves(bottom)))
        deliver(2 * j + 1, 2 * ROWS, PACKED, jnp.where(low_half, swap_halves(top), bottom))
    for copy in copies:
        copy.wait()


def verify_layer(parts, w, wo, kv_cache, tables, lengths, accepted, destination):
    held = kv_cache.shape[0]
    blocks = held // REQ_BLOCK
    full = lambda b, *_: (0, 0)
    packed = pl.BlockSpec((1, PACKED, LANES), lambda b, *_: (b, 0, 0))
    table = pl.BlockSpec((REQ_BLOCK, TREE, LANES), lambda b, *_: (b, 0, 0))
    in_specs = [packed] * (N_TP + 1)
    in_specs[N_TP // 2] = pl.BlockSpec(
        (1, PACKED, LANES), lambda b, *_: (jnp.minimum(b, HALF_BLOCKS - 1), 0, 0)
    )
    in_specs[N_TP] = pl.BlockSpec(
        (1, PACKED, LANES), lambda b, *_: (jnp.maximum(b - HALF_BLOCKS, 0), 0, 0)
    )
    return pl.pallas_call(
        layer_kernel,
        out_shape=[
            jax.ShapeDtypeStruct(
                (HALF_BLOCKS if k % (N_TP // 2) == 0 and k > 0 else blocks, PACKED, LANES), BF
            )
            for k in range(N_TP + 1)
        ]
        + [jax.ShapeDtypeStruct((held, EXTRA, LANES), BF)],
        grid_spec=pltpu.PrefetchScalarGridSpec(
            num_scalar_prefetch=3,
            grid=(blocks,),
            in_specs=in_specs
            + [
                pl.BlockSpec(w.shape, full),
                pl.BlockSpec(wo.shape, full),
                pl.BlockSpec((REQ_BLOCK, 2 * HD, CACHE), lambda b, *_: (b, 0, 0)),
                table,
                table,
                table,
            ],
            out_specs=in_specs + [pl.BlockSpec(memory_space=pl.ANY)],
            scratch_shapes=[
                pltpu.VMEM((ROWS, D), BF),
                pltpu.VMEM((ROWS, (GROUP + 2) * LANES), F32),
                pltpu.VMEM((ROWS, GROUP * LANES), F32),
                pltpu.VMEM((REQ_BLOCK, EXTRA, LANES), BF),
                pltpu.SemaphoreType.DMA((REQ_BLOCK,)),
            ],
        ),
        compiler_params=pltpu.CompilerParams(vmem_limit_bytes=VMEM_LIMIT),
        cost_estimate=pl.CostEstimate(
            flops=24_000_000_000, transcendentals=0, bytes_accessed=10_000_000
        ),
        name="verify_layer",
    )(lengths, accepted, destination, *parts, w, wo, kv_cache, *tables)


def assemble_kernel(cache_ref, extra_ref, o_ref):
    place_row = lax.broadcasted_iota(jnp.int32, (EXTRA, CACHE), 0)
    place_column = lane_index((EXTRA, CACHE))
    upper = lane_index((1, LANES)) >= 64
    for i in range(cache_ref.shape[0]):
        extra = extra_ref[i]
        wide = extra.astype(F32)
        length = wide[DEPTH : DEPTH + 1] * 16.0 + wide[DEPTH + 1 : DEPTH + 2]
        length = jnp.where(upper, length, swap_halves(length)).astype(jnp.int32)
        length = jnp.concatenate([length] * (CACHE // LANES), axis=1)
        offset = place_column - length
        first = jnp.logical_and(offset == place_row, place_row < DEPTH)
        second = jnp.logical_and(offset == place_row - DEPTH, place_row >= DEPTH)
        live = jnp.where(offset[0:1] < 0, 1.0, 0.0).astype(BF)
        contract = (((0,), (0,)), ((), ()))
        new = lax.dot_general(
            extra, jnp.where(first, 1.0, 0.0).astype(BF), contract, preferred_element_type=F32
        )
        rest = lax.dot_general(
            extra, jnp.where(second, 1.0, 0.0).astype(BF), contract, preferred_element_type=F32
        )[: 2 * HD - LANES]
        o_ref[i, :LANES] = cache_ref[i, :LANES] * live + new.astype(BF)
        o_ref[i, LANES:] = cache_ref[i, LANES:] * live + rest.astype(BF)


def assemble_cache(cached, extra):
    step = 4
    cache_spec = pl.BlockSpec((step,) + cached.shape[1:], lambda s: (s, 0, 0))
    extra_spec = pl.BlockSpec((step,) + extra.shape[1:], lambda s: (s, 0, 0))
    return pl.pallas_call(
        assemble_kernel,
        out_shape=jax.ShapeDtypeStruct(cached.shape, BF),
        grid=(cached.shape[0] // step,),
        in_specs=[cache_spec, extra_spec],
        out_specs=cache_spec,
        name="assemble_cache",
    )(cached, extra)


def spread_heads(heads):
    source = jnp.arange(heads * HD)[:, None]
    target = jnp.arange(heads * LANES)[None, :]
    return (source // HD * LANES + source % HD == target).astype(BF)


def exchange(values):
    return lax.all_to_all(values, "req", split_axis=0, concat_axis=0, tiled=True)


def go_up(values):
    return lax.ppermute(values, "tp", [(i, (i + 1) % N_TP) for i in range(N_TP)])


def go_down(values):
    return lax.ppermute(values, "tp", [(i, (i - 1) % N_TP) for i in range(N_TP)])


def add_up(a, b):
    return (a.astype(F32) + b.astype(F32)).astype(BF)


def add_blocks(values, more, first):
    picked = values[first : first + HALF_BLOCKS]
    return lax.dynamic_update_slice(values, add_up(picked, more), (first, 0, 0))


def scatter_ring(targets, cached, extra):
    half = N_TP // 2
    up = go_up(targets[half])
    down = go_down(targets[N_TP])
    for step in range(1, half):
        above, below = targets[half - step], targets[half + step]
        if step == 1:
            above = add_blocks(above, up, 0)
            below = add_blocks(below, down, HALF_BLOCKS)
        else:
            above, below = add_up(above, up), add_up(below, down)
        if step == 3:
            above, below, cached, extra = lax.optimization_barrier(
                (above, below, cached, extra)
            )
        up = go_up(above)
        down = go_down(below)
    return up, down, assemble_cache(cached, exchange(extra))


def per_device(
    hidden, norm_gain, w_query, w_keyval, w_out, kv_cache, lengths, parents, accepted, slot_of
):
    held = hidden.shape[0]
    rows = hidden.reshape(held * TREE, WIDTH)
    me = lax.axis_index("tp").astype(jnp.int32).reshape(1)
    barrier = lax.optimization_barrier

    parts = [pack_rows(rows, me)] * (N_TP + 1)
    destination = slot_of // held
    peer_index = jnp.arange(held, dtype=jnp.int32)
    matches = (destination[None, :] == peer_index[:, None]).astype(jnp.int32)
    send_order = jnp.sum(matches * peer_index[None, :], axis=1)
    ordered = order_cache(kv_cache, send_order)
    below, above = go_up(parts[0]), go_down(parts[0])

    below, above, w_keyval, w_query, ordered = barrier(
        (below, above, w_keyval, w_query, ordered)
    )
    parts[7], parts[1] = below, above
    gain = norm_gain[:, None]
    wkv = lax.dot_general(
        w_keyval, spread_heads(2), (((0,), (0,)), ((), ())), preferred_element_type=F32
    )
    wkv = (wkv * gain).astype(BF)
    wq = (jnp.dot(w_query, spread_heads(GROUP), preferred_element_type=F32) * gain).astype(BF)
    ordered, wkv = barrier((ordered, wkv))
    cached = exchange(ordered)
    weights = arrange_weights(wq, wkv, w_out, me)
    below, above = go_up(below), go_down(above)

    below, above, weights = barrier((below, above, weights))
    parts[6], parts[2] = below, above
    below, above = go_up(below), go_down(above)

    below, above, parents = barrier((below, above, parents))
    parts[5], parts[3] = below, above
    tables = prepare_tables(parents, lengths)
    parts[4] = go_up(below[:HALF_BLOCKS])
    parts[8] = go_down(above[HALF_BLOCKS:])
    picks = accepted.reshape(-1)

    *targets, extra = verify_layer(
        parts, *weights, kv_cache, tables, lengths, picks, destination
    )
    up, down, new_cache = scatter_ring(targets, cached, extra)
    out_rows = finish_rows(targets[0], up, down, rows, me)
    return (out_rows.reshape(hidden.shape), new_cache)


def solution(mesh):
    in_specs = (
        P("req", None, "tp"),
        P(),
        P(None, "tp"),
        P("tp", None),
        P("tp", None),
        P("req", "tp", None),
        P("req"),
        P("req", None),
        P("req", None),
        P("req"),
    )
    out_specs = (P("req", None, "tp"), P("req", "tp", None))
    return jax.shard_map(
        per_device, mesh=mesh, in_specs=in_specs, out_specs=out_specs, check_vma=False
    )
```
